128 devices in a mesh: depth: 32 (over x, z_hi, y), filt: 4 (over z_lo, core).
Axes of the slice: x: 4, y: 4, z: 4 (z_hi: 2, z_lo: 2; z = z_hi * 2 + z_lo), core: 2. Of those that a mesh axis runs over, the one named last changes fastest.
Arguments:
- upper_level: bfloat16 [64, 128, 16, 256], P(None, 'depth', 'filt'), may hold values from -6 to 6
- stride_weight: bfloat16 [8, 128, 64], P(None, 'filt'), may hold values from -0.25 to 0.25
- middle_weight: bfloat16 [27, 128, 128], P(None, 'filt'), may hold values from -0.109375 to 0.109375
- last_weight: bfloat16 [27, 128, 128], P(None, 'filt'), may hold values from -0.109375 to 0.109375
- cotangent: bfloat16 [128, 64, 8, 128], P('filt', 'depth'), may hold values from -0.0234375 to 0.0234375
Outputs:
- result: bfloat16 [128, 64, 8, 128], P('filt', 'depth')
- grad_stride: float32 [8, 128, 64], P(None, 'filt')
- grad_middle: float32 [27, 128, 128], P(None, 'filt')
- grad_last: float32 [27, 128, 128], P(None, 'filt')
The draws below stay inside these ranges and needn't reach their ends.
All inputs are finite; a program needn't handle non-finite values.
Results may differ from the reference program's by a relative error of at most 0.0059.
Values may be sent and summed in bfloat16 or wider, within the bound.
No kernel may reach another device: no remote copies, remote signals or barrier semaphores. Data moves between devices by JAX's collectives and lax.ppermute only.
A program may use at most 64 MiB of HBM per device.

```python
import jax
import jax.numpy as jnp
from jax import lax

C = 128
CIN = 64
W = 128
H = 8
OD = 64


def steps_of(key, extent, shards, smallest, largest):
    factor_of = 1.0
    for position, blocks in shards:
        heights = jax.random.uniform(jax.random.fold_in(jax.random.fold_in(key, 6), position), (blocks,), jnp.float32, smallest / len(shards), largest / len(shards))
        factor_of = factor_of * jnp.repeat(jnp.exp(heights), extent[position] // blocks).reshape((-1,) + (1,) * (len(extent) - 1 - position))
    return factor_of


def normal_values(key, shape, width, reach, cuts=(), held_as=jnp.bfloat16):
    array = jax.random.normal(key, shape, jnp.float32) * width
    if len(cuts) > 0:
        array = steps_of(key, shape, cuts, -0.22, 0.18) * array
    return jnp.clip(array, min=-reach, max=reach).astype(held_as)


def setup_inputs(seed: int = 0) -> dict:
    key_of = jax.random.split(jax.random.key(seed), 6)
    upper_level = normal_values(key_of[0], (CIN, 2 * OD, 2 * H, 2 * W), 1.0, 6.0, ((1, 32), (2, 4)))
    stride_weight = normal_values(key_of[1], (8, C, CIN), (8 * CIN) ** -0.5, 0.25, ((1, 4),))
    middle_weight = normal_values(key_of[2], (27, C, C), (27 * C) ** -0.5, 0.109375, ((1, 4),))
    last_weight = normal_values(key_of[3], (27, C, C), (27 * C) ** -0.5, 0.109375, ((1, 4),))
    cotangent = normal_values(key_of[4], (C, OD, H, W), (OD * H * W) ** -0.5, 0.0234375, ((0, 4), (1, 32)))
    return {"upper_level": upper_level, "stride_weight": stride_weight, "middle_weight": middle_weight, "last_weight": last_weight, "cotangent": cotangent}


def stride_conv(upper, weights):
    kernel = weights.reshape(2, 2, 2, weights.shape[1], weights.shape[2])
    return lax.conv_general_dilated(upper[None], kernel, (2, 2, 2), 'VALID', dimension_numbers=('NCDHW', 'DHWOI', 'NCDHW'), precision=lax.Precision.HIGHEST)[0]

def cube_conv(values, weights):
    kernel = weights.reshape(3, 3, 3, weights.shape[1], weights.shape[2])
    return lax.conv_general_dilated(values[None], kernel, (1, 1, 1), [(1, 1), (1, 1), (1, 1)], dimension_numbers=('NCDHW', 'DHWOI', 'NCDHW'), precision=lax.Precision.HIGHEST)[0]

def silu_slope(value):
    sigma = jax.nn.sigmoid(value)
    return sigma * (1.0 + value * (1.0 - sigma))

def reference(upper_level, stride_weight, middle_weight, last_weight, cotangent):
    upper_full = upper_level.astype(jnp.float32)
    stride_full = stride_weight.astype(jnp.float32)
    middle_full = middle_weight.astype(jnp.float32)
    last_full = last_weight.astype(jnp.float32)
    level_pre = stride_conv(upper_full, stride_full)
    level_act = jax.nn.silu(level_pre).astype(jnp.bfloat16)
    level_full = level_act.astype(jnp.float32)
    mid_pre, pull_middle = jax.vjp(cube_conv, level_full, middle_full)
    mid_act = jax.nn.silu(mid_pre).astype(jnp.bfloat16)
    top_pre, pull_last = jax.vjp(cube_conv, mid_act.astype(jnp.float32), last_full)
    result = top_pre.astype(jnp.bfloat16)
    mid_back, grad_last = pull_last(cotangent.astype(jnp.float32))
    mid_delta = (mid_back * silu_slope(mid_pre)).astype(jnp.bfloat16)
    level_back, grad_middle = pull_middle(mid_delta.astype(jnp.float32))
    level_delta = (level_back * silu_slope(level_pre)).astype(jnp.bfloat16)
    _, pull_stride = jax.vjp(lambda kernel: stride_conv(upper_full, kernel), stride_full)
    grad_stride, = pull_stride(level_delta.astype(jnp.float32))
    return (result, grad_stride, grad_middle, grad_last)
```

```python
import jax
import jax.numpy as jnp
from jax import lax
from jax.sharding import PartitionSpec as P


def padded_2(block, sides, width):
    for axis, dim in sides:
        count = lax.axis_size(axis)
        forward = [(i, i + 1) for i in range(count - 1)]
        backward = [(target, source) for source, target in forward]
        low = lax.ppermute(
            lax.slice_in_dim(block, block.shape[dim] - width, None, axis=dim), axis, forward
        )
        high = lax.ppermute(lax.slice_in_dim(block, 0, width, axis=dim), axis, backward)
        block = jnp.concatenate([low, block, high], axis=dim)
    return block


def silu_slope(value):
    sigma = jax.nn.sigmoid(value)
    return sigma * (1.0 + value * (1.0 - sigma))


def split_columns(upper):
    width = upper.shape[3]
    target = jnp.arange(width)
    source = 2 * (target % (width // 2)) + target // (width // 2)
    pick = (jnp.arange(width)[:, None] == source[None, :]).astype(jnp.bfloat16)
    return jnp.einsum("idhw,wv->idhv", upper, pick)


def stride_pick(upper, tap):
    half = upper.shape[3] // 2
    start = tap % 2 * half
    return upper[:, tap // 4 :: 2, tap // 2 % 2 :: 2, start : start + half]


def summed_over_depth(grads):
    count = lax.axis_size("depth")
    rows = jnp.concatenate([grad.reshape(-1, 128) for grad in grads]).astype(jnp.bfloat16)
    total = rows.shape[0]
    share = -(-total // (16 * count)) * 16
    rows = jnp.pad(rows, ((0, share * count - total), (0, 0))).reshape(count, share, 128)
    terms = lax.all_to_all(rows, "depth", 0, 0, tiled=True)
    mine = jnp.sum(terms.astype(jnp.float32), axis=0).astype(jnp.bfloat16)
    spread = jnp.broadcast_to(mine[None], (count, share, 128))
    full = lax.all_to_all(spread, "depth", 0, 0, tiled=True).reshape(-1, 128)
    outs = []
    at = 0
    for grad in grads:
        size = grad.size // 128
        outs.append(full[at : at + size].astype(jnp.float32).reshape(grad.shape))
        at += size
    return outs


def stride_conv(upper, weights):
    total = jnp.einsum(
        "oi,idhw->odhw", weights[0], stride_pick(upper, 0), preferred_element_type=jnp.float32
    )
    for tap in range(1, 8):
        total = total + jnp.einsum(
            "oi,idhw->odhw",
            weights[tap],
            stride_pick(upper, tap),
            preferred_element_type=jnp.float32,
        )
    return total


def stride_weight_grad(upper, grads):
    return jnp.stack(
        [
            jnp.einsum(
                "odhw,idhw->oi", grads, stride_pick(upper, tap), preferred_element_type=jnp.float32
            )
            for tap in range(8)
        ]
    )


def cube_slice(padded, tap, depth_len, row_len, col_len, flip):
    plane_off, row_off, col_off = (tap // 9, tap // 3 % 3, tap % 3)
    if flip:
        plane_off, row_off, col_off = (2 - plane_off, 2 - row_off, 2 - col_off)
    return padded[
        :,
        plane_off : plane_off + depth_len,
        row_off : row_off + row_len,
        col_off : col_off + col_len,
    ]


def cube_conv(padded, weights):
    depth_len, row_len, col_len = (padded.shape[1] - 2, padded.shape[2] - 2, padded.shape[3] - 2)
    total = jnp.einsum(
        "oi,idhw->odhw",
        weights[0],
        cube_slice(padded, 0, depth_len, row_len, col_len, False),
        preferred_element_type=jnp.float32,
    )
    for tap in range(1, 27):
        total = total + jnp.einsum(
            "oi,idhw->odhw",
            weights[tap],
            cube_slice(padded, tap, depth_len, row_len, col_len, False),
            preferred_element_type=jnp.float32,
        )
    return total


def cube_weight_grad(padded, grads):
    depth_len, row_len, col_len = (grads.shape[1], grads.shape[2], grads.shape[3])
    return jnp.stack(
        [
            jnp.einsum(
                "odhw,idhw->oi",
                grads,
                cube_slice(padded, tap, depth_len, row_len, col_len, False),
                preferred_element_type=jnp.float32,
            )
            for tap in range(27)
        ]
    )


def cube_input_grad(padded, weights):
    depth_len, row_len, col_len = (padded.shape[1] - 2, padded.shape[2] - 2, padded.shape[3] - 2)
    total = jnp.einsum(
        "oi,odhw->idhw",
        weights[0],
        cube_slice(padded, 0, depth_len, row_len, col_len, True),
        preferred_element_type=jnp.float32,
    )
    for tap in range(1, 27):
        total = total + jnp.einsum(
            "oi,odhw->idhw",
            weights[tap],
            cube_slice(padded, tap, depth_len, row_len, col_len, True),
            preferred_element_type=jnp.float32,
        )
    return total


def pad_across(value):
    return jnp.pad(value, ((0, 0), (0, 0), (1, 1), (1, 1)))


def depth_rims(value):
    return padded_2(value, (("depth", 1),), 1)


def planes(value):
    return pad_across(depth_rims(value))


def widen(value):
    return pad_across(lax.all_gather(depth_rims(value), "filt", axis=0, tiled=True))


def summed_input_grad(padded, weights):
    return lax.psum_scatter(
        cube_input_grad(padded, weights), "filt", scatter_dimension=0, tiled=True
    )


def per_device(upper_level, stride_weight, middle_weight, last_weight, cotangent):
    upper_all = lax.all_gather(split_columns(upper_level), "filt", axis=2, tiled=True)
    level_pre = stride_conv(upper_all, stride_weight)
    level_act = jax.nn.silu(level_pre).astype(jnp.bfloat16)
    level_wide = widen(level_act)
    mid_pre = cube_conv(level_wide, middle_weight)
    mid_act = jax.nn.silu(mid_pre).astype(jnp.bfloat16)
    mid_wide = widen(mid_act)
    result = cube_conv(mid_wide, last_weight).astype(jnp.bfloat16)
    grad_last = cube_weight_grad(mid_wide, cotangent)
    mid_back = summed_input_grad(planes(cotangent), last_weight)
    mid_delta = (mid_back * silu_slope(mid_pre)).astype(jnp.bfloat16)
    grad_middle = cube_weight_grad(level_wide, mid_delta)
    level_back = summed_input_grad(planes(mid_delta), middle_weight)
    level_delta = (level_back * silu_slope(level_pre)).astype(jnp.bfloat16)
    grad_stride = stride_weight_grad(upper_all, level_delta)
    grad_stride, grad_middle, grad_last = summed_over_depth(
        (grad_stride, grad_middle, grad_last)
    )
    return (result, grad_stride, grad_middle, grad_last)


def solution(mesh):
    placed = (
        P(None, "depth", "filt", None),
        P(None, "filt", None),
        P(None, "filt", None),
        P(None, "filt", None),
        P("filt", "depth", None, None),
    )
    return jax.shard_map(
        per_device,
        mesh=mesh,
        in_specs=placed,
        out_specs=(
            P("filt", "depth", None, None),
            P(None, "filt", None),
            P(None, "filt", None),
            P(None, "filt", None),
        ),
        check_vma=False,
    )
```

```python
import functools

import jax
import jax.numpy as jnp
from jax import lax
from jax.experimental import pallas as pl
from jax.experimental.pallas import tpu as pltpu
from jax.sharding import PartitionSpec as P

AXES = ("depth", "filt")
CELLS = 128
VMEM = pl.BlockSpec(memory_space=pltpu.VMEM)
SMEM = pl.BlockSpec(memory_space=pltpu.SMEM)
TAPS = [(a, b) for a in range(3) for b in range(3)]


def silu_slope(value):
    sigma = jax.nn.sigmoid(value)
    return sigma * (1.0 + value * (1.0 - sigma))


def pairs_of(move):
    depth, filt = lax.axis_size("depth"), lax.axis_size("filt")
    found = []
    for d in range(depth):
        for f in range(filt):
            e, g = move(d, f)
            if 0 <= e < depth and 0 <= g < filt:
                found.append((d * filt + f, e * filt + g))
    return found


def shifted(value, move):
    return lax.ppermute(value, AXES, pairs_of(move))


def swap_core(value):
    return shifted(value, lambda d, f: (d, f ^ 1))


def swap_chip(value):
    return shifted(value, lambda d, f: (d, f ^ 2))


def swap_chip_across(value):
    return shifted(value, lambda d, f: (d ^ 4, f ^ 2))


def four_parts(value, swap):
    far = swap(value)
    return [value, swap_core(value), far, swap_core(far)]


def call(body, out_shape, scratch=(), flops=0, moved=0, in_specs=None):
    many = isinstance(out_shape, (list, tuple))
    return pl.pallas_call(
        body,
        out_shape=out_shape,
        in_specs=in_specs,
        out_specs=[VMEM] * len(out_shape) if many else VMEM,
        scratch_shapes=list(scratch),
        cost_estimate=pl.CostEstimate(flops=flops, bytes_accessed=moved, transcendentals=0),
    )


def shape(dims, dtype=jnp.bfloat16):
    return jax.ShapeDtypeStruct(dims, dtype)


def dot(left, right):
    return jnp.dot(left, right, preferred_element_type=jnp.float32)


def dot_rows(left, right):
    return lax.dot_general(
        left, right, (((1,), (1,)), ((), ())), preferred_element_type=jnp.float32
    )


def stride_body(info, u_ref, s0, s1, s2, s3, act_ref, pre_ref, columns_ref, weights):
    filt = info[1]
    for j, part in enumerate((s0, s1, s2, s3)):
        start = pl.multiple_of((filt ^ j) * 32, 32)
        weights[pl.ds(start, 32), :] = part[...]
    source = lax.broadcasted_iota(jnp.int32, (256, 256), 0)
    target = lax.broadcasted_iota(jnp.int32, (256, 256), 1)
    pick = source == 2 * (target % 128) + target // 128
    pick = jnp.where(pick, 1.0, 0.0).astype(jnp.bfloat16)
    for p in range(2):
        for r in range(2):
            cell = 2 * p + r
            rows = []
            for a in range(2):
                for b in range(2):
                    split = dot(u_ref[2 * p + a, 2 * r + b], pick).astype(jnp.bfloat16)
                    rows += [split[:, :128], split[:, 128:]]
            block = jnp.concatenate(rows, axis=0)
            columns_ref[:, cell * 128 : cell * 128 + 128] = block
            pre = dot(weights[...], block).T
            pre_ref[p, r] = pre
            act_ref[p, r] = (pre * jax.nn.sigmoid(pre)).astype(jnp.bfloat16)


def turn_body(cot_ref, out_ref):
    for p in range(2):
        for r in range(2):
            block = jnp.concatenate([cot_ref[j, p, r] for j in range(4)], axis=0)
            out_ref[p, r] = block.astype(jnp.float32).T.astype(jnp.bfloat16)


def fill_window(window, left, middle, right):
    window[:, 0:2] = left[...]
    window[:, 2:4] = middle[...]
    window[:, 4:6] = right[...]


def fill_forward(weights, parts, filt):
    for j, part in enumerate(parts):
        start = (filt ^ j) * 32
        for n, (a, b) in enumerate(TAPS):
            for c in range(3):
                at = pl.multiple_of(start + c * 128, 32)
                weights[pl.ds(at, 32), n * 128 : n * 128 + 128] = part[9 * a + 3 * b + c]


def fill_backward(weights, parts, filt):
    for j, part in enumerate(parts):
        start = (filt ^ j) * 32
        for n, (a, b) in enumerate(TAPS):
            at = pl.multiple_of(start + n * 128, 32)
            for c in range(3):
                weights[pl.ds(at, 32), c * 128 : c * 128 + 128] = part[9 * a + 3 * b + c]


def column_of(size):
    return lax.broadcasted_iota(jnp.int32, (size, 1), 0) % CELLS


def from_before(value):
    size = value.shape[0]
    return jnp.where(column_of(size) == 0, 0.0, pltpu.roll(value, 1, 0))


def from_after(value):
    size = value.shape[0]
    return jnp.where(column_of(size) == CELLS - 1, 0.0, pltpu.roll(value, size - 1, 0))


def block_of(ref, p, planes, r, rows):
    return ref[pl.ds(p, planes), r : r + rows].reshape(planes * rows * CELLS, 128)


def conv_forward(ref, p, planes, r, rows, weights):
    wide = jnp.concatenate([block_of(ref, p + a, planes, r + b, rows) for a, b in TAPS], axis=1)
    out = dot_rows(wide, weights[...])
    return from_before(out[:, :128]) + out[:, 128:256] + from_after(out[:, 256:])


def conv_backward(ref, p, planes, r, rows, weights):
    wide = jnp.concatenate(
        [block_of(ref, p + 2 - a, planes, r + 2 - b, rows) for a, b in TAPS], axis=1
    )
    out = dot(wide, weights[...])
    return from_after(out[:, :128]) + out[:, 128:256] + from_before(out[:, 256:])


def inside(info, p):
    depth, filt = info[0], info[1]
    row = lax.broadcasted_iota(jnp.int32, (4 * CELLS, 1), 0) // CELLS
    bad = ((depth == 0) & (p == 0)) | ((depth == info[2] - 1) & (p == 3))
    low = jnp.where(filt == 0, 1, 0)
    high = jnp.where(filt == 3, 2, 3)
    low = jnp.where(bad, 4, low)
    return (row >= low) & (row <= high)


def middle_body(
    info, left, mid, right, m0, m1, m2, m3, l0, l1, l2, l3,
    act_ref, pre_ref, result_ref, window, weights_m, weights_l,
):
    filt = info[1]
    fill_window(window, left, mid, right)
    fill_forward(weights_m, (m0, m1, m2, m3), filt)
    fill_forward(weights_l, (l0, l1, l2, l3), filt)

    def plane(p, carry):
        pre = conv_forward(window, p, 1, 0, 4, weights_m)
        act = jnp.where(inside(info, p), pre * jax.nn.sigmoid(pre), 0.0)
        pre_ref[pl.ds(p, 1)] = pre.reshape(1, 4, CELLS, 128)
        act_ref[pl.ds(p, 1)] = act.astype(jnp.bfloat16).reshape(1, 4, CELLS, 128)
        return carry

    lax.fori_loop(0, 4, plane, 0)
    out = conv_forward(act_ref, 0, 2, 0, 2, weights_l)
    for p in range(2):
        for r in range(2):
            at = (2 * p + r) * CELLS
            block = out[at : at + CELLS].T.astype(jnp.bfloat16)
            for f in range(4):
                result_ref[f, p, r] = block[f * 32 : f * 32 + 32]


def shifts_of(value):
    lane = lax.broadcasted_iota(jnp.int32, value.shape, 1) % CELLS
    size = value.shape[1]
    after = jnp.where(lane == CELLS - 1, 0.0, pltpu.roll(value, size - 1, 1))
    before = jnp.where(lane == 0, 0.0, pltpu.roll(value, 1, 1))
    return jnp.concatenate([after, value, before], axis=0).astype(jnp.bfloat16)


def put_kernel_grad(grads_ref, first, grad):
    for n, (a, b) in enumerate(TAPS):
        for c in range(3):
            for f in range(4):
                at = c * 128 + f * 32
                piece = grad[at : at + 32, n * 128 : n * 128 + 128]
                grads_ref[f, first + 9 * a + 3 * b + c] = piece.astype(jnp.bfloat16)


def back_body(
    info, act_l, act_m, act_r, cot_l, cot_m, cot_r, m0, m1, m2, m3, l0, l1, l2, l3,
    mid_act, mid_pre, level_pre, columns, cot_own,
    grads_ref, window, act_window, weights_m, weights_l, delta,
):
    filt = info[1]
    fill_window(window, cot_l, cot_m, cot_r)
    fill_window(act_window, act_l, act_m, act_r)
    fill_backward(weights_l, (l0, l1, l2, l3), filt)
    fill_backward(weights_m, (m0, m1, m2, m3), filt)

    def plane(p, carry):
        back = conv_backward(window, p, 1, 0, 4, weights_l)
        pre = mid_pre[pl.ds(p, 1)].reshape(4 * CELLS, 128)
        here = jnp.where(inside(info, p), back * silu_slope(pre), 0.0)
        delta[pl.ds(p, 1)] = here.astype(jnp.bfloat16).reshape(1, 4, CELLS, 128)
        return carry

    lax.fori_loop(0, 4, plane, 0)

    own = [
        jnp.concatenate([cot_own[j, p, r] for j in range(4)], axis=0).astype(jnp.float32)
        for p in range(2)
        for r in range(2)
    ]
    cot_rows = shifts_of(jnp.concatenate(own, axis=1))
    wide = jnp.concatenate([block_of(mid_act, a, 2, b, 2) for a, b in TAPS], axis=1)
    put_kernel_grad(grads_ref, 0, dot(cot_rows, wide))

    own = [delta[1 + p, 1 + r].astype(jnp.float32).T for p in range(2) for r in range(2)]
    delta_rows = shifts_of(jnp.concatenate(own, axis=1))
    wide = jnp.concatenate([block_of(act_window, 1 + a, 2, 1 + b, 2) for a, b in TAPS], axis=1)
    put_kernel_grad(grads_ref, 27, dot(delta_rows, wide))

    back = conv_backward(delta, 0, 2, 0, 2, weights_m)
    pre = level_pre[...].reshape(4 * CELLS, 128)
    level_delta = (back * silu_slope(pre)).astype(jnp.bfloat16)
    grad = dot(columns[...], level_delta)
    for n in range(4):
        block = grad[n * 128 : n * 128 + 128].T.astype(jnp.bfloat16)
        for f in range(4):
            grads_ref[f, 54 + n] = block[f * 32 : f * 32 + 32]
    for n in range(58, 64):
        for f in range(4):
            grads_ref[f, n] = jnp.zeros((32, 128), jnp.bfloat16)


def neighbourhood(block):
    low = shifted(block, lambda d, f: (d + 1, f))
    high = shifted(block, lambda d, f: (d - 1, f))
    column = jnp.concatenate([low, block, high], axis=0)
    left = shifted(column, lambda d, f: (d, f + 1))
    right = shifted(column, lambda d, f: (d, f - 1))
    return left, column, right


def per_device(upper_level, stride_weight, middle_weight, last_weight, cotangent):
    depth = lax.axis_size("depth")
    info = jnp.stack([lax.axis_index("depth"), lax.axis_index("filt"), jnp.int32(depth)])
    stride_parts = four_parts(stride_weight.transpose(1, 0, 2).reshape(32, 512), swap_chip)
    middle_parts = four_parts(middle_weight, swap_chip)
    last_parts = four_parts(last_weight, swap_chip_across)

    cot_own = cotangent.reshape(32, 2, 4, 2, 128).transpose(2, 1, 3, 0, 4)
    cot_own = lax.all_to_all(cot_own, "filt", 0, 0, tiled=True)
    cot_cells = call(turn_body, shape((2, 2, 128, 128)), in_specs=[VMEM])(cot_own)
    cot_near = neighbourhood(cot_cells)

    upper = upper_level.transpose(1, 2, 0, 3)
    level_act, level_pre, columns = call(
        stride_body,
        [shape((2, 2, 128, 128)), shape((2, 2, 128, 128), jnp.float32), shape((512, 512))],
        [pltpu.VMEM((128, 512), jnp.bfloat16)],
        flops=200_000_000,
        moved=1_500_000,
        in_specs=[SMEM] + [VMEM] * 5,
    )(info, upper, *stride_parts)
    act_near = neighbourhood(level_act)

    mid_act, mid_pre, result = call(
        middle_body,
        [
            shape((4, 4, 128, 128)),
            shape((4, 4, 128, 128), jnp.float32),
            shape((4, 2, 2, 32, 128)),
        ],
        [
            pltpu.VMEM((6, 6, 128, 128), jnp.bfloat16),
            pltpu.VMEM((384, 1152), jnp.bfloat16),
            pltpu.VMEM((384, 1152), jnp.bfloat16),
        ],
        flops=3_000_000_000,
        moved=5_000_000,
        in_specs=[SMEM] + [VMEM] * 11,
    )(info, *act_near, *middle_parts, *last_parts)

    grads = call(
        back_body,
        shape((4, 64, 32, 128)),
        [
            pltpu.VMEM((6, 6, 128, 128), jnp.bfloat16),
            pltpu.VMEM((6, 6, 128, 128), jnp.bfloat16),
            pltpu.VMEM((1152, 384), jnp.bfloat16),
            pltpu.VMEM((1152, 384), jnp.bfloat16),
            pltpu.VMEM((4, 4, 128, 128), jnp.bfloat16),
        ],
        flops=4_000_000_000,
        moved=8_000_000,
        in_specs=[SMEM] + [VMEM] * 19,
    )(
        info, *act_near, *cot_near, *middle_parts, *last_parts,
        mid_act, mid_pre, level_pre, columns, cot_own,
    )

    result = lax.all_to_all(result, "filt", 0, 0, tiled=True)
    result = result.transpose(3, 1, 0, 2, 4).reshape(32, 2, 8, 128)

    terms = grads.reshape(4 * depth, 64, 128)
    terms = lax.all_to_all(terms, ("filt", "depth"), 0, 0, tiled=True)
    mine = jnp.sum(terms.astype(jnp.float32), axis=0).astype(jnp.bfloat16)
    spread = jnp.broadcast_to(mine[None], (depth, 64, 128))
    full = lax.all_to_all(spread, "depth", 0, 0, tiled=True)
    full = full.reshape(64, 32, 128).astype(jnp.float32)
    grad_stride = full[54:58].reshape(4, 32, 2, 64).transpose(0, 2, 1, 3).reshape(8, 32, 64)
    return (result, grad_stride, full[27:54], full[:27])


def solution(mesh):
    placed = (
        P(None, "depth", "filt", None),
        P(None, "filt", None),
        P(None, "filt", None),
        P(None, "filt", None),
        P("filt", "depth", None, None),
    )
    return jax.shard_map(
        per_device,
        mesh=mesh,
        in_specs=placed,
        out_specs=(
            P("filt", "depth", None, None),
            P(None, "filt", None),
            P(None, "filt", None),
            P(None, "filt", None),
        ),
        check_vma=False,
    )
```

```python
import jax
import jax.numpy as jnp
from jax import lax
from jax.experimental import pallas as pl
from jax.experimental.pallas import tpu as pltpu
from jax.sharding import Mesh
from jax.sharding import PartitionSpec as P


AXES = ("depth", "chip", "core")
FILT = ("chip", "core")
CELLS = 128
VMEM = pl.BlockSpec(memory_space=pltpu.VMEM)
SMEM = pl.BlockSpec(memory_space=pltpu.SMEM)
TAPS = [(a, b) for a in range(3) for b in range(3)]


def silu_slope(value):
    sigma = jax.nn.sigmoid(value)
    return sigma * (1.0 + value * (1.0 - sigma))


def pairs_of(move):
    depth, filt = lax.axis_size("depth"), lax.axis_size(FILT)
    found = []
    for d in range(depth):
        for f in range(filt):
            e, g = move(d, f)
            if 0 <= e < depth and 0 <= g < filt:
                found.append((d * filt + f, e * filt + g))
    return found


def shifted(value, move):
    return lax.ppermute(value, AXES, pairs_of(move))


def swap_core(value):
    return shifted(value, lambda d, f: (d, f ^ 1))


def swap_chip(value):
    return shifted(value, lambda d, f: (d, f ^ 2))


def four_parts(value):
    far = swap_chip(value)
    return [value, swap_core(value), far, swap_core(far)]


def four_parts_across(value):
    near = swap_core(value)
    far = shifted(value, lambda d, f: (d ^ 4, f ^ 2))
    both = shifted(value, lambda d, f: (d ^ 4, f ^ 3))
    return [value, near, far, both]


def call(body, out_shape, scratch=(), flops=0, moved=0, in_specs=None):
    many = isinstance(out_shape, (list, tuple))
    return pl.pallas_call(
        body,
        out_shape=out_shape,
        in_specs=in_specs,
        out_specs=[VMEM] * len(out_shape) if many else VMEM,
        scratch_shapes=list(scratch),
        cost_estimate=pl.CostEstimate(flops=flops, bytes_accessed=moved, transcendentals=0),
    )


def shape(dims, dtype=jnp.bfloat16):
    return jax.ShapeDtypeStruct(dims, dtype)


def dot(left, right):
    return jnp.dot(left, right, preferred_element_type=jnp.float32)


def dot_rows(left, right):
    return lax.dot_general(
        left, right, (((1,), (1,)), ((), ())), preferred_element_type=jnp.float32
    )


def stride_body(info, u_ref, s0, s1, s2, s3, act_ref, pre_ref, columns_ref, weights):
    filt = info[1]
    for j, part in enumerate((s0, s1, s2, s3)):
        start = pl.multiple_of((filt ^ j) * 32, 32)
        for tap in range(0, 8, 2):
            pair = jnp.concatenate([part[tap], part[tap + 1]], axis=1)
            weights[pl.ds(start, 32), tap * 64 : tap * 64 + 128] = pair
    source = lax.broadcasted_iota(jnp.int32, (256, 256), 0)
    target = lax.broadcasted_iota(jnp.int32, (256, 256), 1)
    pick = source == 2 * (target % 128) + target // 128
    pick = jnp.where(pick, 1.0, 0.0).astype(jnp.bfloat16)
    for p in range(2):
        for r in range(2):
            cell = 2 * p + r
            rows = []
            for a in range(2):
                for b in range(2):
                    split = dot(u_ref[2 * p + a, 2 * r + b], pick).astype(jnp.bfloat16)
                    rows += [split[:, :128], split[:, 128:]]
            block = jnp.concatenate(rows, axis=0)
            columns_ref[:, cell * 128 : cell * 128 + 128] = block
            pre = dot(weights[...], block).T
            pre_ref[p, r] = pre
            act_ref[p, r] = (pre * jax.nn.sigmoid(pre)).astype(jnp.bfloat16)


def turn_body(info, own, near, far, both, cells_ref, own_ref, tiles):
    filt, chip = info[1], info[3]
    for p in range(6):
        for r in range(6):
            row = 2 * filt - 2 + r
            valid = jnp.where((row >= 0) & (row <= 7), 1.0, 0.0)
            wide = jnp.clip(row, 0, 7)
            cut = jnp.clip(row - 2 * chip, 0, 5)
            for j, (part, at) in enumerate(((own, wide), (near, wide), (far, cut), (both, cut))):
                start = pl.multiple_of((filt ^ j) * 32, 32)
                tiles[p * 6 + r, pl.ds(start, 32), :] = part[p, at]
            tile = tiles[p * 6 + r]
            cells_ref[p, r] = (tile.astype(jnp.float32).T * valid).astype(jnp.bfloat16)
            if 2 <= p < 4 and 2 <= r < 4:
                own_ref[p - 2, r - 2] = tile


def fill_window(window, left, middle, right):
    window[:, 0:2] = left[...]
    window[:, 2:4] = middle[...]
    window[:, 4:6] = right[...]


def fill_forward(weights, parts, filt):
    for j, part in enumerate(parts):
        start = (filt ^ j) * 32
        for n, (a, b) in enumerate(TAPS):
            for c in range(3):
                at = pl.multiple_of(start + c * 128, 32)
                weights[pl.ds(at, 32), n * 128 : n * 128 + 128] = part[9 * a + 3 * b + c]


def fill_backward(weights, parts, filt):
    for j, part in enumerate(parts):
        start = (filt ^ j) * 32
        for n, (a, b) in enumerate(TAPS):
            at = pl.multiple_of(start + n * 128, 32)
            for c in range(3):
                weights[pl.ds(at, 32), c * 128 : c * 128 + 128] = part[9 * a + 3 * b + c]


def column_of(size):
    return lax.broadcasted_iota(jnp.int32, (size, 1), 0) % CELLS


def from_before(value):
    size = value.shape[0]
    return jnp.where(column_of(size) == 0, 0.0, pltpu.roll(value, 1, 0))


def from_after(value):
    size = value.shape[0]
    return jnp.where(column_of(size) == CELLS - 1, 0.0, pltpu.roll(value, size - 1, 0))


def block_of(ref, p, planes, r, rows):
    return ref[pl.ds(p, planes), r : r + rows].reshape(planes * rows * CELLS, 128)


def conv_forward(ref, p, planes, r, rows, weights):
    wide = jnp.concatenate([block_of(ref, p + a, planes, r + b, rows) for a, b in TAPS], axis=1)
    out = dot_rows(wide, weights[...])
    return from_before(out[:, :128]) + out[:, 128:256] + from_after(out[:, 256:])


def conv_backward(ref, p, planes, r, rows, weights):
    wide = jnp.concatenate(
        [block_of(ref, p + 2 - a, planes, r + 2 - b, rows) for a, b in TAPS], axis=1
    )
    out = dot(wide, weights[...])
    return from_after(out[:, :128]) + out[:, 128:256] + from_before(out[:, 256:])


def inside(info, p):
    depth, filt = info[0], info[1]
    row = lax.broadcasted_iota(jnp.int32, (4 * CELLS, 1), 0) // CELLS
    bad = ((depth == 0) & (p == 0)) | ((depth == lax.axis_size("depth") - 1) & (p == 3))
    low = jnp.where(filt == 0, 1, 0)
    high = jnp.where(filt == 3, 2, 3)
    low = jnp.where(bad, 4, low)
    return (row >= low) & (row <= high)


def middle_body(
    info, left, mid, right, m0, m1, m2, m3, act_ref, pre_ref, window, weights
):
    filt = info[1]
    fill_window(window, left, mid, right)
    fill_forward(weights, (m0, m1, m2, m3), filt)

    def plane(p, carry):
        pre = conv_forward(window, p, 1, 0, 4, weights)
        act = jnp.where(inside(info, p), pre * jax.nn.sigmoid(pre), 0.0)
        pre_ref[pl.ds(p, 1)] = pre.reshape(1, 4, CELLS, 128)
        act_ref[pl.ds(p, 1)] = act.astype(jnp.bfloat16).reshape(1, 4, CELLS, 128)
        return carry

    lax.fori_loop(0, 4, plane, 0)


def result_body(info, act_ref, l0, l1, l2, l3, near_ref, far_ref, weights, turned):
    filt = info[1]
    fill_forward(weights, (l0, l1, l2, l3), filt)
    out = conv_forward(act_ref, 0, 2, 0, 2, weights)
    for p in range(2):
        for r in range(2):
            at = (2 * p + r) * CELLS
            turned[...] = out[at : at + CELLS].T.astype(jnp.bfloat16)
            for j, ref in enumerate((near_ref, far_ref, near_ref, far_ref)):
                start = pl.multiple_of((filt ^ j) * 32, 32)
                ref[j // 2, p, r] = turned[pl.ds(start, 32), :]


def rows_body(info, own, near, far, out_ref):
    filt = info[1]
    for j, part in enumerate((own.at[0], near.at[0], far.at[0], far.at[1])):
        out_ref[filt ^ j] = part[...]


def shifts_of(value):
    lane = lax.broadcasted_iota(jnp.int32, value.shape, 1) % CELLS
    size = value.shape[1]
    after = jnp.where(lane == CELLS - 1, 0.0, pltpu.roll(value, size - 1, 1))
    before = jnp.where(lane == 0, 0.0, pltpu.roll(value, 1, 1))
    return jnp.concatenate([after, value, before], axis=0).astype(jnp.bfloat16)


def in_order(ref, at, core):
    rows = [ref[at + (pl.ds(pl.multiple_of((k ^ core) * 32, 32), 32),)] for k in range(4)]
    return jnp.concatenate(rows, axis=0)


def put_grad(refs, slot, block):
    for k in range(4):
        refs[k % 2][k // 2, slot] = block[k * 32 : k * 32 + 32].astype(jnp.bfloat16)


def put_kernel_grad(refs, first, grad):
    for n, (a, b) in enumerate(TAPS):
        for c in range(3):
            block = grad[c * 128 : c * 128 + 128, n * 128 : n * 128 + 128]
            put_grad(refs, first + 9 * a + 3 * b + c, block)


def back_body(
    info, act_l, act_m, act_r, window, m0, m1, m2, m3, l0, l1, l2, l3,
    mid_act, mid_pre, level_pre, columns, cot_own,
    keep_ref, send_ref, act_window, weights_m, weights_l, delta, turned,
):
    filt, core = info[1], info[4]
    refs = (keep_ref, send_ref)
    fill_window(act_window, act_l, act_m, act_r)
    fill_backward(weights_l, (l0, l1, l2, l3), filt)
    fill_backward(weights_m, (m0, m1, m2, m3), filt)

    def plane(p, carry):
        back = conv_backward(window, p, 1, 0, 4, weights_l)
        pre = mid_pre[pl.ds(p, 1)].reshape(4 * CELLS, 128)
        here = jnp.where(inside(info, p), back * silu_slope(pre), 0.0)
        delta[pl.ds(p, 1)] = here.astype(jnp.bfloat16).reshape(1, 4, CELLS, 128)
        return carry

    lax.fori_loop(0, 4, plane, 0)

    own = [in_order(cot_own, (p, r), core).astype(jnp.float32) for p in range(2) for r in range(2)]
    cot_rows = shifts_of(jnp.concatenate(own, axis=1))
    wide = jnp.concatenate([block_of(mid_act, a, 2, b, 2) for a, b in TAPS], axis=1)
    put_kernel_grad(refs, 0, dot(cot_rows, wide))

    for p in range(2):
        for r in range(2):
            at = (2 * p + r) * CELLS
            turned[:, at : at + CELLS] = delta[1 + p, 1 + r].astype(jnp.float32).T
    delta_rows = shifts_of(in_order(turned, (), core))
    wide = jnp.concatenate([block_of(act_window, 1 + a, 2, 1 + b, 2) for a, b in TAPS], axis=1)
    put_kernel_grad(refs, 27, dot(delta_rows, wide))

    back = conv_backward(delta, 0, 2, 0, 2, weights_m)
    pre = level_pre[...].reshape(4 * CELLS, 128)
    level_delta = (back * silu_slope(pre)).astype(jnp.bfloat16)
    grad = dot(columns[...], level_delta)
    for n in range(4):
        turned[:, n * 128 : n * 128 + 128] = grad[n * 128 : n * 128 + 128].T
    ordered = in_order(turned, (), core)
    for n in range(4):
        put_grad(refs, 54 + n, ordered[:, n * 128 : n * 128 + 128])
    for n in range(58, 64):
        put_grad(refs, n, jnp.zeros((128, 128), jnp.float32))


def neighbourhood(block):
    low = shifted(block, lambda d, f: (d + 1, f))
    high = shifted(block, lambda d, f: (d - 1, f))
    column = jnp.concatenate([low, block, high], axis=0)
    left = shifted(column, lambda d, f: (d, f + 1))
    right = shifted(column, lambda d, f: (d, f - 1))
    return left, column, right


def cotangent_parts(cotangent, chip):
    block = cotangent.transpose(1, 2, 0, 3)
    low = shifted(block, lambda d, f: (d + 1, f))
    high = shifted(block, lambda d, f: (d - 1, f))
    column = jnp.concatenate([low, block, high], axis=0)
    wanted = lax.dynamic_slice_in_dim(column, 2 * (1 - chip), 6, axis=1)
    far = swap_chip(wanted)
    return column, swap_core(column), far, swap_core(far)


def whole(upper_level, stride_weight, middle_weight, last_weight, cotangent):
    depth = lax.axis_size("depth")
    chip, core = lax.axis_index("chip"), lax.axis_index("core")
    info = jnp.stack([lax.axis_index("depth"), 2 * chip + core, jnp.int32(depth), chip, core])
    stride_parts = four_parts(stride_weight)
    middle_parts = four_parts(middle_weight)
    last_parts = four_parts_across(last_weight)
    cot_parts = cotangent_parts(cotangent, chip)
    cot_cells, cot_own = call(
        turn_body,
        [shape((6, 6, 128, 128)), shape((2, 2, 128, 128))],
        [pltpu.VMEM((36, 128, 128), jnp.bfloat16)],
        flops=1_000_000,
        moved=3_000_000,
        in_specs=[SMEM] + [VMEM] * 4,
    )(info, *cot_parts)

    upper = upper_level.transpose(1, 2, 0, 3)
    level_act, level_pre, columns = call(
        stride_body,
        [shape((2, 2, 128, 128)), shape((2, 2, 128, 128), jnp.float32), shape((512, 512))],
        [pltpu.VMEM((128, 512), jnp.bfloat16)],
        flops=200_000_000,
        moved=1_500_000,
        in_specs=[SMEM] + [VMEM] * 5,
    )(info, upper, *stride_parts)
    act_near = neighbourhood(level_act)

    mid_act, mid_pre = call(
        middle_body,
        [shape((4, 4, 128, 128)), shape((4, 4, 128, 128), jnp.float32)],
        [
            pltpu.VMEM((6, 6, 128, 128), jnp.bfloat16),
            pltpu.VMEM((384, 1152), jnp.bfloat16),
        ],
        flops=3_000_000_000,
        moved=4_000_000,
        in_specs=[SMEM] + [VMEM] * 7,
    )(info, *act_near, *middle_parts)

    stay, leave = call(
        result_body,
        [shape((2, 2, 2, 32, 128))] * 2,
        [pltpu.VMEM((384, 1152), jnp.bfloat16), pltpu.VMEM((128, 128), jnp.bfloat16)],
        flops=500_000_000,
        moved=2_000_000,
        in_specs=[SMEM] + [VMEM] * 5,
    )(info, mid_act, *last_parts)
    result_near = swap_core(leave)
    result_far = swap_chip(jnp.stack([stay[1], result_near[1]]))

    keep, send = call(
        back_body,
        [shape((2, 64, 32, 128)), shape((2, 64, 32, 128))],
        [
            pltpu.VMEM((6, 6, 128, 128), jnp.bfloat16),
            pltpu.VMEM((1152, 384), jnp.bfloat16),
            pltpu.VMEM((1152, 384), jnp.bfloat16),
            pltpu.VMEM((4, 4, 128, 128), jnp.bfloat16),
            pltpu.VMEM((128, 512), jnp.float32),
        ],
        flops=4_000_000_000,
        moved=8_000_000,
        in_specs=[SMEM] + [VMEM] * 17,
    )(
        info, *act_near, cot_cells, *middle_parts, *last_parts,
        mid_act, mid_pre, level_pre, columns, cot_own,
    )

    result = call(
        rows_body, shape((4, 2, 2, 32, 128)), in_specs=[SMEM] + [VMEM] * 3
    )(info, stay, result_near, result_far)
    result = result.transpose(3, 1, 0, 2, 4).reshape(32, 2, 8, 128)

    other = swap_core(send)
    terms = (keep.astype(jnp.float32) + other.astype(jnp.float32)).astype(jnp.bfloat16)
    terms = lax.all_to_all(terms.reshape(2 * depth, 64, 128), ("chip", "depth"), 0, 0, tiled=True)
    mine = jnp.sum(terms.astype(jnp.float32), axis=0).astype(jnp.bfloat16)
    spread = jnp.broadcast_to(mine[None], (depth, 64, 128))
    full = lax.all_to_all(spread, "depth", 0, 0, tiled=True)
    full = full.reshape(64, 32, 128).astype(jnp.float32)
    grad_stride = full[54:58].reshape(4, 32, 2, 64).transpose(0, 2, 1, 3).reshape(8, 32, 64)
    return (result, grad_stride, full[27:54], full[:27])


def solution(mesh):
    placed = (
        P(None, "depth", FILT, None),
        P(None, FILT, None),
        P(None, FILT, None),
        P(None, FILT, None),
        P(FILT, "depth", None, None),
    )
    fine = Mesh(mesh.devices.reshape(-1, 2, 2), AXES)
    return jax.shard_map(
        whole,
        mesh=fine,
        in_specs=placed,
        out_specs=(
            P(FILT, "depth", None, None),
            P(None, FILT, None),
            P(None, FILT, None),
            P(None, FILT, None),
        ),
        check_vma=False,
    )
```

```python
import jax
import jax.numpy as jnp
from jax import lax
from jax.experimental import pallas as pl
from jax.experimental.pallas import tpu as pltpu
from jax.sharding import Mesh
from jax.sharding import PartitionSpec as P


AXES = ("depth", "chip", "core")
FILT = ("chip", "core")
CELLS = 128
VMEM = pl.BlockSpec(memory_space=pltpu.VMEM)
SMEM = pl.BlockSpec(memory_space=pltpu.SMEM)
TAPS = [(a, b) for a in range(3) for b in range(3)]


def silu_slope(value):
    sigma = jax.nn.sigmoid(value)
    return sigma * (1.0 + value * (1.0 - sigma))


def pairs_of(move):
    depth, filt = lax.axis_size("depth"), lax.axis_size(FILT)
    found = []
    for d in range(depth):
        for f in range(filt):
            e, g = move(d, f)
            if 0 <= e < depth and 0 <= g < filt:
                found.append((d * filt + f, e * filt + g))
    return found


def shifted(value, move):
    return lax.ppermute(value, AXES, pairs_of(move))


def swap_core(value):
    return shifted(value, lambda d, f: (d, f ^ 1))


def swap_chip(value):
    return shifted(value, lambda d, f: (d, f ^ 2))


def four_parts(value, turn):
    far = shifted(value, lambda d, f: (d ^ turn, f ^ 2))
    return [value, swap_core(value), far, swap_core(far)]


def four_parts_direct(value):
    return [value] + [shifted(value, lambda d, f, step=step: (d, f ^ step)) for step in (1, 2, 3)]


def call(body, out_shape, scratch=(), flops=0, moved=0, in_specs=None):
    many = isinstance(out_shape, (list, tuple))
    return pl.pallas_call(
        body,
        out_shape=out_shape,
        in_specs=in_specs,
        out_specs=[VMEM] * len(out_shape) if many else VMEM,
        scratch_shapes=list(scratch),
        cost_estimate=pl.CostEstimate(flops=flops, bytes_accessed=moved, transcendentals=0),
    )


def shape(dims, dtype=jnp.bfloat16):
    return jax.ShapeDtypeStruct(dims, dtype)


def dot(left, right):
    return jnp.dot(left, right, preferred_element_type=jnp.float32)


def dot_rows(left, right):
    return lax.dot_general(
        left, right, (((1,), (1,)), ((), ())), preferred_element_type=jnp.float32
    )


def stride_body(info, u_ref, s0, s1, s2, s3, cot_ref, pack_ref, pre_ref, columns_ref, weights):
    filt = info[1]
    for j, part in enumerate((s0, s1, s2, s3)):
        start = pl.multiple_of((filt ^ j) * 32, 32)
        for tap in range(0, 8, 2):
            pair = jnp.concatenate([part[tap], part[tap + 1]], axis=1)
            weights[pl.ds(start, 32), tap * 64 : tap * 64 + 128] = pair
    source = lax.broadcasted_iota(jnp.int32, (256, 256), 0)
    target = lax.broadcasted_iota(jnp.int32, (256, 256), 1)
    pick = source == 2 * (target % 128) + target // 128
    pick = jnp.where(pick, 1.0, 0.0).astype(jnp.bfloat16)
    for p in range(2):
        for r in range(2):
            cell = 2 * p + r
            rows = []
            for a in range(2):
                for b in range(2):
                    split = dot(u_ref[2 * p + a, 2 * r + b], pick).astype(jnp.bfloat16)
                    rows += [split[:, :128], split[:, 128:]]
            block = jnp.concatenate(rows, axis=0)
            columns_ref[:, cell * 128 : cell * 128 + 128] = block
            pre = dot(weights[...], block).T
            pre_ref[p, r] = pre
            pack_ref[p, r] = (pre * jax.nn.sigmoid(pre)).astype(jnp.bfloat16)
    pack_ref[:, 2:4] = cot_ref[...]


def turn_body(info, own, near, far, both, cells_ref, own_ref, tiles):
    filt, chip = info[1], info[3]
    for p in range(6):
        for r in range(6):
            row = 2 * filt - 2 + r
            valid = jnp.where((row >= 0) & (row <= 7), 1.0, 0.0)
            wide = jnp.clip(row, 0, 7)
            cut = jnp.clip(row - 2 * chip, 0, 5)
            for j, (part, at) in enumerate(((own, wide), (near, wide), (far, cut), (both, cut))):
                start = pl.multiple_of((filt ^ j) * 32, 32)
                tiles[p * 6 + r, pl.ds(start, 32), :] = part[p, at]
            tile = tiles[p * 6 + r]
            cells_ref[p, r] = (tile.astype(jnp.float32).T * valid).astype(jnp.bfloat16)
            if 2 <= p < 4 and 2 <= r < 4:
                own_ref[p - 2, r - 2] = tile


def fill_window(window, left, middle, right):
    window[:, 0:2] = left[...]
    window[:, 2:4] = middle[...]
    window[:, 4:6] = right[...]


def fill_forward(weights, parts, filt):
    for j, part in enumerate(parts):
        start = (filt ^ j) * 32
        for n, (a, b) in enumerate(TAPS):
            for c in range(3):
                at = pl.multiple_of(start + c * 128, 32)
                weights[pl.ds(at, 32), n * 128 : n * 128 + 128] = part[9 * a + 3 * b + c]


def fill_backward(weights, parts, filt):
    for j, part in enumerate(parts):
        start = (filt ^ j) * 32
        for n, (a, b) in enumerate(TAPS):
            at = pl.multiple_of(start + n * 128, 32)
            for c in range(3):
                weights[pl.ds(at, 32), c * 128 : c * 128 + 128] = part[9 * a + 3 * b + c]


def column_of(size):
    return lax.broadcasted_iota(jnp.int32, (size, 1), 0) % CELLS


def from_before(value):
    size = value.shape[0]
    return jnp.where(column_of(size) == 0, 0.0, pltpu.roll(value, 1, 0))


def from_after(value):
    size = value.shape[0]
    return jnp.where(column_of(size) == CELLS - 1, 0.0, pltpu.roll(value, size - 1, 0))


def block_of(ref, p, planes, r, rows):
    return ref[pl.ds(p, planes), r : r + rows].reshape(planes * rows * CELLS, 128)


def conv_forward(ref, p, planes, r, rows, weights):
    wide = jnp.concatenate([block_of(ref, p + a, planes, r + b, rows) for a, b in TAPS], axis=1)
    out = dot_rows(wide, weights[...])
    return from_before(out[:, :128]) + out[:, 128:256] + from_after(out[:, 256:])


def conv_backward(ref, p, planes, r, rows, weights):
    wide = jnp.concatenate(
        [block_of(ref, p + 2 - a, planes, r + 2 - b, rows) for a, b in TAPS], axis=1
    )
    out = dot(wide, weights[...])
    return from_after(out[:, :128]) + out[:, 128:256] + from_before(out[:, 256:])


def inside(info, p):
    depth, filt = info[0], info[1]
    row = lax.broadcasted_iota(jnp.int32, (4 * CELLS, 1), 0) // CELLS
    bad = ((depth == 0) & (p == 0)) | ((depth == lax.axis_size("depth") - 1) & (p == 3))
    low = jnp.where(filt == 0, 1, 0)
    high = jnp.where(filt == 3, 2, 3)
    low = jnp.where(bad, 4, low)
    return (row >= low) & (row <= high)


def middle_body(
    info, left, mid, right, m0, m1, m2, m3, act_ref, pre_ref, window, weights
):
    filt = info[1]
    fill_window(window, left, mid, right)
    fill_forward(weights, (m0, m1, m2, m3), filt)

    def plane(p, carry):
        pre = conv_forward(window, p, 1, 0, 4, weights)
        act = jnp.where(inside(info, p), pre * jax.nn.sigmoid(pre), 0.0)
        pre_ref[pl.ds(p, 1)] = pre.reshape(1, 4, CELLS, 128)
        act_ref[pl.ds(p, 1)] = act.astype(jnp.bfloat16).reshape(1, 4, CELLS, 128)
        return carry

    lax.fori_loop(0, 4, plane, 0)


def result_body(info, act_ref, l0, l1, l2, l3, near_ref, far_ref, weights, turned):
    filt = info[1]
    fill_forward(weights, (l0, l1, l2, l3), filt)
    out = conv_forward(act_ref, 0, 2, 0, 2, weights)
    for p in range(2):
        for r in range(2):
            at = (2 * p + r) * CELLS
            turned[...] = out[at : at + CELLS].T.astype(jnp.bfloat16)
            for j, ref in enumerate((near_ref, far_ref, near_ref, far_ref)):
                start = pl.multiple_of((filt ^ j) * 32, 32)
                ref[j // 2, p, r] = turned[pl.ds(start, 32), :]


def rows_body(info, own, near, far, out_ref):
    filt = info[1]
    for j, part in enumerate((own.at[0], near.at[0], far.at[0], far.at[1])):
        out_ref[filt ^ j] = part[...]


def shifts_of(value):
    lane = lax.broadcasted_iota(jnp.int32, value.shape, 1) % CELLS
    size = value.shape[1]
    after = jnp.where(lane == CELLS - 1, 0.0, pltpu.roll(value, size - 1, 1))
    before = jnp.where(lane == 0, 0.0, pltpu.roll(value, 1, 1))
    return jnp.concatenate([after, value, before], axis=0).astype(jnp.bfloat16)


def in_order(ref, at, core):
    rows = [ref[at + (pl.ds(pl.multiple_of((k ^ core) * 32, 32), 32),)] for k in range(4)]
    return jnp.concatenate(rows, axis=0)


def put_grad(refs, slot, block):
    for k in range(4):
        refs[k % 2][k // 2, slot] = block[k * 32 : k * 32 + 32].astype(jnp.bfloat16)


def put_kernel_grad(refs, first, grad):
    for n, (a, b) in enumerate(TAPS):
        for c in range(3):
            block = grad[c * 128 : c * 128 + 128, n * 128 : n * 128 + 128]
            put_grad(refs, first + 9 * a + 3 * b + c, block)


def back_body(
    info, act_l, act_m, act_r, window, m0, m1, m2, m3, l0, l1, l2, l3,
    mid_act, mid_pre, level_pre, columns, cot_own,
    keep_ref, send_ref, act_window, weights_m, weights_l, delta, turned,
):
    filt, core = info[1], info[4]
    refs = (keep_ref, send_ref)
    fill_window(act_window, act_l, act_m, act_r)
    fill_backward(weights_l, (l0, l1, l2, l3), filt)
    fill_backward(weights_m, (m0, m1, m2, m3), filt)

    def plane(p, carry):
        back = conv_backward(window, p, 1, 0, 4, weights_l)
        pre = mid_pre[pl.ds(p, 1)].reshape(4 * CELLS, 128)
        here = jnp.where(inside(info, p), back * silu_slope(pre), 0.0)
        delta[pl.ds(p, 1)] = here.astype(jnp.bfloat16).reshape(1, 4, CELLS, 128)
        return carry

    lax.fori_loop(0, 4, plane, 0)

    own = [in_order(cot_own, (p, r), core).astype(jnp.float32) for p in range(2) for r in range(2)]
    cot_rows = shifts_of(jnp.concatenate(own, axis=1))
    wide = jnp.concatenate([block_of(mid_act, a, 2, b, 2) for a, b in TAPS], axis=1)
    put_kernel_grad(refs, 0, dot(cot_rows, wide))

    for p in range(2):
        for r in range(2):
            at = (2 * p + r) * CELLS
            turned[:, at : at + CELLS] = delta[1 + p, 1 + r].astype(jnp.float32).T
    delta_rows = shifts_of(in_order(turned, (), core))
    wide = jnp.concatenate([block_of(act_window, 1 + a, 2, 1 + b, 2) for a, b in TAPS], axis=1)
    put_kernel_grad(refs, 27, dot(delta_rows, wide))

    back = conv_backward(delta, 0, 2, 0, 2, weights_m)
    pre = level_pre[...].reshape(4 * CELLS, 128)
    level_delta = (back * silu_slope(pre)).astype(jnp.bfloat16)
    grad = dot(columns[...], level_delta)
    for n in range(4):
        turned[:, n * 128 : n * 128 + 128] = grad[n * 128 : n * 128 + 128].T
    ordered = in_order(turned, (), core)
    for n in range(4):
        put_grad(refs, 54 + n, ordered[:, n * 128 : n * 128 + 128])
    for n in range(58, 64):
        put_grad(refs, n, jnp.zeros((128, 128), jnp.float32))


def row_parts(column):
    left = shifted(column, lambda d, f: (d, f + 1))
    right = shifted(column, lambda d, f: (d, f - 1))
    return left, column, right


def cotangent_parts(column, chip):
    wanted = lax.dynamic_slice_in_dim(column, 2 * (1 - chip), 6, axis=1)
    far = swap_chip(wanted)
    return column, swap_core(column), far, swap_core(far)


def whole(upper_level, stride_weight, middle_weight, last_weight, cotangent):
    depth = lax.axis_size("depth")
    chip, core = lax.axis_index("chip"), lax.axis_index("core")
    info = jnp.stack([lax.axis_index("depth"), 2 * chip + core, jnp.int32(depth), chip, core])
    stride_parts = four_parts_direct(stride_weight)
    middle_parts = four_parts(middle_weight, 0)
    last_parts = four_parts(last_weight, 4)
    upper = upper_level.transpose(1, 2, 0, 3)
    cot_rows = cotangent.transpose(1, 2, 0, 3).reshape(2, 2, 128, 128)
    pack, level_pre, columns = call(
        stride_body,
        [shape((2, 4, 128, 128)), shape((2, 2, 128, 128), jnp.float32), shape((512, 512))],
        [pltpu.VMEM((128, 512), jnp.bfloat16)],
        flops=200_000_000,
        moved=1_500_000,
        in_specs=[SMEM] + [VMEM] * 6,
    )(info, upper, *stride_parts, cot_rows)
    low = shifted(pack, lambda d, f: (d + 1, f))
    high = shifted(pack, lambda d, f: (d - 1, f))
    act_near = row_parts(jnp.concatenate([x[:, :2] for x in (low, pack, high)], axis=0))
    cot_column = jnp.concatenate([x[:, 2:] for x in (low, pack, high)], axis=0)
    cot_parts = cotangent_parts(cot_column.reshape(6, 8, 32, 128), chip)
    cot_cells, cot_own = call(
        turn_body,
        [shape((6, 6, 128, 128)), shape((2, 2, 128, 128))],
        [pltpu.VMEM((36, 128, 128), jnp.bfloat16)],
        flops=1_000_000,
        moved=3_000_000,
        in_specs=[SMEM] + [VMEM] * 4,
    )(info, *cot_parts)

    mid_act, mid_pre = call(
        middle_body,
        [shape((4, 4, 128, 128)), shape((4, 4, 128, 128), jnp.float32)],
        [
            pltpu.VMEM((6, 6, 128, 128), jnp.bfloat16),
            pltpu.VMEM((384, 1152), jnp.bfloat16),
        ],
        flops=3_000_000_000,
        moved=4_000_000,
        in_specs=[SMEM] + [VMEM] * 7,
    )(info, *act_near, *middle_parts)

    stay, leave = call(
        result_body,
        [shape((2, 2, 2, 32, 128))] * 2,
        [pltpu.VMEM((384, 1152), jnp.bfloat16), pltpu.VMEM((128, 128), jnp.bfloat16)],
        flops=500_000_000,
        moved=2_000_000,
        in_specs=[SMEM] + [VMEM] * 5,
    )(info, mid_act, *last_parts)
    result_near = swap_core(leave)
    result_far = swap_chip(jnp.stack([stay[1], result_near[1]]))

    keep, send = call(
        back_body,
        [shape((2, 64, 32, 128)), shape((2, 64, 32, 128))],
        [
            pltpu.VMEM((6, 6, 128, 128), jnp.bfloat16),
            pltpu.VMEM((1152, 384), jnp.bfloat16),
            pltpu.VMEM((1152, 384), jnp.bfloat16),
            pltpu.VMEM((4, 4, 128, 128), jnp.bfloat16),
            pltpu.VMEM((128, 512), jnp.float32),
        ],
        flops=4_000_000_000,
        moved=8_000_000,
        in_specs=[SMEM] + [VMEM] * 17,
    )(
        info, *act_near, cot_cells, *middle_parts, *last_parts,
        mid_act, mid_pre, level_pre, columns, cot_own,
    )

    result = call(
        rows_body, shape((4, 2, 2, 32, 128)), in_specs=[SMEM] + [VMEM] * 3
    )(info, stay, result_near, result_far)
    result = result.transpose(3, 1, 0, 2, 4).reshape(32, 2, 8, 128)

    other = swap_core(send)
    terms = (keep.astype(jnp.float32) + other.astype(jnp.float32)).astype(jnp.bfloat16)
    terms = lax.all_to_all(terms.reshape(2 * depth, 64, 128), ("chip", "depth"), 0, 0, tiled=True)
    mine = jnp.sum(terms.astype(jnp.float32), axis=0).astype(jnp.bfloat16)
    spread = jnp.broadcast_to(mine[None], (depth, 64, 128))
    full = lax.all_to_all(spread, "depth", 0, 0, tiled=True)
    full = full.reshape(64, 32, 128).astype(jnp.float32)
    grad_stride = full[54:58].reshape(4, 32, 2, 64).transpose(0, 2, 1, 3).reshape(8, 32, 64)
    return (result, grad_stride, full[27:54], full[:27])


def solution(mesh):
    placed = (
        P(None, "depth", FILT, None),
        P(None, FILT, None),
        P(None, FILT, None),
        P(None, FILT, None),
        P(FILT, "depth", None, None),
    )
    fine = Mesh(mesh.devices.reshape(-1, 2, 2), AXES)
    return jax.shard_map(
        whole,
        mesh=fine,
        in_specs=placed,
        out_specs=(
            P(FILT, "depth", None, None),
            P(None, FILT, None),
            P(None, FILT, None),
            P(None, FILT, None),
        ),
        check_vma=False,
    )
```

```python
import jax
import jax.numpy as jnp
from jax import lax
from jax.experimental import pallas as pl
from jax.experimental.pallas import tpu as pltpu
from jax.sharding import Mesh
from jax.sharding import PartitionSpec as P


AXES = ("depth", "chip", "core")
FILT = ("chip", "core")
CELLS = 128
LIMITS = {"stride": 8, "turn": 8, "middle": 14, "result": 8, "back": 24, "rows": 2}
VMEM = pl.BlockSpec(memory_space=pltpu.VMEM)
SMEM = pl.BlockSpec(memory_space=pltpu.SMEM)
TAPS = [(a, b) for a in range(3) for b in range(3)]


def silu_slope(value):
    sigma = jax.nn.sigmoid(value)
    return sigma * (1.0 + value * (1.0 - sigma))


def pairs_of(move):
    depth, filt = lax.axis_size("depth"), lax.axis_size(FILT)
    found = []
    for d in range(depth):
        for f in range(filt):
            e, g = move(d, f)
            if 0 <= e < depth and 0 <= g < filt:
                found.append((d * filt + f, e * filt + g))
    return found


def shifted(value, move):
    return lax.ppermute(value, AXES, pairs_of(move))


def swap_core(value):
    return shifted(value, lambda d, f: (d, f ^ 1))


def swap_chip(value):
    return shifted(value, lambda d, f: (d, f ^ 2))


def four_parts(value, turn):
    far = shifted(value, lambda d, f: (d ^ turn, f ^ 2))
    return [value, swap_core(value), far, swap_core(far)]


def four_parts_direct(value):
    return [value] + [shifted(value, lambda d, f, step=step: (d, f ^ step)) for step in (1, 2, 3)]


def call(name, body, out_shape, scratch=(), flops=0, moved=0, in_specs=None):
    many = isinstance(out_shape, (list, tuple))
    return pl.pallas_call(
        body,
        out_shape=out_shape,
        in_specs=in_specs,
        out_specs=[VMEM] * len(out_shape) if many else VMEM,
        scratch_shapes=list(scratch),
        compiler_params=pltpu.CompilerParams(vmem_limit_bytes=LIMITS[name] << 20),
        cost_estimate=pl.CostEstimate(flops=flops, bytes_accessed=moved, transcendentals=0),
    )


def shape(dims, dtype=jnp.bfloat16):
    return jax.ShapeDtypeStruct(dims, dtype)


def dot(left, right):
    return jnp.dot(left, right, preferred_element_type=jnp.float32)


def dot_rows(left, right):
    return lax.dot_general(
        left, right, (((1,), (1,)), ((), ())), preferred_element_type=jnp.float32
    )


def stride_body(info, u_ref, s0, s1, s2, s3, cot_ref, pack_ref, pre_ref, columns_ref, weights):
    filt = info[1]
    for j, part in enumerate((s0, s1, s2, s3)):
        start = pl.multiple_of((filt ^ j) * 32, 32)
        for tap in range(0, 8, 2):
            pair = jnp.concatenate([part[tap], part[tap + 1]], axis=1)
            weights[pl.ds(start, 32), tap * 64 : tap * 64 + 128] = pair
    source = lax.broadcasted_iota(jnp.int32, (256, 256), 0)
    target = lax.broadcasted_iota(jnp.int32, (256, 256), 1)
    pick = source == 2 * (target % 128) + target // 128
    pick = jnp.where(pick, 1.0, 0.0).astype(jnp.bfloat16)
    for p in range(2):
        for r in range(2):
            cell = 2 * p + r
            rows = []
            for a in range(2):
                for b in range(2):
                    split = dot(u_ref[2 * p + a, 2 * r + b], pick).astype(jnp.bfloat16)
                    rows += [split[:, :128], split[:, 128:]]
            block = jnp.concatenate(rows, axis=0)
            columns_ref[:, cell * 128 : cell * 128 + 128] = block
            pre = dot(weights[...], block).T
            pre_ref[p, r] = pre
            pack_ref[p, r] = (pre * jax.nn.sigmoid(pre)).astype(jnp.bfloat16)
    pack_ref[:, 2:4] = cot_ref[...]


def turn_body(info, own, near, far, both, cells_ref, own_ref, tiles):
    filt, chip = info[1], info[3]
    for p in range(6):
        for r in range(6):
            row = 2 * filt - 2 + r
            valid = jnp.where((row >= 0) & (row <= 7), 1.0, 0.0)
            wide = jnp.clip(row, 0, 7)
            cut = jnp.clip(row - 2 * chip, 0, 5)
            for j, (part, at) in enumerate(((own, wide), (near, wide), (far, cut), (both, cut))):
                start = pl.multiple_of((filt ^ j) * 32, 32)
                tiles[p * 6 + r, pl.ds(start, 32), :] = part[p, at]
            tile = tiles[p * 6 + r]
            cells_ref[p, r] = (tile.astype(jnp.float32).T * valid).astype(jnp.bfloat16)
            if 2 <= p < 4 and 2 <= r < 4:
                own_ref[p - 2, r - 2] = tile


def fill_window(window, left, middle, right):
    window[:, 0:2] = left[...]
    window[:, 2:4] = middle[...]
    window[:, 4:6] = right[...]


def fill_forward(weights, parts, filt):
    for j, part in enumerate(parts):
        start = (filt ^ j) * 32
        for n, (a, b) in enumerate(TAPS):
            for c in range(3):
                at = pl.multiple_of(start + c * 128, 32)
                weights[pl.ds(at, 32), n * 128 : n * 128 + 128] = part[9 * a + 3 * b + c]


def fill_backward(weights, parts, filt):
    for j, part in enumerate(parts):
        start = (filt ^ j) * 32
        for n, (a, b) in enumerate(TAPS):
            at = pl.multiple_of(start + n * 128, 32)
            for c in range(3):
                weights[pl.ds(at, 32), c * 128 : c * 128 + 128] = part[9 * a + 3 * b + c]


def column_of(size):
    return lax.broadcasted_iota(jnp.int32, (size, 1), 0) % CELLS


def from_before(value):
    size = value.shape[0]
    return jnp.where(column_of(size) == 0, 0.0, pltpu.roll(value, 1, 0))


def from_after(value):
    size = value.shape[0]
    return jnp.where(column_of(size) == CELLS - 1, 0.0, pltpu.roll(value, size - 1, 0))


def block_of(ref, p, planes, r, rows):
    return ref[pl.ds(p, planes), r : r + rows].reshape(planes * rows * CELLS, 128)


def conv_forward(ref, p, planes, r, rows, weights):
    wide = jnp.concatenate([block_of(ref, p + a, planes, r + b, rows) for a, b in TAPS], axis=1)
    out = dot_rows(wide, weights[...])
    return from_before(out[:, :128]) + out[:, 128:256] + from_after(out[:, 256:])


def conv_backward(ref, p, planes, r, rows, weights):
    wide = jnp.concatenate(
        [block_of(ref, p + 2 - a, planes, r + 2 - b, rows) for a, b in TAPS], axis=1
    )
    out = dot(wide, weights[...])
    return from_after(out[:, :128]) + out[:, 128:256] + from_before(out[:, 256:])


def inside(info, p):
    depth, filt = info[0], info[1]
    row = lax.broadcasted_iota(jnp.int32, (4 * CELLS, 1), 0) // CELLS
    bad = ((depth == 0) & (p == 0)) | ((depth == lax.axis_size("depth") - 1) & (p == 3))
    low = jnp.where(filt == 0, 1, 0)
    high = jnp.where(filt == 3, 2, 3)
    low = jnp.where(bad, 4, low)
    return (row >= low) & (row <= high)


def middle_body(
    info, left, mid, right, m0, m1, m2, m3, act_ref, pre_ref, window, weights
):
    filt = info[1]
    fill_window(window, left, mid, right)
    fill_forward(weights, (m0, m1, m2, m3), filt)

    def plane(p, carry):
        pre = conv_forward(window, p, 1, 0, 4, weights)
        act = jnp.where(inside(info, p), pre * jax.nn.sigmoid(pre), 0.0)
        pre_ref[pl.ds(p, 1)] = pre.reshape(1, 4, CELLS, 128)
        act_ref[pl.ds(p, 1)] = act.astype(jnp.bfloat16).reshape(1, 4, CELLS, 128)
        return carry

    lax.fori_loop(0, 4, plane, 0)


def result_body(info, act_ref, l0, l1, l2, l3, near_ref, far_ref, weights, turned):
    filt = info[1]
    fill_forward(weights, (l0, l1, l2, l3), filt)
    out = conv_forward(act_ref, 0, 2, 0, 2, weights)
    for p in range(2):
        for r in range(2):
            at = (2 * p + r) * CELLS
            turned[...] = out[at : at + CELLS].T.astype(jnp.bfloat16)
            for j, ref in enumerate((near_ref, far_ref, near_ref, far_ref)):
                start = pl.multiple_of((filt ^ j) * 32, 32)
                ref[j // 2, p, r] = turned[pl.ds(start, 32), :]


def rows_body(info, own, near, far, out_ref):
    filt = info[1]
    for j, part in enumerate((own.at[0], near.at[0], far.at[0], far.at[1])):
        out_ref[filt ^ j] = part[...]


def shifts_of(value):
    lane = lax.broadcasted_iota(jnp.int32, value.shape, 1) % CELLS
    size = value.shape[1]
    after = jnp.where(lane == CELLS - 1, 0.0, pltpu.roll(value, size - 1, 1))
    before = jnp.where(lane == 0, 0.0, pltpu.roll(value, 1, 1))
    return jnp.concatenate([after, value, before], axis=0).astype(jnp.bfloat16)


def in_order(ref, at, core):
    rows = [ref[at + (pl.ds(pl.multiple_of((k ^ core) * 32, 32), 32),)] for k in range(4)]
    return jnp.concatenate(rows, axis=0)


def put_grad(refs, slot, block):
    for k in range(4):
        refs[k % 2][k // 2, slot] = block[k * 32 : k * 32 + 32].astype(jnp.bfloat16)


def put_kernel_grad(refs, first, grad):
    for n, (a, b) in enumerate(TAPS):
        for c in range(3):
            block = grad[c * 128 : c * 128 + 128, n * 128 : n * 128 + 128]
            put_grad(refs, first + 9 * a + 3 * b + c, block)


def back_body(
    info, act_l, act_m, act_r, window, m0, m1, m2, m3, l0, l1, l2, l3,
    mid_act, mid_pre, level_pre, columns, cot_own,
    keep_ref, send_ref, act_window, weights_m, weights_l, delta, turned,
):
    filt, core = info[1], info[4]
    refs = (keep_ref, send_ref)
    fill_window(act_window, act_l, act_m, act_r)
    fill_backward(weights_l, (l0, l1, l2, l3), filt)
    fill_backward(weights_m, (m0, m1, m2, m3), filt)

    def plane(p, carry):
        back = conv_backward(window, p, 1, 0, 4, weights_l)
        pre = mid_pre[pl.ds(p, 1)].reshape(4 * CELLS, 128)
        here = jnp.where(inside(info, p), back * silu_slope(pre), 0.0)
        delta[pl.ds(p, 1)] = here.astype(jnp.bfloat16).reshape(1, 4, CELLS, 128)
        return carry

    lax.fori_loop(0, 4, plane, 0)

    own = [in_order(cot_own, (p, r), core).astype(jnp.float32) for p in range(2) for r in range(2)]
    cot_rows = shifts_of(jnp.concatenate(own, axis=1))
    wide = jnp.concatenate([block_of(mid_act, a, 2, b, 2) for a, b in TAPS], axis=1)
    put_kernel_grad(refs, 0, dot(cot_rows, wide))

    for p in range(2):
        for r in range(2):
            at = (2 * p + r) * CELLS
            turned[:, at : at + CELLS] = delta[1 + p, 1 + r].astype(jnp.float32).T
    delta_rows = shifts_of(in_order(turned, (), core))
    wide = jnp.concatenate([block_of(act_window, 1 + a, 2, 1 + b, 2) for a, b in TAPS], axis=1)
    put_kernel_grad(refs, 27, dot(delta_rows, wide))

    back = conv_backward(delta, 0, 2, 0, 2, weights_m)
    pre = level_pre[...].reshape(4 * CELLS, 128)
    level_delta = (back * silu_slope(pre)).astype(jnp.bfloat16)
    grad = dot(columns[...], level_delta)
    for n in range(4):
        turned[:, n * 128 : n * 128 + 128] = grad[n * 128 : n * 128 + 128].T
    ordered = in_order(turned, (), core)
    for n in range(4):
        put_grad(refs, 54 + n, ordered[:, n * 128 : n * 128 + 128])
    for n in range(58, 64):
        put_grad(refs, n, jnp.zeros((128, 128), jnp.float32))


def row_parts(column):
    left = shifted(column, lambda d, f: (d, f + 1))
    right = shifted(column, lambda d, f: (d, f - 1))
    return left, column, right


def cotangent_parts(column, chip):
    wanted = lax.dynamic_slice_in_dim(column, 2 * (1 - chip), 6, axis=1)
    far = swap_chip(wanted)
    return column, swap_core(column), far, swap_core(far)


def whole(upper_level, stride_weight, middle_weight, last_weight, cotangent):
    depth = lax.axis_size("depth")
    chip, core = lax.axis_index("chip"), lax.axis_index("core")
    info = jnp.stack([lax.axis_index("depth"), 2 * chip + core, jnp.int32(depth), chip, core])
    stride_parts = four_parts_direct(stride_weight)
    middle_parts = four_parts(middle_weight, 0)
    last_parts = four_parts(last_weight, 4)
    upper = upper_level.transpose(1, 2, 0, 3)
    cot_rows = cotangent.transpose(1, 2, 0, 3).reshape(2, 2, 128, 128)
    pack, level_pre, columns = call(
        "stride",
        stride_body,
        [shape((2, 4, 128, 128)), shape((2, 2, 128, 128), jnp.float32), shape((512, 512))],
        [pltpu.VMEM((128, 512), jnp.bfloat16)],
        flops=200_000_000,
        moved=1_500_000,
        in_specs=[SMEM] + [VMEM] * 6,
    )(info, upper, *stride_parts, cot_rows)
    low = shifted(pack, lambda d, f: (d + 1, f))
    high = shifted(pack, lambda d, f: (d - 1, f))
    act_near = row_parts(jnp.concatenate([x[:, :2] for x in (low, pack, high)], axis=0))
    cot_column = jnp.concatenate([x[:, 2:] for x in (low, pack, high)], axis=0)
    cot_parts = cotangent_parts(cot_column.reshape(6, 8, 32, 128), chip)
    cot_cells, cot_own = call(
        "turn",
        turn_body,
        [shape((6, 6, 128, 128)), shape((2, 2, 128, 128))],
        [pltpu.VMEM((36, 128, 128), jnp.bfloat16)],
        flops=1_000_000,
        moved=3_000_000,
        in_specs=[SMEM] + [VMEM] * 4,
    )(info, *cot_parts)

    mid_act, mid_pre = call(
        "middle",
        middle_body,
        [shape((4, 4, 128, 128)), shape((4, 4, 128, 128), jnp.float32)],
        [
            pltpu.VMEM((6, 6, 128, 128), jnp.bfloat16),
            pltpu.VMEM((384, 1152), jnp.bfloat16),
        ],
        flops=3_000_000_000,
        moved=4_000_000,
        in_specs=[SMEM] + [VMEM] * 7,
    )(info, *act_near, *middle_parts)

    stay, leave = call(
        "result",
        result_body,
        [shape((2, 2, 2, 32, 128))] * 2,
        [pltpu.VMEM((384, 1152), jnp.bfloat16), pltpu.VMEM((128, 128), jnp.bfloat16)],
        flops=500_000_000,
        moved=2_000_000,
        in_specs=[SMEM] + [VMEM] * 5,
    )(info, mid_act, *last_parts)
    result_near = swap_core(leave)
    result_far = swap_chip(jnp.stack([stay[1], result_near[1]]))

    keep, send = call(
        "back",
        back_body,
        [shape((2, 64, 32, 128)), shape((2, 64, 32, 128))],
        [
            pltpu.VMEM((6, 6, 128, 128), jnp.bfloat16),
            pltpu.VMEM((1152, 384), jnp.bfloat16),
            pltpu.VMEM((1152, 384), jnp.bfloat16),
            pltpu.VMEM((4, 4, 128, 128), jnp.bfloat16),
            pltpu.VMEM((128, 512), jnp.float32),
        ],
        flops=4_000_000_000,
        moved=8_000_000,
        in_specs=[SMEM] + [VMEM] * 17,
    )(
        info, *act_near, cot_cells, *middle_parts, *last_parts,
        mid_act, mid_pre, level_pre, columns, cot_own,
    )

    result = call(
        "rows", rows_body, shape((4, 2, 2, 32, 128)), in_specs=[SMEM] + [VMEM] * 3
    )(info, stay, result_near, result_far)
    result = result.transpose(3, 1, 0, 2, 4).reshape(32, 2, 8, 128)

    other = swap_core(send)
    terms = (keep.astype(jnp.float32) + other.astype(jnp.float32)).astype(jnp.bfloat16)
    terms = lax.all_to_all(terms.reshape(2 * depth, 64, 128), ("chip", "depth"), 0, 0, tiled=True)
    mine = jnp.sum(terms.astype(jnp.float32), axis=0).astype(jnp.bfloat16)
    spread = jnp.broadcast_to(mine[None], (depth, 64, 128))
    full = lax.all_to_all(spread, "depth", 0, 0, tiled=True)
    full = full.reshape(64, 32, 128).astype(jnp.float32)
    grad_stride = full[54:58].reshape(4, 32, 2, 64).transpose(0, 2, 1, 3).reshape(8, 32, 64)
    return (result, grad_stride, full[27:54], full[:27])


def solution(mesh):
    placed = (
        P(None, "depth", FILT, None),
        P(None, FILT, None),
        P(None, FILT, None),
        P(None, FILT, None),
        P(FILT, "depth", None, None),
    )
    fine = Mesh(mesh.devices.reshape(-1, 2, 2), AXES)
    return jax.shard_map(
        whole,
        mesh=fine,
        in_specs=placed,
        out_specs=(
            P(FILT, "depth", None, None),
            P(None, FILT, None),
            P(None, FILT, None),
            P(None, FILT, None),
        ),
        check_vma=False,
    )
```

```python
import jax
import jax.numpy as jnp
from jax import lax
from jax.experimental import pallas as pl
from jax.experimental.pallas import tpu as pltpu
from jax.sharding import Mesh
from jax.sharding import PartitionSpec as P


AXES = ("depth", "chip", "core")
FILT = ("chip", "core")
CELLS = 128
LIMITS = {
    "stride": 8, "turn": 8, "weights": 10, "middle": 14, "result": 8, "back": 20, "rows": 2, "sum": 6
}
VMEM = pl.BlockSpec(memory_space=pltpu.VMEM)
SMEM = pl.BlockSpec(memory_space=pltpu.SMEM)
TAPS = [(a, b) for a in range(3) for b in range(3)]


def silu_slope(value):
    sigma = jax.nn.sigmoid(value)
    return sigma * (1.0 + value * (1.0 - sigma))


def pairs_of(move):
    depth, filt = lax.axis_size("depth"), lax.axis_size(FILT)
    found = []
    for d in range(depth):
        for f in range(filt):
            e, g = move(d, f)
            if 0 <= e < depth and 0 <= g < filt:
                found.append((d * filt + f, e * filt + g))
    return found


def shifted(value, move):
    return lax.ppermute(value, AXES, pairs_of(move))


def swap_core(value):
    return shifted(value, lambda d, f: (d, f ^ 1))


def swap_chip(value):
    return shifted(value, lambda d, f: (d, f ^ 2))


def four_parts(value, turn):
    far = shifted(value, lambda d, f: (d ^ turn, f ^ 2))
    return [value, swap_core(value), far, swap_core(far)]


def four_parts_direct(value):
    return [value] + [shifted(value, lambda d, f, step=step: (d, f ^ step)) for step in (1, 2, 3)]


def call(name, body, out_shape, scratch=(), flops=0, moved=0, in_specs=None):
    many = isinstance(out_shape, (list, tuple))
    return pl.pallas_call(
        body,
        out_shape=out_shape,
        in_specs=in_specs,
        out_specs=[VMEM] * len(out_shape) if many else VMEM,
        scratch_shapes=list(scratch),
        compiler_params=pltpu.CompilerParams(vmem_limit_bytes=LIMITS[name] << 20),
        cost_estimate=pl.CostEstimate(flops=flops, bytes_accessed=moved, transcendentals=0),
    )


def shape(dims, dtype=jnp.bfloat16):
    return jax.ShapeDtypeStruct(dims, dtype)


def dot(left, right):
    return jnp.dot(left, right, preferred_element_type=jnp.float32)


def dot_rows(left, right):
    return lax.dot_general(
        left, right, (((1,), (1,)), ((), ())), preferred_element_type=jnp.float32
    )


def stride_body(info, u_ref, s0, s1, s2, s3, cot_ref, pack_ref, pre_ref, columns_ref, weights):
    filt = info[1]
    for j, part in enumerate((s0, s1, s2, s3)):
        start = pl.multiple_of((filt ^ j) * 32, 32)
        for tap in range(0, 8, 2):
            pair = jnp.concatenate([part[tap], part[tap + 1]], axis=1)
            weights[pl.ds(start, 32), tap * 64 : tap * 64 + 128] = pair
    source = lax.broadcasted_iota(jnp.int32, (256, 256), 0)
    target = lax.broadcasted_iota(jnp.int32, (256, 256), 1)
    pick = source == 2 * (target % 128) + target // 128
    pick = jnp.where(pick, 1.0, 0.0).astype(jnp.bfloat16)
    for p in range(2):
        for r in range(2):
            cell = 2 * p + r
            rows = []
            for a in range(2):
                for b in range(2):
                    split = dot(u_ref[2 * p + a, 2 * r + b], pick).astype(jnp.bfloat16)
                    rows += [split[:, :128], split[:, 128:]]
            block = jnp.concatenate(rows, axis=0)
            columns_ref[:, cell * 128 : cell * 128 + 128] = block
            pre = dot(weights[...], block).T
            pre_ref[p, r] = pre
            pack_ref[p, r] = (pre * jax.nn.sigmoid(pre)).astype(jnp.bfloat16)
    pack_ref[:, 2:4] = cot_ref[...]


def turn_body(info, own, near, far, both, cells_ref, own_ref, tiles):
    filt, chip = info[1], info[3]
    for p in range(6):
        for r in range(6):
            row = 2 * filt - 2 + r
            valid = jnp.where((row >= 0) & (row <= 7), 1.0, 0.0)
            wide = jnp.clip(row, 0, 7)
            cut = jnp.clip(row - 2 * chip, 0, 5)
            for j, (part, at) in enumerate(((own, wide), (near, wide), (far, cut), (both, cut))):
                start = pl.multiple_of((filt ^ j) * 32, 32)
                tiles[p * 6 + r, pl.ds(start, 32), :] = part[p, at]
            tile = tiles[p * 6 + r]
            cells_ref[p, r] = (tile.astype(jnp.float32).T * valid).astype(jnp.bfloat16)
            if 2 <= p < 4 and 2 <= r < 4:
                own_ref[p - 2, r - 2] = tile


def fill_window(window, middle, near, cross, core):
    window[:, 2:4] = middle[...]
    window[:, pl.ds(4 - 4 * core, 2)] = near[...]
    window[:, pl.ds(4 * core, 2)] = cross[...]


def fill_forward(weights, parts, filt):
    for j, part in enumerate(parts):
        start = (filt ^ j) * 32
        for n, (a, b) in enumerate(TAPS):
            for c in range(3):
                at = pl.multiple_of(start + c * 128, 32)
                weights[pl.ds(at, 32), n * 128 : n * 128 + 128] = part[9 * a + 3 * b + c]


def fill_backward(weights, parts, filt):
    for j, part in enumerate(parts):
        start = (filt ^ j) * 32
        for n, (a, b) in enumerate(TAPS):
            at = pl.multiple_of(start + n * 128, 32)
            for c in range(3):
                weights[pl.ds(at, 32), c * 128 : c * 128 + 128] = part[9 * a + 3 * b + c]


def weights_body(info, m0, m1, m2, m3, l0, l1, l2, l3, fm_ref, fl_ref, bl_ref, bm_ref):
    filt = info[1]
    fill_forward(fm_ref, (m0, m1, m2, m3), filt)
    fill_forward(fl_ref, (l0, l1, l2, l3), filt)
    fill_backward(bl_ref, (l0, l1, l2, l3), filt)
    fill_backward(bm_ref, (m0, m1, m2, m3), filt)


def column_of(size):
    return lax.broadcasted_iota(jnp.int32, (size, 1), 0) % CELLS


def from_before(value):
    size = value.shape[0]
    return jnp.where(column_of(size) == 0, 0.0, pltpu.roll(value, 1, 0))


def from_after(value):
    size = value.shape[0]
    return jnp.where(column_of(size) == CELLS - 1, 0.0, pltpu.roll(value, size - 1, 0))


def block_of(ref, p, planes, r, rows):
    return ref[pl.ds(p, planes), r : r + rows].reshape(planes * rows * CELLS, 128)


def conv_forward(ref, p, planes, r, rows, weights):
    wide = jnp.concatenate([block_of(ref, p + a, planes, r + b, rows) for a, b in TAPS], axis=1)
    out = dot_rows(wide, weights[...])
    return from_before(out[:, :128]) + out[:, 128:256] + from_after(out[:, 256:])


def conv_backward(ref, p, planes, r, rows, weights):
    wide = jnp.concatenate(
        [block_of(ref, p + 2 - a, planes, r + 2 - b, rows) for a, b in TAPS], axis=1
    )
    out = dot(wide, weights[...])
    return from_after(out[:, :128]) + out[:, 128:256] + from_before(out[:, 256:])


def inside(info, p):
    depth, filt = info[0], info[1]
    row = lax.broadcasted_iota(jnp.int32, (4 * CELLS, 1), 0) // CELLS
    bad = ((depth == 0) & (p == 0)) | ((depth == lax.axis_size("depth") - 1) & (p == 3))
    low = jnp.where(filt == 0, 1, 0)
    high = jnp.where(filt == 3, 2, 3)
    low = jnp.where(bad, 4, low)
    return (row >= low) & (row <= high)


def middle_body(info, mid, near, cross, weights, act_ref, pre_ref, window):
    fill_window(window, mid, near, cross, info[4])

    def plane(p, carry):
        pre = conv_forward(window, p, 1, 0, 4, weights)
        act = jnp.where(inside(info, p), pre * jax.nn.sigmoid(pre), 0.0)
        pre_ref[pl.ds(p, 1)] = pre.reshape(1, 4, CELLS, 128)
        act_ref[pl.ds(p, 1)] = act.astype(jnp.bfloat16).reshape(1, 4, CELLS, 128)
        return carry

    lax.fori_loop(0, 4, plane, 0)


def result_body(info, act_ref, weights, near_ref, far_ref, turned):
    filt = info[1]
    out = conv_forward(act_ref, 0, 2, 0, 2, weights)
    for p in range(2):
        for r in range(2):
            at = (2 * p + r) * CELLS
            turned[...] = out[at : at + CELLS].T.astype(jnp.bfloat16)
            for j, ref in enumerate((near_ref, far_ref, near_ref, far_ref)):
                start = pl.multiple_of((filt ^ j) * 32, 32)
                ref[j // 2, p, r] = turned[pl.ds(start, 32), :]


def rows_body(info, own, near, far, out_ref):
    filt = info[1]
    for j, part in enumerate((own.at[0], near.at[0], far.at[0], far.at[1])):
        out_ref[filt ^ j] = part[...]


def shifts_of(value):
    lane = lax.broadcasted_iota(jnp.int32, value.shape, 1) % CELLS
    size = value.shape[1]
    after = jnp.where(lane == CELLS - 1, 0.0, pltpu.roll(value, size - 1, 1))
    before = jnp.where(lane == 0, 0.0, pltpu.roll(value, 1, 1))
    return jnp.concatenate([after, value, before], axis=0).astype(jnp.bfloat16)


def in_order(ref, at, core):
    rows = [ref[at + (pl.ds(pl.multiple_of((k ^ core) * 32, 32), 32),)] for k in range(4)]
    return jnp.concatenate(rows, axis=0)


def put_grad(refs, slot, block):
    for k in range(4):
        refs[k % 2][k // 2, slot] = block[k * 32 : k * 32 + 32].astype(jnp.bfloat16)


def put_kernel_grad(refs, first, grad):
    for n, (a, b) in enumerate(TAPS):
        for c in range(3):
            block = grad[c * 128 : c * 128 + 128, n * 128 : n * 128 + 128]
            put_grad(refs, first + 9 * a + 3 * b + c, block)


def back_body(
    info, act_window, window, weights_l, weights_m, mid_act, mid_pre, level_pre, columns, cot_own,
    keep_ref, send_ref, delta, turned,
):
    core = info[4]
    refs = (keep_ref, send_ref)

    def plane(p, carry):
        back = conv_backward(window, p, 1, 0, 4, weights_l)
        pre = mid_pre[pl.ds(p, 1)].reshape(4 * CELLS, 128)
        here = jnp.where(inside(info, p), back * silu_slope(pre), 0.0)
        delta[pl.ds(p, 1)] = here.astype(jnp.bfloat16).reshape(1, 4, CELLS, 128)
        return carry

    lax.fori_loop(0, 4, plane, 0)

    own = [in_order(cot_own, (p, r), core).astype(jnp.float32) for p in range(2) for r in range(2)]
    cot_rows = shifts_of(jnp.concatenate(own, axis=1))
    wide = jnp.concatenate([block_of(mid_act, a, 2, b, 2) for a, b in TAPS], axis=1)
    put_kernel_grad(refs, 0, dot(cot_rows, wide))

    for p in range(2):
        for r in range(2):
            at = (2 * p + r) * CELLS
            turned[:, at : at + CELLS] = delta[1 + p, 1 + r].astype(jnp.float32).T
    delta_rows = shifts_of(in_order(turned, (), core))
    wide = jnp.concatenate([block_of(act_window, 1 + a, 2, 1 + b, 2) for a, b in TAPS], axis=1)
    put_kernel_grad(refs, 27, dot(delta_rows, wide))

    back = conv_backward(delta, 0, 2, 0, 2, weights_m)
    pre = level_pre[...].reshape(4 * CELLS, 128)
    level_delta = (back * silu_slope(pre)).astype(jnp.bfloat16)
    grad = dot(columns[...], level_delta)
    for n in range(4):
        turned[:, n * 128 : n * 128 + 128] = grad[n * 128 : n * 128 + 128].T
    ordered = in_order(turned, (), core)
    for n in range(4):
        put_grad(refs, 54 + n, ordered[:, n * 128 : n * 128 + 128])
    for n in range(58, 64):
        put_grad(refs, n, jnp.zeros((128, 128), jnp.float32))


def sum_body(terms_ref, out_ref):
    total = jnp.sum(terms_ref[...].astype(jnp.float32), axis=0).astype(jnp.bfloat16)
    out_ref[...] = jnp.broadcast_to(total[None], out_ref.shape)


def cotangent_parts(column, chip):
    wanted = lax.dynamic_slice_in_dim(column, 2 * (1 - chip), 6, axis=1)
    far = swap_chip(wanted)
    return column, swap_core(column), far, swap_core(far)


def whole(upper_level, stride_weight, middle_weight, last_weight, cotangent):
    depth = lax.axis_size("depth")
    chip, core = lax.axis_index("chip"), lax.axis_index("core")
    info = jnp.stack([lax.axis_index("depth"), 2 * chip + core, jnp.int32(depth), chip, core])
    stride_parts = four_parts_direct(stride_weight)
    middle_parts = four_parts(middle_weight, 0)
    last_parts = four_parts(last_weight, 4)
    upper = upper_level.transpose(1, 2, 0, 3)
    cot_rows = cotangent.transpose(1, 2, 0, 3).reshape(2, 2, 128, 128)
    pack, level_pre, columns = call(
        "stride",
        stride_body,
        [shape((2, 4, 128, 128)), shape((2, 2, 128, 128), jnp.float32), shape((512, 512))],
        [pltpu.VMEM((128, 512), jnp.bfloat16)],
        flops=200_000_000,
        moved=1_500_000,
        in_specs=[SMEM] + [VMEM] * 6,
    )(info, upper, *stride_parts, cot_rows)
    odd = lax.axis_index("depth") % 2 == 1
    pair = shifted(pack, lambda d, f: (d ^ 1, f))
    next_pair = shifted(pack, lambda d, f: (d + 1 if d % 2 else d - 1, f))
    act_column, cot_column = [
        jnp.concatenate(
            [
                jnp.where(odd, pair[:, at], next_pair[:, at]),
                pack[:, at],
                jnp.where(odd, next_pair[:, at], pair[:, at]),
            ],
            axis=0,
        )
        for at in (slice(0, 2), slice(2, 4))
    ]
    act_near = swap_core(act_column)
    act_cross = shifted(act_column, lambda d, f: (d, 3 - f) if f in (1, 2) else (-1, f))
    cot_parts = cotangent_parts(cot_column.reshape(6, 8, 32, 128), chip)
    cot_cells, cot_own = call(
        "turn",
        turn_body,
        [shape((6, 6, 128, 128)), shape((2, 2, 128, 128))],
        [pltpu.VMEM((36, 128, 128), jnp.bfloat16)],
        flops=1_000_000,
        moved=3_000_000,
        in_specs=[SMEM] + [VMEM] * 4,
    )(info, *cot_parts)

    forward_m, forward_l, backward_l, backward_m = call(
        "weights",
        weights_body,
        [shape((384, 1152))] * 2 + [shape((1152, 384))] * 2,
        flops=1_000_000,
        moved=6_000_000,
        in_specs=[SMEM] + [VMEM] * 8,
    )(info, *middle_parts, *last_parts)

    mid_act, mid_pre, act_window = call(
        "middle",
        middle_body,
        [shape((4, 4, 128, 128)), shape((4, 4, 128, 128), jnp.float32), shape((6, 6, 128, 128))],
        flops=3_000_000_000,
        moved=4_000_000,
        in_specs=[SMEM] + [VMEM] * 4,
    )(info, act_column, act_near, act_cross, forward_m)

    stay, leave = call(
        "result",
        result_body,
        [shape((2, 2, 2, 32, 128))] * 2,
        [pltpu.VMEM((128, 128), jnp.bfloat16)],
        flops=500_000_000,
        moved=2_000_000,
        in_specs=[SMEM] + [VMEM] * 2,
    )(info, mid_act, forward_l)
    result_near = swap_core(leave)
    result_far = swap_chip(jnp.stack([stay[1], result_near[1]]))

    keep, send = call(
        "back",
        back_body,
        [shape((2, 64, 32, 128)), shape((2, 64, 32, 128))],
        [pltpu.VMEM((4, 4, 128, 128), jnp.bfloat16), pltpu.VMEM((128, 512), jnp.float32)],
        flops=4_000_000_000,
        moved=8_000_000,
        in_specs=[SMEM] + [VMEM] * 9,
    )(
        info, act_window, cot_cells, backward_l, backward_m,
        mid_act, mid_pre, level_pre, columns, cot_own,
    )

    result = call(
        "rows", rows_body, shape((4, 2, 2, 32, 128)), in_specs=[SMEM] + [VMEM] * 3
    )(info, stay, result_near, result_far)
    result = result.transpose(3, 1, 0, 2, 4).reshape(32, 2, 8, 128)

    other = swap_core(send)
    terms = (keep.astype(jnp.float32) + other.astype(jnp.float32)).astype(jnp.bfloat16)
    terms = lax.all_to_all(terms.reshape(2 * depth, 64, 128), ("chip", "depth"), 0, 0, tiled=True)
    spread = call("sum", sum_body, shape((depth, 64, 128)), in_specs=[VMEM])(terms)
    full = lax.all_to_all(spread, "depth", 0, 0, tiled=True)
    full = full.reshape(64, 32, 128).astype(jnp.float32)
    grad_stride = full[54:58].reshape(4, 32, 2, 64).transpose(0, 2, 1, 3).reshape(8, 32, 64)
    return (result, grad_stride, full[27:54], full[:27])


def solution(mesh):
    placed = (
        P(None, "depth", FILT, None),
        P(None, FILT, None),
        P(None, FILT, None),
        P(None, FILT, None),
        P(FILT, "depth", None, None),
    )
    fine = Mesh(mesh.devices.reshape(-1, 2, 2), AXES)
    return jax.shard_map(
        whole,
        mesh=fine,
        in_specs=placed,
        out_specs=(
            P(FILT, "depth", None, None),
            P(None, FILT, None),
            P(None, FILT, None),
            P(None, FILT, None),
        ),
        check_vma=False,
    )
```

```python
import jax
import jax.numpy as jnp
from jax import lax
from jax.experimental import pallas as pl
from jax.experimental.pallas import tpu as pltpu
from jax.sharding import Mesh
from jax.sharding import PartitionSpec as P


AXES = ("depth", "chip", "core")
FILT = ("chip", "core")
CELLS = 128
LIMITS = {
    "stride": 8, "act_join": 4, "cot_join": 4, "turn": 8, "weights": 10, "middle": 20, "result": 8,
    "back": 28, "rows": 2, "sum": 6, "finish": 4,
}
VMEM = pl.BlockSpec(memory_space=pltpu.VMEM)
SMEM = pl.BlockSpec(memory_space=pltpu.SMEM)
TAPS = [(a, b) for a in range(3) for b in range(3)]


def silu_slope(value):
    sigma = jax.nn.sigmoid(value)
    return sigma * (1.0 + value * (1.0 - sigma))


def pairs_of(move):
    depth, filt = lax.axis_size("depth"), lax.axis_size(FILT)
    found = []
    for d in range(depth):
        for f in range(filt):
            e, g = move(d, f)
            if 0 <= e < depth and 0 <= g < filt:
                found.append((d * filt + f, e * filt + g))
    return found


def shifted(value, move):
    return lax.ppermute(value, AXES, pairs_of(move))


def swap_core(value):
    return shifted(value, lambda d, f: (d, f ^ 1))


def swap_chip(value):
    return shifted(value, lambda d, f: (d, f ^ 2))


def four_parts(value, turn):
    far = shifted(value, lambda d, f: (d ^ turn, f ^ 2))
    return [value, swap_core(value), far, swap_core(far)]


def call(name, body, out_shape, scratch=(), flops=0, moved=0, in_specs=None):
    many = isinstance(out_shape, (list, tuple))
    return pl.pallas_call(
        body,
        out_shape=out_shape,
        in_specs=in_specs,
        out_specs=[VMEM] * len(out_shape) if many else VMEM,
        scratch_shapes=list(scratch),
        compiler_params=pltpu.CompilerParams(vmem_limit_bytes=LIMITS[name] << 20),
        cost_estimate=pl.CostEstimate(flops=flops, bytes_accessed=moved, transcendentals=0),
    )


def shape(dims, dtype=jnp.bfloat16):
    return jax.ShapeDtypeStruct(dims, dtype)


def dot(left, right):
    return jnp.dot(left, right, preferred_element_type=jnp.float32)


def dot_rows(left, right):
    return lax.dot_general(
        left, right, (((1,), (1,)), ((), ())), preferred_element_type=jnp.float32
    )


def stride_body(info, u_ref, s0, s1, s2, s3, cot_ref, pack_ref, pre_ref, columns_ref, weights):
    filt = info[1]
    for j, part in enumerate((s0, s1, s2, s3)):
        start = pl.multiple_of((filt ^ j) * 32, 32)
        for tap in range(0, 8, 2):
            pair = jnp.concatenate([part[tap], part[tap + 1]], axis=1)
            weights[pl.ds(start, 32), tap * 64 : tap * 64 + 128] = pair
    source = lax.broadcasted_iota(jnp.int32, (256, 256), 0)
    target = lax.broadcasted_iota(jnp.int32, (256, 256), 1)
    pick = source == 2 * (target % 128) + target // 128
    pick = jnp.where(pick, 1.0, 0.0).astype(jnp.bfloat16)
    for p in range(2):
        for r in range(2):
            cell = 2 * p + r
            rows = []
            for a in range(2):
                for b in range(2):
                    split = dot(u_ref[2 * p + a, 2 * r + b], pick).astype(jnp.bfloat16)
                    rows += [split[:, :128], split[:, 128:]]
            block = jnp.concatenate(rows, axis=0)
            columns_ref[:, cell * 128 : cell * 128 + 128] = block
            pre = dot(weights[...], block).T
            pre_ref[p, r] = pre
            act = (pre * jax.nn.sigmoid(pre)).astype(jnp.bfloat16)
            pack_ref[p, r * 128 : r * 128 + 128] = act
    pack_ref[:, 256:512] = cot_ref[...]


def act_body(info, pack, pair, beyond, column_ref):
    odd = info[0] & 1
    column_ref[2:4] = pack[:, :256]
    column_ref[pl.ds(4 - 4 * odd, 2)] = pair[:, :256]
    column_ref[pl.ds(4 * odd, 2)] = beyond[:, :256]


def cot_body(info, pack, pair, beyond, column_ref, wanted_ref):
    odd, chip = info[0] & 1, info[3]
    start = pl.multiple_of(256 + 64 * (1 - chip), 64)
    for at, part in ((2, pack), (4 - 4 * odd, pair), (4 * odd, beyond)):
        column_ref[pl.ds(at, 2)] = part[:, 256:512]
        wanted_ref[pl.ds(at, 2)] = part[:, pl.ds(start, 192)]


def turn_body(info, own, near, far, both, cells_ref, own_ref, tiles):
    filt, chip = info[1], info[3]
    for p in range(6):
        for r in range(6):
            row = 2 * filt - 2 + r
            valid = jnp.where((row >= 0) & (row <= 7), 1.0, 0.0)
            wide = jnp.clip(row, 0, 7)
            cut = jnp.clip(row - 2 * chip, 0, 5)
            for j, (part, at) in enumerate(((own, wide), (near, wide), (far, cut), (both, cut))):
                start = pl.multiple_of((filt ^ j) * 32, 32)
                tiles[p * 6 + r, pl.ds(start, 32), :] = part[p, at]
            tile = tiles[p * 6 + r]
            cells_ref[p, r] = (tile.astype(jnp.float32).T * valid).astype(jnp.bfloat16)
            if 2 <= p < 4 and 2 <= r < 4:
                own_ref[p - 2, r - 2] = tile


def fill_window(window, middle, near, cross, core):
    window[:, 2:4] = middle[...]
    window[:, pl.ds(4 - 4 * core, 2)] = near[...]
    window[:, pl.ds(4 * core, 2)] = cross[...]


def fill_forward(weights, parts, filt):
    for j, part in enumerate(parts):
        start = (filt ^ j) * 32
        for n, (a, b) in enumerate(TAPS):
            for c in range(3):
                at = pl.multiple_of(start + c * 128, 32)
                weights[pl.ds(at, 32), n * 128 : n * 128 + 128] = part[9 * a + 3 * b + c]


def fill_backward(weights, parts, filt):
    for j, part in enumerate(parts):
        start = (filt ^ j) * 32
        for n, (a, b) in enumerate(TAPS):
            at = pl.multiple_of(start + n * 128, 32)
            for c in range(3):
                weights[pl.ds(at, 32), c * 128 : c * 128 + 128] = part[9 * a + 3 * b + c]


def weights_body(info, m0, m1, m2, m3, l0, l1, l2, l3, fm_ref, fl_ref, bl_ref, bm_ref):
    filt = info[1]
    fill_forward(fm_ref, (m0, m1, m2, m3), filt)
    fill_forward(fl_ref, (l0, l1, l2, l3), filt)
    fill_backward(bl_ref, (l0, l1, l2, l3), filt)
    fill_backward(bm_ref, (m0, m1, m2, m3), filt)


def column_of(size):
    return lax.broadcasted_iota(jnp.int32, (size, 1), 0) % CELLS


def from_before(value):
    size = value.shape[0]
    return jnp.where(column_of(size) == 0, 0.0, pltpu.roll(value, 1, 0))


def from_after(value):
    size = value.shape[0]
    return jnp.where(column_of(size) == CELLS - 1, 0.0, pltpu.roll(value, size - 1, 0))


def block_of(ref, p, planes, r, rows):
    return ref[pl.ds(p, planes), r : r + rows].reshape(planes * rows * CELLS, 128)


def conv_forward(ref, p, planes, r, rows, weights):
    wide = jnp.concatenate([block_of(ref, p + a, planes, r + b, rows) for a, b in TAPS], axis=1)
    out = dot_rows(wide, weights[...])
    return from_before(out[:, :128]) + out[:, 128:256] + from_after(out[:, 256:])


def conv_backward(ref, p, planes, r, rows, weights):
    wide = jnp.concatenate(
        [block_of(ref, p + 2 - a, planes, r + 2 - b, rows) for a, b in TAPS], axis=1
    )
    out = dot(wide, weights[...])
    return from_after(out[:, :128]) + out[:, 128:256] + from_before(out[:, 256:])


def inside(info):
    depth, filt = info[0], info[1]
    cell = lax.broadcasted_iota(jnp.int32, (16 * CELLS, 1), 0) // CELLS
    plane, row = cell // 4, cell % 4
    valid = (plane >= jnp.where(depth == 0, 1, 0)) & (row >= jnp.where(filt == 0, 1, 0))
    last = jnp.where(depth == lax.axis_size("depth") - 1, 2, 3)
    return valid & (plane <= last) & (row <= jnp.where(filt == 3, 2, 3))


def middle_body(info, mid, near, cross, weights, act_ref, pre_ref, window):
    fill_window(window, mid, near, cross, info[4])

    pre = conv_forward(window, 0, 4, 0, 4, weights)
    act = jnp.where(inside(info), pre * jax.nn.sigmoid(pre), 0.0)
    pre_ref[...] = pre.reshape(4, 4, CELLS, 128)
    act_ref[...] = act.astype(jnp.bfloat16).reshape(4, 4, CELLS, 128)


def result_body(info, act_ref, weights, near_ref, far_ref, turned):
    filt = info[1]
    out = conv_forward(act_ref, 0, 2, 0, 2, weights)
    for p in range(2):
        for r in range(2):
            at = (2 * p + r) * CELLS
            turned[...] = out[at : at + CELLS].T.astype(jnp.bfloat16)
            for j, ref in enumerate((near_ref, far_ref, near_ref, far_ref)):
                start = pl.multiple_of((filt ^ j) * 32, 32)
                ref[j // 2, p, r] = turned[pl.ds(start, 32), :]


def rows_body(info, own, near, far, out_ref):
    filt = info[1]
    for j, part in enumerate((own.at[0], near.at[0], far.at[0], far.at[1])):
        out_ref[filt ^ j] = part[...]


def shifts_of(value):
    lane = lax.broadcasted_iota(jnp.int32, value.shape, 1) % CELLS
    size = value.shape[1]
    after = jnp.where(lane == CELLS - 1, 0.0, pltpu.roll(value, size - 1, 1))
    before = jnp.where(lane == 0, 0.0, pltpu.roll(value, 1, 1))
    return jnp.concatenate([after, value, before], axis=0).astype(jnp.bfloat16)


def in_order(ref, at, core):
    rows = [ref[at + (pl.ds(pl.multiple_of((k ^ core) * 32, 32), 32),)] for k in range(4)]
    return jnp.concatenate(rows, axis=0)


def put_grad(refs, slot, block):
    for k in range(4):
        refs[k % 2][k // 2, slot] = block[k * 32 : k * 32 + 32].astype(jnp.bfloat16)


def put_kernel_grad(refs, first, grad):
    for n, (a, b) in enumerate(TAPS):
        for c in range(3):
            block = grad[c * 128 : c * 128 + 128, n * 128 : n * 128 + 128]
            put_grad(refs, first + 9 * a + 3 * b + c, block)


def back_body(
    info, act_window, window, weights_l, weights_m, mid_act, mid_pre, level_pre, columns, cot_own,
    keep_ref, send_ref, delta, turned,
):
    core = info[4]
    refs = (keep_ref, send_ref)

    back = conv_backward(window, 0, 4, 0, 4, weights_l)
    here = jnp.where(inside(info), back * silu_slope(mid_pre[...].reshape(16 * CELLS, 128)), 0.0)
    delta[...] = here.astype(jnp.bfloat16).reshape(4, 4, CELLS, 128)

    own = [in_order(cot_own, (p, r), core).astype(jnp.float32) for p in range(2) for r in range(2)]
    cot_rows = shifts_of(jnp.concatenate(own, axis=1))
    wide = jnp.concatenate([block_of(mid_act, a, 2, b, 2) for a, b in TAPS], axis=1)
    put_kernel_grad(refs, 0, dot(cot_rows, wide))

    for p in range(2):
        for r in range(2):
            at = (2 * p + r) * CELLS
            turned[:, at : at + CELLS] = delta[1 + p, 1 + r].astype(jnp.float32).T
    delta_rows = shifts_of(in_order(turned, (), core))
    wide = jnp.concatenate([block_of(act_window, 1 + a, 2, 1 + b, 2) for a, b in TAPS], axis=1)
    put_kernel_grad(refs, 27, dot(delta_rows, wide))

    back = conv_backward(delta, 0, 2, 0, 2, weights_m)
    pre = level_pre[...].reshape(4 * CELLS, 128)
    level_delta = (back * silu_slope(pre)).astype(jnp.bfloat16)
    grad = dot(columns[...], level_delta)
    for n in range(4):
        turned[:, n * 128 : n * 128 + 128] = grad[n * 128 : n * 128 + 128].T
    ordered = in_order(turned, (), core)
    for n in range(4):
        put_grad(refs, 54 + n, ordered[:, n * 128 : n * 128 + 128])
    for n in range(58, 64):
        put_grad(refs, n, jnp.zeros((128, 128), jnp.float32))


def finish_body(full_ref, stride_ref, middle_ref, last_ref):
    last_ref[...] = full_ref[0:27].astype(jnp.float32)
    middle_ref[...] = full_ref[27:54].astype(jnp.float32)
    for n in range(4):
        block = full_ref[54 + n].astype(jnp.float32)
        stride_ref[2 * n] = block[:, :64]
        stride_ref[2 * n + 1] = block[:, 64:]


def sum_body(terms_ref, out_ref):
    total = jnp.sum(terms_ref[...].astype(jnp.float32), axis=0).astype(jnp.bfloat16)
    out_ref[...] = jnp.broadcast_to(total[None], out_ref.shape)


def whole(upper_level, stride_weight, middle_weight, last_weight, cotangent):
    depth = lax.axis_size("depth")
    chip, core = lax.axis_index("chip"), lax.axis_index("core")
    info = jnp.stack([lax.axis_index("depth"), 2 * chip + core, jnp.int32(depth), chip, core])
    stride_parts = four_parts(stride_weight, 0)
    middle_parts = four_parts(middle_weight, 0)
    last_parts = four_parts(last_weight, 4)
    upper = upper_level.transpose(1, 2, 0, 3)
    cot_rows = cotangent.transpose(1, 2, 0, 3).reshape(2, 256, 128)
    pack, level_pre, columns = call(
        "stride",
        stride_body,
        [shape((2, 512, 128)), shape((2, 2, 128, 128), jnp.float32), shape((512, 512))],
        [pltpu.VMEM((128, 512), jnp.bfloat16)],
        flops=200_000_000,
        moved=1_500_000,
        in_specs=[SMEM] + [VMEM] * 6,
    )(info, upper, *stride_parts, cot_rows)
    beyond = shifted(pack, lambda d, f: (d + 1 if d % 2 else d - 1, f))
    pair = shifted(pack, lambda d, f: (d ^ 1, f))
    act_column = call(
        "act_join", act_body, shape((6, 256, 128)), in_specs=[SMEM] + [VMEM] * 3
    )(info, pack, pair, beyond)
    act_cross = shifted(act_column, lambda d, f: (d, 3 - f) if f in (1, 2) else (-1, f))
    act_near = swap_core(act_column)
    act_parts = [x.reshape(6, 2, 128, 128) for x in (act_column, act_near, act_cross)]
    cot_column, cot_wanted = call(
        "cot_join",
        cot_body,
        [shape((6, 256, 128)), shape((6, 192, 128))],
        in_specs=[SMEM] + [VMEM] * 3,
    )(info, pack, pair, beyond)
    cot_near = swap_core(cot_column)
    cot_far = swap_chip(cot_wanted)
    cot_both = swap_core(cot_far)
    cot_parts = [x.reshape(6, -1, 32, 128) for x in (cot_column, cot_near, cot_far, cot_both)]
    cot_cells, cot_own = call(
        "turn",
        turn_body,
        [shape((6, 6, 128, 128)), shape((2, 2, 128, 128))],
        [pltpu.VMEM((36, 128, 128), jnp.bfloat16)],
        flops=1_000_000,
        moved=3_000_000,
        in_specs=[SMEM] + [VMEM] * 4,
    )(info, *cot_parts)

    forward_m, forward_l, backward_l, backward_m = call(
        "weights",
        weights_body,
        [shape((384, 1152))] * 2 + [shape((1152, 384))] * 2,
        flops=1_000_000,
        moved=6_000_000,
        in_specs=[SMEM] + [VMEM] * 8,
    )(info, *middle_parts, *last_parts)

    mid_act, mid_pre, act_window = call(
        "middle",
        middle_body,
        [shape((4, 4, 128, 128)), shape((4, 4, 128, 128), jnp.float32), shape((6, 6, 128, 128))],
        flops=3_000_000_000,
        moved=4_000_000,
        in_specs=[SMEM] + [VMEM] * 4,
    )(info, *act_parts, forward_m)

    stay, leave = call(
        "result",
        result_body,
        [shape((2, 2, 2, 32, 128))] * 2,
        [pltpu.VMEM((128, 128), jnp.bfloat16)],
        flops=500_000_000,
        moved=2_000_000,
        in_specs=[SMEM] + [VMEM] * 2,
    )(info, mid_act, forward_l)
    result_near = swap_core(leave)
    result_far = swap_chip(jnp.stack([stay[1], result_near[1]]))

    keep, send = call(
        "back",
        back_body,
        [shape((2, 64, 32, 128)), shape((2, 64, 32, 128))],
        [pltpu.VMEM((4, 4, 128, 128), jnp.bfloat16), pltpu.VMEM((128, 512), jnp.float32)],
        flops=4_000_000_000,
        moved=8_000_000,
        in_specs=[SMEM] + [VMEM] * 9,
    )(
        info, act_window, cot_cells, backward_l, backward_m,
        mid_act, mid_pre, level_pre, columns, cot_own,
    )

    result = call(
        "rows", rows_body, shape((4, 2, 2, 32, 128)), in_specs=[SMEM] + [VMEM] * 3
    )(info, stay, result_near, result_far)
    result = result.transpose(3, 1, 0, 2, 4).reshape(32, 2, 8, 128)

    other = swap_core(send)
    terms = (keep.astype(jnp.float32) + other.astype(jnp.float32)).astype(jnp.bfloat16)
    terms = lax.all_to_all(terms.reshape(2 * depth, 64, 128), ("chip", "depth"), 0, 0, tiled=True)
    spread = call("sum", sum_body, shape((depth, 64, 128)), in_specs=[VMEM])(terms)
    full = lax.all_to_all(spread, "depth", 0, 0, tiled=True)
    grads = call(
        "finish",
        finish_body,
        [
            shape((8, 32, 64), jnp.float32),
            shape((27, 32, 128), jnp.float32),
            shape((27, 32, 128), jnp.float32),
        ],
        in_specs=[VMEM],
    )(full.reshape(64, 32, 128))
    return (result, *grads)


def solution(mesh):
    placed = (
        P(None, "depth", FILT, None),
        P(None, FILT, None),
        P(None, FILT, None),
        P(None, FILT, None),
        P(FILT, "depth", None, None),
    )
    fine = Mesh(mesh.devices.reshape(-1, 2, 2), AXES)
    return jax.shard_map(
        whole,
        mesh=fine,
        in_specs=placed,
        out_specs=(
            P(FILT, "depth", None, None),
            P(None, FILT, None),
            P(None, FILT, None),
            P(None, FILT, None),
        ),
        check_vma=False,
    )
```

```python
import jax
import jax.numpy as jnp
from jax import lax
from jax.experimental import pallas as pl
from jax.experimental.pallas import tpu as pltpu
from jax.sharding import Mesh
from jax.sharding import PartitionSpec as P


AXES = ("depth", "chip", "core")
FILT = ("chip", "core")
CELLS = 128
LIMITS = {
    "stride": 8, "join": 6, "weights": 10, "middle": 20, "result": 8, "grad_l": 10, "back": 26,
    "rows": 2, "sum": 6, "finish": 4,
}
VMEM = pl.BlockSpec(memory_space=pltpu.VMEM)
SMEM = pl.BlockSpec(memory_space=pltpu.SMEM)
TAPS = [(a, b) for a in range(3) for b in range(3)]


def silu_slope(value):
    sigma = jax.nn.sigmoid(value)
    return sigma * (1.0 + value * (1.0 - sigma))


def pairs_of(move):
    depth, filt = lax.axis_size("depth"), lax.axis_size(FILT)
    found = []
    for d in range(depth):
        for f in range(filt):
            e, g = move(d, f)
            if 0 <= e < depth and 0 <= g < filt:
                found.append((d * filt + f, e * filt + g))
    return found


def shifted(value, move):
    return lax.ppermute(value, AXES, pairs_of(move))


def swap_core(value):
    return shifted(value, lambda d, f: (d, f ^ 1))


def swap_chip(value):
    return shifted(value, lambda d, f: (d, f ^ 2))


def four_parts(value, turn):
    far = shifted(value, lambda d, f: (d ^ turn, f ^ 2))
    return [value, swap_core(value), far, swap_core(far)]


def call(name, body, out_shape, scratch=(), flops=0, moved=0, in_specs=None):
    many = isinstance(out_shape, (list, tuple))
    return pl.pallas_call(
        body,
        out_shape=out_shape,
        in_specs=in_specs,
        out_specs=[VMEM] * len(out_shape) if many else VMEM,
        scratch_shapes=list(scratch),
        compiler_params=pltpu.CompilerParams(vmem_limit_bytes=LIMITS[name] << 20),
        cost_estimate=pl.CostEstimate(flops=flops, bytes_accessed=moved, transcendentals=0),
    )


def shape(dims, dtype=jnp.bfloat16):
    return jax.ShapeDtypeStruct(dims, dtype)


def dot(left, right):
    return jnp.dot(left, right, preferred_element_type=jnp.float32)


def dot_rows(left, right):
    return lax.dot_general(
        left, right, (((1,), (1,)), ((), ())), preferred_element_type=jnp.float32
    )


def stride_body(
    info, u_ref, s0, s1, s2, s3, c0, c1, c2, c3,
    pack_ref, pre_ref, columns_ref, cot_ref, weights,
):
    filt = info[1]
    for j, part in enumerate((s0, s1, s2, s3)):
        start = pl.multiple_of((filt ^ j) * 32, 32)
        for tap in range(0, 8, 2):
            pair = jnp.concatenate([part[tap], part[tap + 1]], axis=1)
            weights[pl.ds(start, 32), tap * 64 : tap * 64 + 128] = pair
    source = lax.broadcasted_iota(jnp.int32, (256, 256), 0)
    target = lax.broadcasted_iota(jnp.int32, (256, 256), 1)
    pick = source == 2 * (target % 128) + target // 128
    pick = jnp.where(pick, 1.0, 0.0).astype(jnp.bfloat16)
    for p in range(2):
        for r in range(2):
            cell = 2 * p + r
            rows = []
            for a in range(2):
                for b in range(2):
                    split = dot(u_ref[2 * p + a, 2 * r + b], pick).astype(jnp.bfloat16)
                    rows += [split[:, :128], split[:, 128:]]
            block = jnp.concatenate(rows, axis=0)
            columns_ref[:, cell * 128 : cell * 128 + 128] = block
            pre = dot(weights[...], block).T
            pre_ref[p, r] = pre
            act = (pre * jax.nn.sigmoid(pre)).astype(jnp.bfloat16)
            pack_ref[p, r * 128 : r * 128 + 128] = act
            for j, part in enumerate((c0, c1, c2, c3)):
                start = pl.multiple_of((filt ^ j) * 32, 32)
                cot_ref[p, r, pl.ds(start, 32), :] = part[filt, r, p]
            cot = cot_ref[p, r].astype(jnp.float32).T.astype(jnp.bfloat16)
            pack_ref[p, 256 + r * 128 : 384 + r * 128] = cot


def join_body(info, pack, pair, beyond, act_ref, cot_ref):
    odd = info[0] & 1
    for at, part in ((2, pack), (4 - 4 * odd, pair), (4 * odd, beyond)):
        act_ref[pl.ds(at, 2)] = part[:, :256]
        cot_ref[pl.ds(at, 2)] = part[:, 256:]


def fill_window(window, middle, near, cross, core):
    window[:, 2:4] = middle[...]
    window[:, pl.ds(4 - 4 * core, 2)] = near[...]
    window[:, pl.ds(4 * core, 2)] = cross[...]


def fill_forward(weights, parts, filt):
    for j, part in enumerate(parts):
        start = (filt ^ j) * 32
        for n, (a, b) in enumerate(TAPS):
            for c in range(3):
                at = pl.multiple_of(start + c * 128, 32)
                weights[pl.ds(at, 32), n * 128 : n * 128 + 128] = part[9 * a + 3 * b + c]


def fill_backward(weights, parts, filt):
    for j, part in enumerate(parts):
        start = (filt ^ j) * 32
        for n, (a, b) in enumerate(TAPS):
            at = pl.multiple_of(start + n * 128, 32)
            for c in range(3):
                weights[pl.ds(at, 32), c * 128 : c * 128 + 128] = part[9 * a + 3 * b + c]


def weights_body(info, m0, m1, m2, m3, l0, l1, l2, l3, fm_ref, fl_ref, bl_ref, bm_ref):
    filt = info[1]
    fill_forward(fm_ref, (m0, m1, m2, m3), filt)
    fill_forward(fl_ref, (l0, l1, l2, l3), filt)
    fill_backward(bl_ref, (l0, l1, l2, l3), filt)
    fill_backward(bm_ref, (m0, m1, m2, m3), filt)


def column_of(size):
    return lax.broadcasted_iota(jnp.int32, (size, 1), 0) % CELLS


def from_before(value):
    size = value.shape[0]
    return jnp.where(column_of(size) == 0, 0.0, pltpu.roll(value, 1, 0))


def from_after(value):
    size = value.shape[0]
    return jnp.where(column_of(size) == CELLS - 1, 0.0, pltpu.roll(value, size - 1, 0))


def block_of(ref, p, planes, r, rows):
    return ref[pl.ds(p, planes), r : r + rows].reshape(planes * rows * CELLS, 128)


def conv_forward(ref, p, planes, r, rows, weights):
    wide = jnp.concatenate([block_of(ref, p + a, planes, r + b, rows) for a, b in TAPS], axis=1)
    out = dot_rows(wide, weights[...])
    return from_before(out[:, :128]) + out[:, 128:256] + from_after(out[:, 256:])


def conv_backward(ref, p, planes, r, rows, weights):
    wide = jnp.concatenate(
        [block_of(ref, p + 2 - a, planes, r + 2 - b, rows) for a, b in TAPS], axis=1
    )
    out = dot(wide, weights[...])
    return from_after(out[:, :128]) + out[:, 128:256] + from_before(out[:, 256:])


def inside(info):
    depth, filt = info[0], info[1]
    cell = lax.broadcasted_iota(jnp.int32, (16 * CELLS, 1), 0) // CELLS
    plane, row = cell // 4, cell % 4
    valid = (plane >= jnp.where(depth == 0, 1, 0)) & (row >= jnp.where(filt == 0, 1, 0))
    last = jnp.where(depth == lax.axis_size("depth") - 1, 2, 3)
    return valid & (plane <= last) & (row <= jnp.where(filt == 3, 2, 3))


def middle_body(info, mid, near, cross, weights, act_ref, pre_ref, window):
    fill_window(window, mid, near, cross, info[4])

    pre = conv_forward(window, 0, 4, 0, 4, weights)
    act = jnp.where(inside(info), pre * jax.nn.sigmoid(pre), 0.0)
    pre_ref[...] = pre.reshape(4, 4, CELLS, 128)
    act_ref[...] = act.astype(jnp.bfloat16).reshape(4, 4, CELLS, 128)


def result_body(info, act_ref, weights, near_ref, far_ref, turned):
    filt = info[1]
    out = conv_forward(act_ref, 0, 2, 0, 2, weights)
    for p in range(2):
        for r in range(2):
            at = (2 * p + r) * CELLS
            turned[...] = out[at : at + CELLS].T.astype(jnp.bfloat16)
            for j, ref in enumerate((near_ref, far_ref, near_ref, far_ref)):
                start = pl.multiple_of((filt ^ j) * 32, 32)
                ref[j // 2, p, r] = turned[pl.ds(start, 32), :]


def rows_body(info, own, near, far, out_ref):
    filt = info[1]
    for j, part in enumerate((own.at[0], near.at[0], far.at[0], far.at[1])):
        out_ref[filt ^ j] = part[...]


def shifts_of(value):
    lane = lax.broadcasted_iota(jnp.int32, value.shape, 1) % CELLS
    size = value.shape[1]
    after = jnp.where(lane == CELLS - 1, 0.0, pltpu.roll(value, size - 1, 1))
    before = jnp.where(lane == 0, 0.0, pltpu.roll(value, 1, 1))
    return jnp.concatenate([after, value, before], axis=0).astype(jnp.bfloat16)


def in_order(ref, at, core):
    rows = [ref[at + (pl.ds(pl.multiple_of((k ^ core) * 32, 32), 32),)] for k in range(4)]
    return jnp.concatenate(rows, axis=0)


def put_grad(refs, slot, block):
    for k in range(4):
        refs[k % 2][k // 2, slot] = block[k * 32 : k * 32 + 32].astype(jnp.bfloat16)


def put_kernel_grad(refs, first, grad):
    for n, (a, b) in enumerate(TAPS):
        for c in range(3):
            block = grad[c * 128 : c * 128 + 128, n * 128 : n * 128 + 128]
            put_grad(refs, first + 9 * a + 3 * b + c, block)


def last_body(info, mid_act, cot_own, keep_ref, send_ref):
    core = info[4]
    own = [in_order(cot_own, (p, r), core).astype(jnp.float32) for p in range(2) for r in range(2)]
    cot_rows = shifts_of(jnp.concatenate(own, axis=1))
    wide = jnp.concatenate([block_of(mid_act, a, 2, b, 2) for a, b in TAPS], axis=1)
    put_kernel_grad((keep_ref, send_ref), 0, dot(cot_rows, wide))


def back_body(
    info, act_window, mid, near, cross, weights_l, weights_m, mid_pre, level_pre, columns,
    keep_ref, send_ref, window, delta, turned,
):
    core = info[4]
    refs = (keep_ref, send_ref)
    fill_window(window, mid, near, cross, core)

    back = conv_backward(window, 0, 4, 0, 4, weights_l)
    here = jnp.where(inside(info), back * silu_slope(mid_pre[...].reshape(16 * CELLS, 128)), 0.0)
    delta[...] = here.astype(jnp.bfloat16).reshape(4, 4, CELLS, 128)

    for p in range(2):
        for r in range(2):
            at = (2 * p + r) * CELLS
            turned[:, at : at + CELLS] = delta[1 + p, 1 + r].astype(jnp.float32).T
    delta_rows = shifts_of(in_order(turned, (), core))
    wide = jnp.concatenate([block_of(act_window, 1 + a, 2, 1 + b, 2) for a, b in TAPS], axis=1)
    put_kernel_grad(refs, 0, dot(delta_rows, wide))

    back = conv_backward(delta, 0, 2, 0, 2, weights_m)
    pre = level_pre[...].reshape(4 * CELLS, 128)
    level_delta = (back * silu_slope(pre)).astype(jnp.bfloat16)
    grad = dot(columns[...], level_delta)
    for n in range(4):
        turned[:, n * 128 : n * 128 + 128] = grad[n * 128 : n * 128 + 128].T
    ordered = in_order(turned, (), core)
    for n in range(4):
        put_grad(refs, 27 + n, ordered[:, n * 128 : n * 128 + 128])
    for n in range(31, 37):
        put_grad(refs, n, jnp.zeros((128, 128), jnp.float32))


def finish_body(full_ref, stride_ref, middle_ref, last_ref):
    last_ref[...] = full_ref[0:27].astype(jnp.float32)
    middle_ref[...] = full_ref[27:54].astype(jnp.float32)
    for n in range(4):
        block = full_ref[54 + n].astype(jnp.float32)
        stride_ref[2 * n] = block[:, :64]
        stride_ref[2 * n + 1] = block[:, 64:]


def sum_body(terms_ref, out_ref):
    total = jnp.sum(terms_ref[...].astype(jnp.float32), axis=0).astype(jnp.bfloat16)
    out_ref[...] = jnp.broadcast_to(total[None], out_ref.shape)


def row_parts(column):
    def inner(d, f):
        return (d, 3 - f) if f in (1, 2) else (-1, f)

    cross = shifted(column, inner)
    return column, swap_core(column), cross


def whole(upper_level, stride_weight, middle_weight, last_weight, cotangent):
    depth = lax.axis_size("depth")
    chip, core = lax.axis_index("chip"), lax.axis_index("core")
    info = jnp.stack([lax.axis_index("depth"), 2 * chip + core, jnp.int32(depth), chip, core])
    cot_rows = cotangent.reshape(32, 2, 4, 2, 128).transpose(2, 3, 1, 0, 4)
    cot_parts = four_parts(cot_rows, 0)
    stride_parts = four_parts(stride_weight, 0)
    middle_parts = four_parts(middle_weight, 0)
    last_parts = four_parts(last_weight, 4)
    upper = upper_level.transpose(1, 2, 0, 3)

    pack, level_pre, columns, cot_own = call(
        "stride",
        stride_body,
        [
            shape((2, 512, 128)),
            shape((2, 2, 128, 128), jnp.float32),
            shape((512, 512)),
            shape((2, 2, 128, 128)),
        ],
        [pltpu.VMEM((128, 512), jnp.bfloat16)],
        flops=200_000_000,
        moved=1_500_000,
        in_specs=[SMEM] + [VMEM] * 9,
    )(info, upper, *stride_parts, *cot_parts)
    beyond = shifted(pack, lambda d, f: (d + 1 if d % 2 else d - 1, f))
    pair = shifted(pack, lambda d, f: (d ^ 1, f))
    columns_joined = call(
        "join", join_body, [shape((6, 256, 128))] * 2, in_specs=[SMEM] + [VMEM] * 3
    )(info, pack, pair, beyond)
    act_parts, back_parts = [
        [x.reshape(6, 2, 128, 128) for x in (column, near, cross)]
        for column, near, cross in (row_parts(columns_joined[0]), row_parts(columns_joined[1]))
    ]

    forward_m, forward_l, backward_l, backward_m = call(
        "weights",
        weights_body,
        [shape((384, 1152))] * 2 + [shape((1152, 384))] * 2,
        flops=1_000_000,
        moved=6_000_000,
        in_specs=[SMEM] + [VMEM] * 8,
    )(info, *middle_parts, *last_parts)

    mid_act, mid_pre, act_window = call(
        "middle",
        middle_body,
        [shape((4, 4, 128, 128)), shape((4, 4, 128, 128), jnp.float32), shape((6, 6, 128, 128))],
        flops=3_000_000_000,
        moved=4_000_000,
        in_specs=[SMEM] + [VMEM] * 4,
    )(info, *act_parts, forward_m)

    stay, leave = call(
        "result",
        result_body,
        [shape((2, 2, 2, 32, 128))] * 2,
        [pltpu.VMEM((128, 128), jnp.bfloat16)],
        flops=500_000_000,
        moved=2_000_000,
        in_specs=[SMEM] + [VMEM] * 2,
    )(info, mid_act, forward_l)
    result_near = swap_core(leave)
    result_far = swap_chip(jnp.stack([stay[1], result_near[1]]))

    keep_l, send_l = call(
        "grad_l",
        last_body,
        [shape((2, 27, 32, 128))] * 2,
        flops=500_000_000,
        moved=3_000_000,
        in_specs=[SMEM] + [VMEM] * 2,
    )(info, mid_act, cot_own)
    other_l = swap_core(send_l)

    keep, send = call(
        "back",
        back_body,
        [shape((2, 37, 32, 128))] * 2,
        [
            pltpu.VMEM((6, 6, 128, 128), jnp.bfloat16),
            pltpu.VMEM((4, 4, 128, 128), jnp.bfloat16),
            pltpu.VMEM((128, 512), jnp.float32),
        ],
        flops=4_000_000_000,
        moved=8_000_000,
        in_specs=[SMEM] + [VMEM] * 9,
    )(
        info, act_window, *back_parts, backward_l, backward_m, mid_pre, level_pre, columns
    )

    result = call(
        "rows", rows_body, shape((4, 2, 2, 32, 128)), in_specs=[SMEM] + [VMEM] * 3
    )(info, stay, result_near, result_far)
    result = result.transpose(3, 1, 0, 2, 4).reshape(32, 2, 8, 128)

    other = swap_core(send)
    terms = jnp.concatenate(
        [
            (x.astype(jnp.float32) + y.astype(jnp.float32)).astype(jnp.bfloat16)
            for x, y in ((keep_l, other_l), (keep, other))
        ],
        axis=1,
    )
    terms = lax.all_to_all(terms.reshape(2 * depth, 64, 128), ("chip", "depth"), 0, 0, tiled=True)
    spread = call("sum", sum_body, shape((depth, 64, 128)), in_specs=[VMEM])(terms)
    full = lax.all_to_all(spread, "depth", 0, 0, tiled=True)
    grads = call(
        "finish",
        finish_body,
        [
            shape((8, 32, 64), jnp.float32),
            shape((27, 32, 128), jnp.float32),
            shape((27, 32, 128), jnp.float32),
        ],
        in_specs=[VMEM],
    )(full.reshape(64, 32, 128))
    return (result, *grads)


def solution(mesh):
    placed = (
        P(None, "depth", FILT, None),
        P(None, FILT, None),
        P(None, FILT, None),
        P(None, FILT, None),
        P(FILT, "depth", None, None),
    )
    fine = Mesh(mesh.devices.reshape(-1, 2, 2), AXES)
    return jax.shard_map(
        whole,
        mesh=fine,
        in_specs=placed,
        out_specs=(
            P(FILT, "depth", None, None),
            P(None, FILT, None),
            P(None, FILT, None),
            P(None, FILT, None),
        ),
        check_vma=False,
    )
```

```python
import jax
import jax.numpy as jnp
from jax import lax
from jax.experimental import pallas as pl
from jax.experimental.pallas import tpu as pltpu
from jax.sharding import Mesh
from jax.sharding import PartitionSpec as P


AXES = ("depth", "chip", "core")
FILT = ("chip", "core")
CELLS = 128
LIMITS = {
    "stride": 8, "cells": 4, "join": 6, "weights": 10, "middle": 20, "result": 8, "grad_l": 10, "back": 26,
    "rows": 2, "sum": 6, "finish": 4,
}
VMEM = pl.BlockSpec(memory_space=pltpu.VMEM)
SMEM = pl.BlockSpec(memory_space=pltpu.SMEM)
TAPS = [(a, b) for a in range(3) for b in range(3)]


def silu_slope(value):
    sigma = jax.nn.sigmoid(value)
    return sigma * (1.0 + value * (1.0 - sigma))


def pairs_of(move):
    depth, filt = lax.axis_size("depth"), lax.axis_size(FILT)
    found = []
    for d in range(depth):
        for f in range(filt):
            e, g = move(d, f)
            if 0 <= e < depth and 0 <= g < filt:
                found.append((d * filt + f, e * filt + g))
    return found


def shifted(value, move):
    return lax.ppermute(value, AXES, pairs_of(move))


def swap_core(value):
    return shifted(value, lambda d, f: (d, f ^ 1))


def swap_chip(value):
    return shifted(value, lambda d, f: (d, f ^ 2))


def four_parts(value, turn):
    far = shifted(value, lambda d, f: (d ^ turn, f ^ 2))
    return [value, swap_core(value), far, swap_core(far)]


def call(name, body, out_shape, scratch=(), flops=0, moved=0, in_specs=None):
    many = isinstance(out_shape, (list, tuple))
    return pl.pallas_call(
        body,
        out_shape=out_shape,
        in_specs=in_specs,
        out_specs=[VMEM] * len(out_shape) if many else VMEM,
        scratch_shapes=list(scratch),
        compiler_params=pltpu.CompilerParams(vmem_limit_bytes=LIMITS[name] << 20),
        cost_estimate=pl.CostEstimate(flops=flops, bytes_accessed=moved, transcendentals=0),
    )


def shape(dims, dtype=jnp.bfloat16):
    return jax.ShapeDtypeStruct(dims, dtype)


def dot(left, right):
    return jnp.dot(left, right, preferred_element_type=jnp.float32)


def dot_rows(left, right):
    return lax.dot_general(
        left, right, (((1,), (1,)), ((), ())), preferred_element_type=jnp.float32
    )


def stride_body(info, u_ref, s0, s1, s2, s3, act_ref, pre_ref, columns_ref, weights):
    filt = info[1]
    for j, part in enumerate((s0, s1, s2, s3)):
        start = pl.multiple_of((filt ^ j) * 32, 32)
        for tap in range(0, 8, 2):
            pair = jnp.concatenate([part[tap], part[tap + 1]], axis=1)
            weights[pl.ds(start, 32), tap * 64 : tap * 64 + 128] = pair
    source = lax.broadcasted_iota(jnp.int32, (256, 256), 0)
    target = lax.broadcasted_iota(jnp.int32, (256, 256), 1)
    pick = source == 2 * (target % 128) + target // 128
    pick = jnp.where(pick, 1.0, 0.0).astype(jnp.bfloat16)
    for p in range(2):
        for r in range(2):
            cell = 2 * p + r
            rows = []
            for a in range(2):
                for b in range(2):
                    split = dot(u_ref[2 * p + a, 2 * r + b], pick).astype(jnp.bfloat16)
                    rows += [split[:, :128], split[:, 128:]]
            block = jnp.concatenate(rows, axis=0)
            columns_ref[:, cell * 128 : cell * 128 + 128] = block
            pre = dot(weights[...], block).T
            pre_ref[p, r] = pre
            act = (pre * jax.nn.sigmoid(pre)).astype(jnp.bfloat16)
            act_ref[p, r * 128 : r * 128 + 128] = act


def cells_body(info, c0, c1, c2, c3, own_ref, cells_ref):
    filt = info[1]
    for p in range(2):
        for r in range(2):
            for j, part in enumerate((c0, c1, c2, c3)):
                start = pl.multiple_of((filt ^ j) * 32, 32)
                own_ref[p, r, pl.ds(start, 32), :] = part[filt, r, p]
            cot = own_ref[p, r].astype(jnp.float32).T.astype(jnp.bfloat16)
            cells_ref[p, r * 128 : r * 128 + 128] = cot


def join_body(info, own, pair, beyond, column_ref):
    odd = info[0] & 1
    for at, part in ((2, own), (4 - 4 * odd, pair), (4 * odd, beyond)):
        column_ref[pl.ds(at, 2)] = part[...]


def fill_window(window, middle, near, cross, core):
    window[:, 2:4] = middle[...]
    window[:, pl.ds(4 - 4 * core, 2)] = near[...]
    window[:, pl.ds(4 * core, 2)] = cross[...]


def fill_forward(weights, parts, filt):
    for j, part in enumerate(parts):
        start = (filt ^ j) * 32
        for n, (a, b) in enumerate(TAPS):
            for c in range(3):
                at = pl.multiple_of(start + c * 128, 32)
                weights[pl.ds(at, 32), n * 128 : n * 128 + 128] = part[9 * a + 3 * b + c]


def fill_backward(weights, parts, filt):
    for j, part in enumerate(parts):
        start = (filt ^ j) * 32
        for n, (a, b) in enumerate(TAPS):
            at = pl.multiple_of(start + n * 128, 32)
            for c in range(3):
                weights[pl.ds(at, 32), c * 128 : c * 128 + 128] = part[9 * a + 3 * b + c]


def weights_body(info, m0, m1, m2, m3, l0, l1, l2, l3, fm_ref, fl_ref, bl_ref, bm_ref):
    filt = info[1]
    fill_forward(fm_ref, (m0, m1, m2, m3), filt)
    fill_forward(fl_ref, (l0, l1, l2, l3), filt)
    fill_backward(bl_ref, (l0, l1, l2, l3), filt)
    fill_backward(bm_ref, (m0, m1, m2, m3), filt)


def column_of(size):
    return lax.broadcasted_iota(jnp.int32, (size, 1), 0) % CELLS


def from_before(value):
    size = value.shape[0]
    return jnp.where(column_of(size) == 0, 0.0, pltpu.roll(value, 1, 0))


def from_after(value):
    size = value.shape[0]
    return jnp.where(column_of(size) == CELLS - 1, 0.0, pltpu.roll(value, size - 1, 0))


def block_of(ref, p, planes, r, rows):
    return ref[pl.ds(p, planes), r : r + rows].reshape(planes * rows * CELLS, 128)


def conv_forward(ref, p, planes, r, rows, weights):
    wide = jnp.concatenate([block_of(ref, p + a, planes, r + b, rows) for a, b in TAPS], axis=1)
    out = dot_rows(wide, weights[...])
    return from_before(out[:, :128]) + out[:, 128:256] + from_after(out[:, 256:])


def conv_backward(ref, p, planes, r, rows, weights):
    wide = jnp.concatenate(
        [block_of(ref, p + 2 - a, planes, r + 2 - b, rows) for a, b in TAPS], axis=1
    )
    out = dot(wide, weights[...])
    return from_after(out[:, :128]) + out[:, 128:256] + from_before(out[:, 256:])


def inside(info):
    depth, filt = info[0], info[1]
    cell = lax.broadcasted_iota(jnp.int32, (16 * CELLS, 1), 0) // CELLS
    plane, row = cell // 4, cell % 4
    valid = (plane >= jnp.where(depth == 0, 1, 0)) & (row >= jnp.where(filt == 0, 1, 0))
    last = jnp.where(depth == lax.axis_size("depth") - 1, 2, 3)
    return valid & (plane <= last) & (row <= jnp.where(filt == 3, 2, 3))


def middle_body(info, mid, near, cross, weights, act_ref, pre_ref, window):
    fill_window(window, mid, near, cross, info[4])

    pre = conv_forward(window, 0, 4, 0, 4, weights)
    act = jnp.where(inside(info), pre * jax.nn.sigmoid(pre), 0.0)
    pre_ref[...] = pre.reshape(4, 4, CELLS, 128)
    act_ref[...] = act.astype(jnp.bfloat16).reshape(4, 4, CELLS, 128)


def result_body(info, act_ref, weights, near_ref, far_ref, turned):
    filt = info[1]
    out = conv_forward(act_ref, 0, 2, 0, 2, weights)
    for p in range(2):
        for r in range(2):
            at = (2 * p + r) * CELLS
            turned[...] = out[at : at + CELLS].T.astype(jnp.bfloat16)
            for j, ref in enumerate((near_ref, far_ref, near_ref, far_ref)):
                start = pl.multiple_of((filt ^ j) * 32, 32)
                ref[j // 2, p, r] = turned[pl.ds(start, 32), :]


def rows_body(info, own, near, far, out_ref):
    filt = info[1]
    for j, part in enumerate((own.at[0], near.at[0], far.at[0], far.at[1])):
        out_ref[filt ^ j] = part[...]


def shifts_of(value):
    lane = lax.broadcasted_iota(jnp.int32, value.shape, 1) % CELLS
    size = value.shape[1]
    after = jnp.where(lane == CELLS - 1, 0.0, pltpu.roll(value, size - 1, 1))
    before = jnp.where(lane == 0, 0.0, pltpu.roll(value, 1, 1))
    return jnp.concatenate([after, value, before], axis=0).astype(jnp.bfloat16)


def in_order(ref, at, core):
    rows = [ref[at + (pl.ds(pl.multiple_of((k ^ core) * 32, 32), 32),)] for k in range(4)]
    return jnp.concatenate(rows, axis=0)


def put_grad(refs, slot, block):
    for k in range(4):
        refs[k % 2][k // 2, slot] = block[k * 32 : k * 32 + 32].astype(jnp.bfloat16)


def put_kernel_grad(refs, first, grad):
    for n, (a, b) in enumerate(TAPS):
        for c in range(3):
            block = grad[c * 128 : c * 128 + 128, n * 128 : n * 128 + 128]
            put_grad(refs, first + 9 * a + 3 * b + c, block)


def last_body(info, mid_act, cot_own, keep_ref, send_ref):
    core = info[4]
    own = [in_order(cot_own, (p, r), core).astype(jnp.float32) for p in range(2) for r in range(2)]
    cot_rows = shifts_of(jnp.concatenate(own, axis=1))
    wide = jnp.concatenate([block_of(mid_act, a, 2, b, 2) for a, b in TAPS], axis=1)
    put_kernel_grad((keep_ref, send_ref), 0, dot(cot_rows, wide))


def back_body(
    info, act_window, mid, near, cross, weights_l, weights_m, mid_pre, level_pre, columns,
    keep_ref, send_ref, window, delta, turned,
):
    core = info[4]
    refs = (keep_ref, send_ref)
    fill_window(window, mid, near, cross, core)

    back = conv_backward(window, 0, 4, 0, 4, weights_l)
    here = jnp.where(inside(info), back * silu_slope(mid_pre[...].reshape(16 * CELLS, 128)), 0.0)
    delta[...] = here.astype(jnp.bfloat16).reshape(4, 4, CELLS, 128)

    for p in range(2):
        for r in range(2):
            at = (2 * p + r) * CELLS
            turned[:, at : at + CELLS] = delta[1 + p, 1 + r].astype(jnp.float32).T
    delta_rows = shifts_of(in_order(turned, (), core))
    wide = jnp.concatenate([block_of(act_window, 1 + a, 2, 1 + b, 2) for a, b in TAPS], axis=1)
    put_kernel_grad(refs, 0, dot(delta_rows, wide))

    back = conv_backward(delta, 0, 2, 0, 2, weights_m)
    pre = level_pre[...].reshape(4 * CELLS, 128)
    level_delta = (back * silu_slope(pre)).astype(jnp.bfloat16)
    grad = dot(columns[...], level_delta)
    for n in range(4):
        turned[:, n * 128 : n * 128 + 128] = grad[n * 128 : n * 128 + 128].T
    ordered = in_order(turned, (), core)
    for n in range(4):
        put_grad(refs, 27 + n, ordered[:, n * 128 : n * 128 + 128])
    for n in range(31, 37):
        put_grad(refs, n, jnp.zeros((128, 128), jnp.float32))


def finish_body(full_ref, stride_ref, middle_ref, last_ref):
    last_ref[...] = full_ref[0:27].astype(jnp.float32)
    middle_ref[...] = full_ref[27:54].astype(jnp.float32)
    for n in range(4):
        block = full_ref[54 + n].astype(jnp.float32)
        stride_ref[2 * n] = block[:, :64]
        stride_ref[2 * n + 1] = block[:, 64:]


def sum_body(terms_ref, out_ref):
    total = jnp.sum(terms_ref[...].astype(jnp.float32), axis=0).astype(jnp.bfloat16)
    out_ref[...] = jnp.broadcast_to(total[None], out_ref.shape)


def neighbourhood(info, own):
    def inner(d, f):
        return (d, 3 - f) if f in (1, 2) else (-1, f)

    beyond = shifted(own, lambda d, f: (d + 1 if d % 2 else d - 1, f))
    pair = shifted(own, lambda d, f: (d ^ 1, f))
    column = call(
        "join", join_body, shape((6, 256, 128)), in_specs=[SMEM] + [VMEM] * 3
    )(info, own, pair, beyond)
    cross = shifted(column, inner)
    near = swap_core(column)
    return [x.reshape(6, 2, 128, 128) for x in (column, near, cross)]


def whole(upper_level, stride_weight, middle_weight, last_weight, cotangent):
    depth = lax.axis_size("depth")
    chip, core = lax.axis_index("chip"), lax.axis_index("core")
    info = jnp.stack([lax.axis_index("depth"), 2 * chip + core, jnp.int32(depth), chip, core])
    cot_rows = cotangent.reshape(32, 2, 4, 2, 128).transpose(2, 3, 1, 0, 4)
    cot_parts = four_parts(cot_rows, 0)
    stride_parts = four_parts(stride_weight, 0)
    middle_parts = four_parts(middle_weight, 0)
    last_parts = four_parts(last_weight, 4)
    upper = upper_level.transpose(1, 2, 0, 3)

    level_act, level_pre, columns = call(
        "stride",
        stride_body,
        [
            shape((2, 256, 128)),
            shape((2, 2, 128, 128), jnp.float32),
            shape((512, 512)),
        ],
        [pltpu.VMEM((128, 512), jnp.bfloat16)],
        flops=200_000_000,
        moved=1_500_000,
        in_specs=[SMEM] + [VMEM] * 5,
    )(info, upper, *stride_parts)
    act_parts = neighbourhood(info, level_act)
    cot_own, cot_cells = call(
        "cells",
        cells_body,
        [shape((2, 2, 128, 128)), shape((2, 256, 128))],
        in_specs=[SMEM] + [VMEM] * 4,
    )(info, *cot_parts)
    back_parts = neighbourhood(info, cot_cells)

    forward_m, forward_l, backward_l, backward_m = call(
        "weights",
        weights_body,
        [shape((384, 1152))] * 2 + [shape((1152, 384))] * 2,
        flops=1_000_000,
        moved=6_000_000,
        in_specs=[SMEM] + [VMEM] * 8,
    )(info, *middle_parts, *last_parts)

    mid_act, mid_pre, act_window = call(
        "middle",
        middle_body,
        [shape((4, 4, 128, 128)), shape((4, 4, 128, 128), jnp.float32), shape((6, 6, 128, 128))],
        flops=3_000_000_000,
        moved=4_000_000,
        in_specs=[SMEM] + [VMEM] * 4,
    )(info, *act_parts, forward_m)

    stay, leave = call(
        "result",
        result_body,
        [shape((2, 2, 2, 32, 128))] * 2,
        [pltpu.VMEM((128, 128), jnp.bfloat16)],
        flops=500_000_000,
        moved=2_000_000,
        in_specs=[SMEM] + [VMEM] * 2,
    )(info, mid_act, forward_l)
    result_near = swap_core(leave)
    result_far = swap_chip(jnp.stack([stay[1], result_near[1]]))

    keep_l, send_l = call(
        "grad_l",
        last_body,
        [shape((2, 27, 32, 128))] * 2,
        flops=500_000_000,
        moved=3_000_000,
        in_specs=[SMEM] + [VMEM] * 2,
    )(info, mid_act, cot_own)
    other_l = swap_core(send_l)

    keep, send = call(
        "back",
        back_body,
        [shape((2, 37, 32, 128))] * 2,
        [
            pltpu.VMEM((6, 6, 128, 128), jnp.bfloat16),
            pltpu.VMEM((4, 4, 128, 128), jnp.bfloat16),
            pltpu.VMEM((128, 512), jnp.float32),
        ],
        flops=4_000_000_000,
        moved=8_000_000,
        in_specs=[SMEM] + [VMEM] * 9,
    )(
        info, act_window, *back_parts, backward_l, backward_m, mid_pre, level_pre, columns
    )

    result = call(
        "rows", rows_body, shape((4, 2, 2, 32, 128)), in_specs=[SMEM] + [VMEM] * 3
    )(info, stay, result_near, result_far)
    result = result.transpose(3, 1, 0, 2, 4).reshape(32, 2, 8, 128)

    other = swap_core(send)
    terms = jnp.concatenate(
        [
            (x.astype(jnp.float32) + y.astype(jnp.float32)).astype(jnp.bfloat16)
            for x, y in ((keep_l, other_l), (keep, other))
        ],
        axis=1,
    )
    terms = lax.all_to_all(terms.reshape(2 * depth, 64, 128), ("chip", "depth"), 0, 0, tiled=True)
    spread = call("sum", sum_body, shape((depth, 64, 128)), in_specs=[VMEM])(terms)
    full = lax.all_to_all(spread, "depth", 0, 0, tiled=True)
    grads = call(
        "finish",
        finish_body,
        [
            shape((8, 32, 64), jnp.float32),
            shape((27, 32, 128), jnp.float32),
            shape((27, 32, 128), jnp.float32),
        ],
        in_specs=[VMEM],
    )(full.reshape(64, 32, 128))
    return (result, *grads)


def solution(mesh):
    placed = (
        P(None, "depth", FILT, None),
        P(None, FILT, None),
        P(None, FILT, None),
        P(None, FILT, None),
        P(FILT, "depth", None, None),
    )
    fine = Mesh(mesh.devices.reshape(-1, 2, 2), AXES)
    return jax.shard_map(
        whole,
        mesh=fine,
        in_specs=placed,
        out_specs=(
            P(FILT, "depth", None, None),
            P(None, FILT, None),
            P(None, FILT, None),
            P(None, FILT, None),
        ),
        check_vma=False,
    )
```

```python
import jax
import jax.numpy as jnp
from jax import lax
from jax.experimental import pallas as pl
from jax.experimental.pallas import tpu as pltpu
from jax.sharding import Mesh
from jax.sharding import PartitionSpec as P


AXES = ("depth", "chip", "core")
FILT = ("chip", "core")
CELLS = 128
LIMITS = {
    "stride": 8, "join": 6, "weights": 10, "middle": 20, "result": 8, "grad_l": 10, "back": 26,
    "rows": 2, "sum": 6, "finish": 4,
}
VMEM = pl.BlockSpec(memory_space=pltpu.VMEM)
SMEM = pl.BlockSpec(memory_space=pltpu.SMEM)
TAPS = [(a, b) for a in range(3) for b in range(3)]


def silu_slope(value):
    sigma = jax.nn.sigmoid(value)
    return sigma * (1.0 + value * (1.0 - sigma))


def pairs_of(move):
    depth, filt = lax.axis_size("depth"), lax.axis_size(FILT)
    found = []
    for d in range(depth):
        for f in range(filt):
            e, g = move(d, f)
            if 0 <= e < depth and 0 <= g < filt:
                found.append((d * filt + f, e * filt + g))
    return found


def shifted(value, move):
    return lax.ppermute(value, AXES, pairs_of(move))


def swap_core(value):
    return shifted(value, lambda d, f: (d, f ^ 1))


def swap_chip(value):
    return shifted(value, lambda d, f: (d, f ^ 2))


def four_parts(value, turn):
    far = shifted(value, lambda d, f: (d ^ turn, f ^ 2))
    return [value, swap_core(value), far, swap_core(far)]


def call(name, body, out_shape, scratch=(), flops=0, moved=0, in_specs=None):
    many = isinstance(out_shape, (list, tuple))
    return pl.pallas_call(
        body,
        out_shape=out_shape,
        in_specs=in_specs,
        out_specs=[VMEM] * len(out_shape) if many else VMEM,
        scratch_shapes=list(scratch),
        compiler_params=pltpu.CompilerParams(vmem_limit_bytes=LIMITS[name] << 20),
        cost_estimate=pl.CostEstimate(flops=flops, bytes_accessed=moved, transcendentals=0),
    )


def shape(dims, dtype=jnp.bfloat16):
    return jax.ShapeDtypeStruct(dims, dtype)


def dot(left, right):
    return jnp.dot(left, right, preferred_element_type=jnp.float32)


def dot_rows(left, right):
    return lax.dot_general(
        left, right, (((1,), (1,)), ((), ())), preferred_element_type=jnp.float32
    )


def stride_body(
    info, u_ref, s0, s1, s2, s3, c0, c1, c2, c3,
    act_ref, pre_ref, columns_ref, cot_ref, cells_ref, weights,
):
    filt = info[1]
    for j, part in enumerate((s0, s1, s2, s3)):
        start = pl.multiple_of((filt ^ j) * 32, 32)
        for tap in range(0, 8, 2):
            pair = jnp.concatenate([part[tap], part[tap + 1]], axis=1)
            weights[pl.ds(start, 32), tap * 64 : tap * 64 + 128] = pair
    source = lax.broadcasted_iota(jnp.int32, (256, 256), 0)
    target = lax.broadcasted_iota(jnp.int32, (256, 256), 1)
    pick = source == 2 * (target % 128) + target // 128
    pick = jnp.where(pick, 1.0, 0.0).astype(jnp.bfloat16)
    for p in range(2):
        for r in range(2):
            cell = 2 * p + r
            rows = []
            for a in range(2):
                for b in range(2):
                    split = dot(u_ref[2 * p + a, 2 * r + b], pick).astype(jnp.bfloat16)
                    rows += [split[:, :128], split[:, 128:]]
            block = jnp.concatenate(rows, axis=0)
            columns_ref[:, cell * 128 : cell * 128 + 128] = block
            pre = dot(weights[...], block).T
            pre_ref[p, r] = pre
            act = (pre * jax.nn.sigmoid(pre)).astype(jnp.bfloat16)
            act_ref[p, r * 128 : r * 128 + 128] = act
            for j, part in enumerate((c0, c1, c2, c3)):
                start = pl.multiple_of((filt ^ j) * 32, 32)
                cot_ref[p, r, pl.ds(start, 32), :] = part[filt, r, p]
            cot = cot_ref[p, r].astype(jnp.float32).T.astype(jnp.bfloat16)
            cells_ref[p, r * 128 : r * 128 + 128] = cot


def join_body(info, own, pair, beyond, column_ref):
    odd = info[0] & 1
    for at, part in ((2, own), (4 - 4 * odd, pair), (4 * odd, beyond)):
        column_ref[pl.ds(at, 2)] = part[...]


def fill_window(window, middle, near, cross, core):
    window[:, 2:4] = middle[...]
    window[:, pl.ds(4 - 4 * core, 2)] = near[...]
    window[:, pl.ds(4 * core, 2)] = cross[...]


def fill_forward(weights, parts, filt):
    for j, part in enumerate(parts):
        start = (filt ^ j) * 32
        for n, (a, b) in enumerate(TAPS):
            for c in range(3):
                at = pl.multiple_of(start + c * 128, 32)
                weights[pl.ds(at, 32), n * 128 : n * 128 + 128] = part[9 * a + 3 * b + c]


def fill_backward(weights, parts, filt):
    for j, part in enumerate(parts):
        start = (filt ^ j) * 32
        for n, (a, b) in enumerate(TAPS):
            at = pl.multiple_of(start + n * 128, 32)
            for c in range(3):
                weights[pl.ds(at, 32), c * 128 : c * 128 + 128] = part[9 * a + 3 * b + c]


def weights_body(info, m0, m1, m2, m3, l0, l1, l2, l3, fm_ref, fl_ref, bl_ref, bm_ref):
    filt = info[1]
    fill_forward(fm_ref, (m0, m1, m2, m3), filt)
    fill_forward(fl_ref, (l0, l1, l2, l3), filt)
    fill_backward(bl_ref, (l0, l1, l2, l3), filt)
    fill_backward(bm_ref, (m0, m1, m2, m3), filt)


def column_of(size):
    return lax.broadcasted_iota(jnp.int32, (size, 1), 0) % CELLS


def from_before(value):
    size = value.shape[0]
    return jnp.where(column_of(size) == 0, 0.0, pltpu.roll(value, 1, 0))


def from_after(value):
    size = value.shape[0]
    return jnp.where(column_of(size) == CELLS - 1, 0.0, pltpu.roll(value, size - 1, 0))


def block_of(ref, p, planes, r, rows):
    return ref[pl.ds(p, planes), r : r + rows].reshape(planes * rows * CELLS, 128)


def conv_forward(ref, p, planes, r, rows, weights):
    wide = jnp.concatenate([block_of(ref, p + a, planes, r + b, rows) for a, b in TAPS], axis=1)
    out = dot_rows(wide, weights[...])
    return from_before(out[:, :128]) + out[:, 128:256] + from_after(out[:, 256:])


def conv_backward(ref, p, planes, r, rows, weights):
    wide = jnp.concatenate(
        [block_of(ref, p + 2 - a, planes, r + 2 - b, rows) for a, b in TAPS], axis=1
    )
    out = dot(wide, weights[...])
    return from_after(out[:, :128]) + out[:, 128:256] + from_before(out[:, 256:])


def inside(info):
    depth, filt = info[0], info[1]
    cell = lax.broadcasted_iota(jnp.int32, (16 * CELLS, 1), 0) // CELLS
    plane, row = cell // 4, cell % 4
    valid = (plane >= jnp.where(depth == 0, 1, 0)) & (row >= jnp.where(filt == 0, 1, 0))
    last = jnp.where(depth == lax.axis_size("depth") - 1, 2, 3)
    return valid & (plane <= last) & (row <= jnp.where(filt == 3, 2, 3))


def middle_body(info, mid, near, cross, weights, act_ref, pre_ref, window):
    fill_window(window, mid, near, cross, info[4])

    pre = conv_forward(window, 0, 4, 0, 4, weights)
    act = jnp.where(inside(info), pre * jax.nn.sigmoid(pre), 0.0)
    pre_ref[...] = pre.reshape(4, 4, CELLS, 128)
    act_ref[...] = act.astype(jnp.bfloat16).reshape(4, 4, CELLS, 128)


def result_body(info, act_ref, weights, near_ref, far_ref, turned):
    filt = info[1]
    out = conv_forward(act_ref, 0, 2, 0, 2, weights)
    for p in range(2):
        for r in range(2):
            at = (2 * p + r) * CELLS
            turned[...] = out[at : at + CELLS].T.astype(jnp.bfloat16)
            for j, ref in enumerate((near_ref, far_ref, near_ref, far_ref)):
                start = pl.multiple_of((filt ^ j) * 32, 32)
                ref[j // 2, p, r] = turned[pl.ds(start, 32), :]


def rows_body(info, own, near, far, out_ref):
    filt = info[1]
    for j, part in enumerate((own.at[0], near.at[0], far.at[0], far.at[1])):
        out_ref[filt ^ j] = part[...]


def shifts_of(value):
    lane = lax.broadcasted_iota(jnp.int32, value.shape, 1) % CELLS
    size = value.shape[1]
    after = jnp.where(lane == CELLS - 1, 0.0, pltpu.roll(value, size - 1, 1))
    before = jnp.where(lane == 0, 0.0, pltpu.roll(value, 1, 1))
    return jnp.concatenate([after, value, before], axis=0).astype(jnp.bfloat16)


def in_order(ref, at, core):
    rows = [ref[at + (pl.ds(pl.multiple_of((k ^ core) * 32, 32), 32),)] for k in range(4)]
    return jnp.concatenate(rows, axis=0)


def put_grad(refs, slot, block):
    for k in range(4):
        refs[k % 2][k // 2, slot] = block[k * 32 : k * 32 + 32].astype(jnp.bfloat16)


def put_kernel_grad(refs, first, grad):
    for n, (a, b) in enumerate(TAPS):
        for c in range(3):
            block = grad[c * 128 : c * 128 + 128, n * 128 : n * 128 + 128]
            put_grad(refs, first + 9 * a + 3 * b + c, block)


def last_body(info, mid_act, cot_own, keep_ref, send_ref):
    core = info[4]
    own = [in_order(cot_own, (p, r), core).astype(jnp.float32) for p in range(2) for r in range(2)]
    cot_rows = shifts_of(jnp.concatenate(own, axis=1))
    wide = jnp.concatenate([block_of(mid_act, a, 2, b, 2) for a, b in TAPS], axis=1)
    put_kernel_grad((keep_ref, send_ref), 0, dot(cot_rows, wide))


def back_body(
    info, act_window, mid, near, cross, weights_l, weights_m, mid_pre, level_pre, columns,
    keep_ref, send_ref, window, delta, turned,
):
    core = info[4]
    refs = (keep_ref, send_ref)
    fill_window(window, mid, near, cross, core)

    back = conv_backward(window, 0, 4, 0, 4, weights_l)
    here = jnp.where(inside(info), back * silu_slope(mid_pre[...].reshape(16 * CELLS, 128)), 0.0)
    delta[...] = here.astype(jnp.bfloat16).reshape(4, 4, CELLS, 128)

    for p in range(2):
        for r in range(2):
            at = (2 * p + r) * CELLS
            turned[:, at : at + CELLS] = delta[1 + p, 1 + r].astype(jnp.float32).T
    delta_rows = shifts_of(in_order(turned, (), core))
    wide = jnp.concatenate([block_of(act_window, 1 + a, 2, 1 + b, 2) for a, b in TAPS], axis=1)
    put_kernel_grad(refs, 0, dot(delta_rows, wide))

    back = conv_backward(delta, 0, 2, 0, 2, weights_m)
    pre = level_pre[...].reshape(4 * CELLS, 128)
    level_delta = (back * silu_slope(pre)).astype(jnp.bfloat16)
    grad = dot(columns[...], level_delta)
    for n in range(4):
        turned[:, n * 128 : n * 128 + 128] = grad[n * 128 : n * 128 + 128].T
    ordered = in_order(turned, (), core)
    for n in range(4):
        put_grad(refs, 27 + n, ordered[:, n * 128 : n * 128 + 128])
    for n in range(31, 37):
        put_grad(refs, n, jnp.zeros((128, 128), jnp.float32))


def finish_body(full_ref, stride_ref, middle_ref, last_ref):
    last_ref[...] = full_ref[0:27].astype(jnp.float32)
    middle_ref[...] = full_ref[27:54].astype(jnp.float32)
    for n in range(4):
        block = full_ref[54 + n].astype(jnp.float32)
        stride_ref[2 * n] = block[:, :64]
        stride_ref[2 * n + 1] = block[:, 64:]


def sum_body(terms_ref, out_ref):
    total = jnp.sum(terms_ref[...].astype(jnp.float32), axis=0).astype(jnp.bfloat16)
    out_ref[...] = jnp.broadcast_to(total[None], out_ref.shape)


def neighbourhood(info, own):
    def inner(d, f):
        return (d, 3 - f) if f in (1, 2) else (-1, f)

    beyond = shifted(own, lambda d, f: (d + 1 if d % 2 else d - 1, f))
    pair = shifted(own, lambda d, f: (d ^ 1, f))
    column = call(
        "join", join_body, shape((6, 256, 128)), in_specs=[SMEM] + [VMEM] * 3
    )(info, own, pair, beyond)
    cross = shifted(column, inner)
    near = swap_core(column)
    return [x.reshape(6, 2, 128, 128) for x in (column, near, cross)]


def whole(upper_level, stride_weight, middle_weight, last_weight, cotangent):
    depth = lax.axis_size("depth")
    chip, core = lax.axis_index("chip"), lax.axis_index("core")
    info = jnp.stack([lax.axis_index("depth"), 2 * chip + core, jnp.int32(depth), chip, core])
    cot_rows = cotangent.reshape(32, 2, 4, 2, 128).transpose(2, 3, 1, 0, 4)
    cot_parts = four_parts(cot_rows, 0)
    stride_parts = four_parts(stride_weight, 0)
    middle_parts = four_parts(middle_weight, 0)
    last_parts = four_parts(last_weight, 4)
    upper = upper_level.transpose(1, 2, 0, 3)

    level_act, level_pre, columns, cot_own, cot_cells = call(
        "stride",
        stride_body,
        [
            shape((2, 256, 128)),
            shape((2, 2, 128, 128), jnp.float32),
            shape((512, 512)),
            shape((2, 2, 128, 128)),
            shape((2, 256, 128)),
        ],
        [pltpu.VMEM((128, 512), jnp.bfloat16)],
        flops=200_000_000,
        moved=1_500_000,
        in_specs=[SMEM] + [VMEM] * 9,
    )(info, upper, *stride_parts, *cot_parts)
    act_parts = neighbourhood(info, level_act)
    back_parts = neighbourhood(info, cot_cells)

    forward_m, forward_l, backward_l, backward_m = call(
        "weights",
        weights_body,
        [shape((384, 1152))] * 2 + [shape((1152, 384))] * 2,
        flops=1_000_000,
        moved=6_000_000,
        in_specs=[SMEM] + [VMEM] * 8,
    )(info, *middle_parts, *last_parts)

    mid_act, mid_pre, act_window = call(
        "middle",
        middle_body,
        [shape((4, 4, 128, 128)), shape((4, 4, 128, 128), jnp.float32), shape((6, 6, 128, 128))],
        flops=3_000_000_000,
        moved=4_000_000,
        in_specs=[SMEM] + [VMEM] * 4,
    )(info, *act_parts, forward_m)

    stay, leave = call(
        "result",
        result_body,
        [shape((2, 2, 2, 32, 128))] * 2,
        [pltpu.VMEM((128, 128), jnp.bfloat16)],
        flops=500_000_000,
        moved=2_000_000,
        in_specs=[SMEM] + [VMEM] * 2,
    )(info, mid_act, forward_l)
    result_near = swap_core(leave)
    result_far = swap_chip(jnp.stack([stay[1], result_near[1]]))

    keep_l, send_l = call(
        "grad_l",
        last_body,
        [shape((2, 27, 32, 128))] * 2,
        flops=500_000_000,
        moved=3_000_000,
        in_specs=[SMEM] + [VMEM] * 2,
    )(info, mid_act, cot_own)
    other_l = swap_core(send_l)

    keep, send = call(
        "back",
        back_body,
        [shape((2, 37, 32, 128))] * 2,
        [
            pltpu.VMEM((6, 6, 128, 128), jnp.bfloat16),
            pltpu.VMEM((4, 4, 128, 128), jnp.bfloat16),
            pltpu.VMEM((128, 512), jnp.float32),
        ],
        flops=4_000_000_000,
        moved=8_000_000,
        in_specs=[SMEM] + [VMEM] * 9,
    )(
        info, act_window, *back_parts, backward_l, backward_m, mid_pre, level_pre, columns
    )

    result = call(
        "rows", rows_body, shape((4, 2, 2, 32, 128)), in_specs=[SMEM] + [VMEM] * 3
    )(info, stay, result_near, result_far)
    result = result.transpose(3, 1, 0, 2, 4).reshape(32, 2, 8, 128)

    other = swap_core(send)
    terms = jnp.concatenate(
        [
            (x.astype(jnp.float32) + y.astype(jnp.float32)).astype(jnp.bfloat16)
            for x, y in ((keep_l, other_l), (keep, other))
        ],
        axis=1,
    )
    terms = lax.all_to_all(terms.reshape(2 * depth, 64, 128), ("chip", "depth"), 0, 0, tiled=True)
    spread = call("sum", sum_body, shape((depth, 64, 128)), in_specs=[VMEM])(terms)
    full = lax.all_to_all(spread, "depth", 0, 0, tiled=True)
    grads = call(
        "finish",
        finish_body,
        [
            shape((8, 32, 64), jnp.float32),
            shape((27, 32, 128), jnp.float32),
            shape((27, 32, 128), jnp.float32),
        ],
        in_specs=[VMEM],
    )(full.reshape(64, 32, 128))
    return (result, *grads)


def solution(mesh):
    placed = (
        P(None, "depth", FILT, None),
        P(None, FILT, None),
        P(None, FILT, None),
        P(None, FILT, None),
        P(FILT, "depth", None, None),
    )
    fine = Mesh(mesh.devices.reshape(-1, 2, 2), AXES)
    return jax.shard_map(
        whole,
        mesh=fine,
        in_specs=placed,
        out_specs=(
            P(FILT, "depth", None, None),
            P(None, FILT, None),
            P(None, FILT, None),
            P(None, FILT, None),
        ),
        check_vma=False,
    )
```

```python
import jax
import jax.numpy as jnp
from jax import lax
from jax.experimental import pallas as pl
from jax.experimental.pallas import tpu as pltpu
from jax.sharding import Mesh
from jax.sharding import PartitionSpec as P


AXES = ("depth", "chip", "core")
FILT = ("chip", "core")
CELLS = 128
LIMITS = {
    "stride": 8, "join": 6, "weights": 10, "middle": 20, "result": 8, "grad_l": 10, "back": 26,
    "rows": 2, "sum": 6, "finish": 4,
}
VMEM = pl.BlockSpec(memory_space=pltpu.VMEM)
SMEM = pl.BlockSpec(memory_space=pltpu.SMEM)
TAPS = [(a, b) for a in range(3) for b in range(3)]


def silu_slope(value):
    sigma = jax.nn.sigmoid(value)
    return sigma * (1.0 + value * (1.0 - sigma))


def pairs_of(move):
    depth, filt = lax.axis_size("depth"), lax.axis_size(FILT)
    found = []
    for d in range(depth):
        for f in range(filt):
            e, g = move(d, f)
            if 0 <= e < depth and 0 <= g < filt:
                found.append((d * filt + f, e * filt + g))
    return found


def shifted(value, move):
    return lax.ppermute(value, AXES, pairs_of(move))


def swap_core(value):
    return shifted(value, lambda d, f: (d, f ^ 1))


def swap_chip(value):
    return shifted(value, lambda d, f: (d, f ^ 2))


def four_parts(value, turn):
    far = shifted(value, lambda d, f: (d ^ turn, f ^ 2))
    return [value, swap_core(value), far, swap_core(far)]


def call(name, body, out_shape, scratch=(), flops=0, moved=0, in_specs=None):
    many = isinstance(out_shape, (list, tuple))
    return pl.pallas_call(
        body,
        out_shape=out_shape,
        in_specs=in_specs,
        out_specs=[VMEM] * len(out_shape) if many else VMEM,
        scratch_shapes=list(scratch),
        compiler_params=pltpu.CompilerParams(vmem_limit_bytes=LIMITS[name] << 20),
        cost_estimate=pl.CostEstimate(flops=flops, bytes_accessed=moved, transcendentals=0),
    )


def shape(dims, dtype=jnp.bfloat16):
    return jax.ShapeDtypeStruct(dims, dtype)


def dot(left, right):
    return jnp.dot(left, right, preferred_element_type=jnp.float32)


def dot_rows(left, right):
    return lax.dot_general(
        left, right, (((1,), (1,)), ((), ())), preferred_element_type=jnp.float32
    )


def stride_body(
    info, u_ref, s0, s1, s2, s3, c0, c1, c2, c3,
    act_ref, pre_ref, columns_ref, cot_ref, cells_ref, weights,
):
    filt = info[1]
    for j, part in enumerate((s0, s1, s2, s3)):
        start = pl.multiple_of((filt ^ j) * 32, 32)
        for tap in range(0, 8, 2):
            pair = jnp.concatenate([part[tap], part[tap + 1]], axis=1)
            weights[pl.ds(start, 32), tap * 64 : tap * 64 + 128] = pair
    source = lax.broadcasted_iota(jnp.int32, (256, 256), 0)
    target = lax.broadcasted_iota(jnp.int32, (256, 256), 1)
    pick = source == 2 * (target % 128) + target // 128
    pick = jnp.where(pick, 1.0, 0.0).astype(jnp.bfloat16)
    for p in range(2):
        for r in range(2):
            cell = 2 * p + r
            rows = []
            for a in range(2):
                for b in range(2):
                    split = dot(u_ref[2 * p + a, 2 * r + b], pick).astype(jnp.bfloat16)
                    rows += [split[:, :128], split[:, 128:]]
            block = jnp.concatenate(rows, axis=0)
            columns_ref[:, cell * 128 : cell * 128 + 128] = block
            pre = dot(weights[...], block).T
            pre_ref[p, r] = pre
            act = (pre * jax.nn.sigmoid(pre)).astype(jnp.bfloat16)
            act_ref[p, r * 128 : r * 128 + 128] = act
            for j, part in enumerate((c0, c1, c2, c3)):
                start = pl.multiple_of((filt ^ j) * 32, 32)
                cot_ref[p, r, pl.ds(start, 32), :] = part[filt, r, p]
            cot = cot_ref[p, r].astype(jnp.float32).T.astype(jnp.bfloat16)
            cells_ref[p, r * 128 : r * 128 + 128] = cot


def join_body(info, own, pair, beyond, column_ref):
    odd = info[0] & 1
    for at, part in ((2, own), (4 - 4 * odd, pair), (4 * odd, beyond)):
        column_ref[pl.ds(at, 2)] = part[...]


def fill_window(window, middle, near, cross, core):
    window[:, 2:4] = middle[...]
    window[:, pl.ds(4 - 4 * core, 2)] = near[...]
    window[:, pl.ds(4 * core, 2)] = cross[...]


def fill_forward(weights, parts, filt):
    for j, part in enumerate(parts):
        start = (filt ^ j) * 32
        for n, (a, b) in enumerate(TAPS):
            for c in range(3):
                at = pl.multiple_of(start + c * 128, 32)
                weights[pl.ds(at, 32), n * 128 : n * 128 + 128] = part[9 * a + 3 * b + c]


def fill_backward(weights, parts, filt):
    for j, part in enumerate(parts):
        start = (filt ^ j) * 32
        for n, (a, b) in enumerate(TAPS):
            at = pl.multiple_of(start + n * 128, 32)
            for c in range(3):
                weights[pl.ds(at, 32), c * 128 : c * 128 + 128] = part[9 * a + 3 * b + c]


def weights_body(info, m0, m1, m2, m3, l0, l1, l2, l3, fm_ref, fl_ref, bl_ref, bm_ref):
    filt = info[1]
    fill_forward(fm_ref, (m0, m1, m2, m3), filt)
    fill_forward(fl_ref, (l0, l1, l2, l3), filt)
    fill_backward(bl_ref, (l0, l1, l2, l3), filt)
    fill_backward(bm_ref, (m0, m1, m2, m3), filt)


def column_of(size):
    return lax.broadcasted_iota(jnp.int32, (size, 1), 0) % CELLS


def from_before(value):
    size = value.shape[0]
    return jnp.where(column_of(size) == 0, 0.0, pltpu.roll(value, 1, 0))


def from_after(value):
    size = value.shape[0]
    return jnp.where(column_of(size) == CELLS - 1, 0.0, pltpu.roll(value, size - 1, 0))


def block_of(ref, p, planes, r, rows):
    return ref[pl.ds(p, planes), r : r + rows].reshape(planes * rows * CELLS, 128)


def conv_forward(ref, p, planes, r, rows, weights):
    wide = jnp.concatenate([block_of(ref, p + a, planes, r + b, rows) for a, b in TAPS], axis=1)
    out = dot_rows(wide, weights[...])
    return from_before(out[:, :128]) + out[:, 128:256] + from_after(out[:, 256:])


def conv_backward(ref, p, planes, r, rows, weights):
    wide = jnp.concatenate(
        [block_of(ref, p + 2 - a, planes, r + 2 - b, rows) for a, b in TAPS], axis=1
    )
    out = dot(wide, weights[...])
    return from_after(out[:, :128]) + out[:, 128:256] + from_before(out[:, 256:])


def inside(info):
    depth, filt = info[0], info[1]
    cell = lax.broadcasted_iota(jnp.int32, (16 * CELLS, 1), 0) // CELLS
    plane, row = cell // 4, cell % 4
    valid = (plane >= jnp.where(depth == 0, 1, 0)) & (row >= jnp.where(filt == 0, 1, 0))
    last = jnp.where(depth == lax.axis_size("depth") - 1, 2, 3)
    return valid & (plane <= last) & (row <= jnp.where(filt == 3, 2, 3))


def middle_body(info, mid, near, cross, weights, act_ref, pre_ref, window):
    fill_window(window, mid, near, cross, info[4])

    pre = conv_forward(window, 0, 4, 0, 4, weights)
    act = jnp.where(inside(info), pre * jax.nn.sigmoid(pre), 0.0)
    pre_ref[...] = pre.reshape(4, 4, CELLS, 128)
    act_ref[...] = act.astype(jnp.bfloat16).reshape(4, 4, CELLS, 128)


def result_body(info, act_ref, weights, near_ref, far_ref, turned):
    filt = info[1]
    out = conv_forward(act_ref, 0, 2, 0, 2, weights)
    for p in range(2):
        for r in range(2):
            at = (2 * p + r) * CELLS
            turned[...] = out[at : at + CELLS].T.astype(jnp.bfloat16)
            for j, ref in enumerate((near_ref, far_ref, near_ref, far_ref)):
                start = pl.multiple_of((filt ^ j) * 32, 32)
                ref[j // 2, p, r] = turned[pl.ds(start, 32), :]


def rows_body(info, own, near, far, out_ref):
    filt = info[1]
    for j, part in enumerate((own.at[0], near.at[0], far.at[0], far.at[1])):
        out_ref[filt ^ j] = part[...]


def shifts_of(value):
    lane = lax.broadcasted_iota(jnp.int32, value.shape, 1) % CELLS
    size = value.shape[1]
    after = jnp.where(lane == CELLS - 1, 0.0, pltpu.roll(value, size - 1, 1))
    before = jnp.where(lane == 0, 0.0, pltpu.roll(value, 1, 1))
    return jnp.concatenate([after, value, before], axis=0).astype(jnp.bfloat16)


def in_order(ref, at, core):
    rows = [ref[at + (pl.ds(pl.multiple_of((k ^ core) * 32, 32), 32),)] for k in range(4)]
    return jnp.concatenate(rows, axis=0)


def put_grad(refs, slot, block):
    for k in range(4):
        refs[k % 2][k // 2, slot] = block[k * 32 : k * 32 + 32].astype(jnp.bfloat16)


def put_kernel_grad(refs, first, grad):
    for n, (a, b) in enumerate(TAPS):
        for c in range(3):
            block = grad[c * 128 : c * 128 + 128, n * 128 : n * 128 + 128]
            put_grad(refs, first + 9 * a + 3 * b + c, block)


def last_body(info, mid_act, cot_own, keep_ref, send_ref):
    core = info[4]
    own = [in_order(cot_own, (p, r), core).astype(jnp.float32) for p in range(2) for r in range(2)]
    cot_rows = shifts_of(jnp.concatenate(own, axis=1))
    wide = jnp.concatenate([block_of(mid_act, a, 2, b, 2) for a, b in TAPS], axis=1)
    put_kernel_grad((keep_ref, send_ref), 0, dot(cot_rows, wide))


def back_body(
    info, act_window, mid, near, cross, weights_l, weights_m, mid_pre, level_pre, columns,
    keep_ref, send_ref, window, delta, turned,
):
    core = info[4]
    refs = (keep_ref, send_ref)
    fill_window(window, mid, near, cross, core)

    back = conv_backward(window, 0, 4, 0, 4, weights_l)
    here = jnp.where(inside(info), back * silu_slope(mid_pre[...].reshape(16 * CELLS, 128)), 0.0)
    delta[...] = here.astype(jnp.bfloat16).reshape(4, 4, CELLS, 128)

    for p in range(2):
        for r in range(2):
            at = (2 * p + r) * CELLS
            turned[:, at : at + CELLS] = delta[1 + p, 1 + r].astype(jnp.float32).T
    delta_rows = shifts_of(in_order(turned, (), core))
    wide = jnp.concatenate([block_of(act_window, 1 + a, 2, 1 + b, 2) for a, b in TAPS], axis=1)
    put_kernel_grad(refs, 0, dot(delta_rows, wide))

    back = conv_backward(delta, 0, 2, 0, 2, weights_m)
    pre = level_pre[...].reshape(4 * CELLS, 128)
    level_delta = (back * silu_slope(pre)).astype(jnp.bfloat16)
    grad = dot(columns[...], level_delta)
    for n in range(4):
        turned[:, n * 128 : n * 128 + 128] = grad[n * 128 : n * 128 + 128].T
    ordered = in_order(turned, (), core)
    for n in range(4):
        put_grad(refs, 27 + n, ordered[:, n * 128 : n * 128 + 128])
    for n in range(31, 37):
        put_grad(refs, n, jnp.zeros((128, 128), jnp.float32))


def finish_body(full_ref, stride_ref, middle_ref, last_ref):
    last_ref[...] = full_ref[0:27].astype(jnp.float32)
    middle_ref[...] = full_ref[27:54].astype(jnp.float32)
    for n in range(4):
        block = full_ref[54 + n].astype(jnp.float32)
        stride_ref[2 * n] = block[:, :64]
        stride_ref[2 * n + 1] = block[:, 64:]


def sum_body(terms_ref, out_ref):
    count, rows = terms_ref.shape[0], terms_ref.shape[1]
    for at in range(0, rows, 16):
        sums = [terms_ref[k, at : at + 16].astype(jnp.float32) for k in range(4)]
        for k in range(4, count):
            sums[k % 4] = sums[k % 4] + terms_ref[k, at : at + 16].astype(jnp.float32)
        total = ((sums[0] + sums[1]) + (sums[2] + sums[3])).astype(jnp.bfloat16)
        for d in range(out_ref.shape[0]):
            out_ref[d, at : at + 16] = total


def neighbourhood(info, own):
    def inner(d, f):
        return (d, 3 - f) if f in (1, 2) else (-1, f)

    beyond = shifted(own, lambda d, f: (d + 1 if d % 2 else d - 1, f))
    pair = shifted(own, lambda d, f: (d ^ 1, f))
    column = call(
        "join", join_body, shape((6, 256, 128)), in_specs=[SMEM] + [VMEM] * 3
    )(info, own, pair, beyond)
    cross = shifted(column, inner)
    near = swap_core(column)
    return [x.reshape(6, 2, 128, 128) for x in (column, near, cross)]


def whole(upper_level, stride_weight, middle_weight, last_weight, cotangent):
    depth = lax.axis_size("depth")
    chip, core = lax.axis_index("chip"), lax.axis_index("core")
    info = jnp.stack([lax.axis_index("depth"), 2 * chip + core, jnp.int32(depth), chip, core])
    cot_rows = cotangent.reshape(32, 2, 4, 2, 128).transpose(2, 3, 1, 0, 4)
    cot_parts = four_parts(cot_rows, 0)
    stride_parts = four_parts(stride_weight, 0)
    middle_parts = four_parts(middle_weight, 0)
    last_parts = four_parts(last_weight, 4)
    upper = upper_level.transpose(1, 2, 0, 3)

    level_act, level_pre, columns, cot_own, cot_cells = call(
        "stride",
        stride_body,
        [
            shape((2, 256, 128)),
            shape((2, 2, 128, 128), jnp.float32),
            shape((512, 512)),
            shape((2, 2, 128, 128)),
            shape((2, 256, 128)),
        ],
        [pltpu.VMEM((128, 512), jnp.bfloat16)],
        flops=200_000_000,
        moved=1_500_000,
        in_specs=[SMEM] + [VMEM] * 9,
    )(info, upper, *stride_parts, *cot_parts)
    act_parts = neighbourhood(info, level_act)
    back_parts = neighbourhood(info, cot_cells)

    forward_m, forward_l, backward_l, backward_m = call(
        "weights",
        weights_body,
        [shape((384, 1152))] * 2 + [shape((1152, 384))] * 2,
        flops=1_000_000,
        moved=6_000_000,
        in_specs=[SMEM] + [VMEM] * 8,
    )(info, *middle_parts, *last_parts)

    mid_act, mid_pre, act_window = call(
        "middle",
        middle_body,
        [shape((4, 4, 128, 128)), shape((4, 4, 128, 128), jnp.float32), shape((6, 6, 128, 128))],
        flops=3_000_000_000,
        moved=4_000_000,
        in_specs=[SMEM] + [VMEM] * 4,
    )(info, *act_parts, forward_m)

    stay, leave = call(
        "result",
        result_body,
        [shape((2, 2, 2, 32, 128))] * 2,
        [pltpu.VMEM((128, 128), jnp.bfloat16)],
        flops=500_000_000,
        moved=2_000_000,
        in_specs=[SMEM] + [VMEM] * 2,
    )(info, mid_act, forward_l)
    result_near = swap_core(leave)
    result_far = swap_chip(jnp.stack([stay[1], result_near[1]]))

    keep_l, send_l = call(
        "grad_l",
        last_body,
        [shape((2, 27, 32, 128))] * 2,
        flops=500_000_000,
        moved=3_000_000,
        in_specs=[SMEM] + [VMEM] * 2,
    )(info, mid_act, cot_own)
    other_l = swap_core(send_l)

    keep, send = call(
        "back",
        back_body,
        [shape((2, 37, 32, 128))] * 2,
        [
            pltpu.VMEM((6, 6, 128, 128), jnp.bfloat16),
            pltpu.VMEM((4, 4, 128, 128), jnp.bfloat16),
            pltpu.VMEM((128, 512), jnp.float32),
        ],
        flops=4_000_000_000,
        moved=8_000_000,
        in_specs=[SMEM] + [VMEM] * 9,
    )(
        info, act_window, *back_parts, backward_l, backward_m, mid_pre, level_pre, columns
    )

    result = call(
        "rows", rows_body, shape((4, 2, 2, 32, 128)), in_specs=[SMEM] + [VMEM] * 3
    )(info, stay, result_near, result_far)
    result = result.transpose(3, 1, 0, 2, 4).reshape(32, 2, 8, 128)

    other = swap_core(send)
    terms = jnp.concatenate(
        [
            (x.astype(jnp.float32) + y.astype(jnp.float32)).astype(jnp.bfloat16)
            for x, y in ((keep_l, other_l), (keep, other))
        ],
        axis=1,
    )
    terms = lax.all_to_all(terms.reshape(2 * depth, 64, 128), ("chip", "depth"), 0, 0, tiled=True)
    spread = call("sum", sum_body, shape((depth, 64, 128)), in_specs=[VMEM])(terms)
    full = lax.all_to_all(spread, "depth", 0, 0, tiled=True)
    grads = call(
        "finish",
        finish_body,
        [
            shape((8, 32, 64), jnp.float32),
            shape((27, 32, 128), jnp.float32),
            shape((27, 32, 128), jnp.float32),
        ],
        in_specs=[VMEM],
    )(full.reshape(64, 32, 128))
    return (result, *grads)


def solution(mesh):
    placed = (
        P(None, "depth", FILT, None),
        P(None, FILT, None),
        P(None, FILT, None),
        P(None, FILT, None),
        P(FILT, "depth", None, None),
    )
    fine = Mesh(mesh.devices.reshape(-1, 2, 2), AXES)
    return jax.shard_map(
        whole,
        mesh=fine,
        in_specs=placed,
        out_specs=(
            P(FILT, "depth", None, None),
            P(None, FILT, None),
            P(None, FILT, None),
            P(None, FILT, None),
        ),
        check_vma=False,
    )
```

```python
import functools

import jax
import jax.numpy as jnp
from jax import lax
from jax.experimental import pallas as pl
from jax.experimental.pallas import tpu as pltpu
from jax.sharding import Mesh
from jax.sharding import PartitionSpec as P


AXES = ("depth", "chip", "core")
FILT = ("chip", "core")
CELLS = 128
LIMITS = {
    "stride": 8, "join": 6, "weights": 10, "middle": 20, "result": 8, "grad_l": 10, "back": 26,
    "rows": 2, "sum": 6, "finish": 4,
}
VMEM = pl.BlockSpec(memory_space=pltpu.VMEM)
SMEM = pl.BlockSpec(memory_space=pltpu.SMEM)
TAPS = [(a, b) for a in range(3) for b in range(3)]


def silu_slope(value):
    sigma = jax.nn.sigmoid(value)
    return sigma * (1.0 + value * (1.0 - sigma))


def pairs_of(move):
    depth, filt = lax.axis_size("depth"), lax.axis_size(FILT)
    found = []
    for d in range(depth):
        for f in range(filt):
            e, g = move(d, f)
            if 0 <= e < depth and 0 <= g < filt:
                found.append((d * filt + f, e * filt + g))
    return found


def shifted(value, move):
    return lax.ppermute(value, AXES, pairs_of(move))


def swap_core(value):
    return shifted(value, lambda d, f: (d, f ^ 1))


def swap_chip(value):
    return shifted(value, lambda d, f: (d, f ^ 2))


def four_parts(value, turn):
    far = shifted(value, lambda d, f: (d ^ turn, f ^ 2))
    return [value, swap_core(value), far, swap_core(far)]


def call(name, body, out_shape, scratch=(), flops=0, moved=0, in_specs=None):
    many = isinstance(out_shape, (list, tuple))
    return pl.pallas_call(
        body,
        out_shape=out_shape,
        in_specs=in_specs,
        out_specs=[VMEM] * len(out_shape) if many else VMEM,
        scratch_shapes=list(scratch),
        compiler_params=pltpu.CompilerParams(vmem_limit_bytes=LIMITS[name] << 20),
        cost_estimate=pl.CostEstimate(flops=flops, bytes_accessed=moved, transcendentals=0),
    )


def shape(dims, dtype=jnp.bfloat16):
    return jax.ShapeDtypeStruct(dims, dtype)


def dot(left, right):
    return jnp.dot(left, right, preferred_element_type=jnp.float32)


def dot_rows(left, right):
    return lax.dot_general(
        left, right, (((1,), (1,)), ((), ())), preferred_element_type=jnp.float32
    )


def stride_body(
    info, u_ref, s0, s1, s2, s3, c0, c1, c2, c3,
    act_ref, pre_ref, columns_ref, cot_ref, cells_ref, pack_ref, weights,
):
    filt = info[1]
    for j, part in enumerate((s0, s1, s2, s3)):
        start = pl.multiple_of((filt ^ j) * 32, 32)
        for tap in range(0, 8, 2):
            pair = jnp.concatenate([part[tap], part[tap + 1]], axis=1)
            weights[pl.ds(start, 32), tap * 64 : tap * 64 + 128] = pair
    source = lax.broadcasted_iota(jnp.int32, (256, 256), 0)
    target = lax.broadcasted_iota(jnp.int32, (256, 256), 1)
    pick = source == 2 * (target % 128) + target // 128
    pick = jnp.where(pick, 1.0, 0.0).astype(jnp.bfloat16)
    for p in range(2):
        for r in range(2):
            cell = 2 * p + r
            rows = []
            for a in range(2):
                for b in range(2):
                    split = dot(u_ref[2 * p + a, 2 * r + b], pick).astype(jnp.bfloat16)
                    rows += [split[:, :128], split[:, 128:]]
            block = jnp.concatenate(rows, axis=0)
            columns_ref[:, cell * 128 : cell * 128 + 128] = block
            pre = dot(weights[...], block).T
            pre_ref[p, r] = pre
            act = (pre * jax.nn.sigmoid(pre)).astype(jnp.bfloat16)
            act_ref[p, r * 128 : r * 128 + 128] = act
            pack_ref[p, r * 128 : r * 128 + 128] = act
            for j, part in enumerate((c0, c1, c2, c3)):
                start = pl.multiple_of((filt ^ j) * 32, 32)
                cot_ref[p, r, pl.ds(start, 32), :] = part[filt, r, p]
            cot = cot_ref[p, r].astype(jnp.float32).T.astype(jnp.bfloat16)
            cells_ref[p, r * 128 : r * 128 + 128] = cot
            pack_ref[p, 256 + r * 128 : 384 + r * 128] = cot


def join_body(first, info, own, pair, beyond, column_ref):
    odd = info[0] & 1
    column_ref[2:4] = own[...]
    column_ref[pl.ds(4 - 4 * odd, 2)] = pair[...]
    column_ref[pl.ds(4 * odd, 2)] = beyond[:, first : first + 256]


def fill_window(window, middle, near, cross, core):
    window[:, 2:4] = middle[...]
    window[:, pl.ds(4 - 4 * core, 2)] = near[...]
    window[:, pl.ds(4 * core, 2)] = cross[...]


def fill_forward(weights, parts, filt):
    for j, part in enumerate(parts):
        start = (filt ^ j) * 32
        for n, (a, b) in enumerate(TAPS):
            for c in range(3):
                at = pl.multiple_of(start + c * 128, 32)
                weights[pl.ds(at, 32), n * 128 : n * 128 + 128] = part[9 * a + 3 * b + c]


def fill_backward(weights, parts, filt):
    for j, part in enumerate(parts):
        start = (filt ^ j) * 32
        for n, (a, b) in enumerate(TAPS):
            at = pl.multiple_of(start + n * 128, 32)
            for c in range(3):
                weights[pl.ds(at, 32), c * 128 : c * 128 + 128] = part[9 * a + 3 * b + c]


def weights_body(info, m0, m1, m2, m3, l0, l1, l2, l3, fm_ref, fl_ref, bl_ref, bm_ref):
    filt = info[1]
    fill_forward(fm_ref, (m0, m1, m2, m3), filt)
    fill_forward(fl_ref, (l0, l1, l2, l3), filt)
    fill_backward(bl_ref, (l0, l1, l2, l3), filt)
    fill_backward(bm_ref, (m0, m1, m2, m3), filt)


def column_of(size):
    return lax.broadcasted_iota(jnp.int32, (size, 1), 0) % CELLS


def from_before(value):
    size = value.shape[0]
    return jnp.where(column_of(size) == 0, 0.0, pltpu.roll(value, 1, 0))


def from_after(value):
    size = value.shape[0]
    return jnp.where(column_of(size) == CELLS - 1, 0.0, pltpu.roll(value, size - 1, 0))


def block_of(ref, p, planes, r, rows):
    return ref[pl.ds(p, planes), r : r + rows].reshape(planes * rows * CELLS, 128)


def conv_forward(ref, p, planes, r, rows, weights):
    wide = jnp.concatenate([block_of(ref, p + a, planes, r + b, rows) for a, b in TAPS], axis=1)
    out = dot_rows(wide, weights[...])
    return from_before(out[:, :128]) + out[:, 128:256] + from_after(out[:, 256:])


def conv_backward(ref, p, planes, r, rows, weights):
    wide = jnp.concatenate(
        [block_of(ref, p + 2 - a, planes, r + 2 - b, rows) for a, b in TAPS], axis=1
    )
    out = dot(wide, weights[...])
    return from_after(out[:, :128]) + out[:, 128:256] + from_before(out[:, 256:])


def inside(info):
    depth, filt = info[0], info[1]
    cell = lax.broadcasted_iota(jnp.int32, (16 * CELLS, 1), 0) // CELLS
    plane, row = cell // 4, cell % 4
    valid = (plane >= jnp.where(depth == 0, 1, 0)) & (row >= jnp.where(filt == 0, 1, 0))
    last = jnp.where(depth == lax.axis_size("depth") - 1, 2, 3)
    return valid & (plane <= last) & (row <= jnp.where(filt == 3, 2, 3))


def middle_body(info, mid, near, cross, weights, act_ref, pre_ref, window):
    fill_window(window, mid, near, cross, info[4])

    pre = conv_forward(window, 0, 4, 0, 4, weights)
    act = jnp.where(inside(info), pre * jax.nn.sigmoid(pre), 0.0)
    pre_ref[...] = pre.reshape(4, 4, CELLS, 128)
    act_ref[...] = act.astype(jnp.bfloat16).reshape(4, 4, CELLS, 128)


def result_body(info, act_ref, weights, near_ref, far_ref, turned):
    filt = info[1]
    out = conv_forward(act_ref, 0, 2, 0, 2, weights)
    for p in range(2):
        for r in range(2):
            at = (2 * p + r) * CELLS
            turned[...] = out[at : at + CELLS].T.astype(jnp.bfloat16)
            for j, ref in enumerate((near_ref, far_ref, near_ref, far_ref)):
                start = pl.multiple_of((filt ^ j) * 32, 32)
                ref[j // 2, p, r] = turned[pl.ds(start, 32), :]


def rows_body(info, own, near, far, out_ref):
    filt = info[1]
    for j, part in enumerate((own.at[0], near.at[0], far.at[0], far.at[1])):
        out_ref[filt ^ j] = part[...]


def shifts_of(value):
    lane = lax.broadcasted_iota(jnp.int32, value.shape, 1) % CELLS
    size = value.shape[1]
    after = jnp.where(lane == CELLS - 1, 0.0, pltpu.roll(value, size - 1, 1))
    before = jnp.where(lane == 0, 0.0, pltpu.roll(value, 1, 1))
    return jnp.concatenate([after, value, before], axis=0).astype(jnp.bfloat16)


def in_order(ref, at, core):
    rows = [ref[at + (pl.ds(pl.multiple_of((k ^ core) * 32, 32), 32),)] for k in range(4)]
    return jnp.concatenate(rows, axis=0)


def put_grad(refs, slot, block):
    for k in range(4):
        refs[k % 2][k // 2, slot] = block[k * 32 : k * 32 + 32].astype(jnp.bfloat16)


def put_kernel_grad(refs, first, grad):
    for n, (a, b) in enumerate(TAPS):
        for c in range(3):
            block = grad[c * 128 : c * 128 + 128, n * 128 : n * 128 + 128]
            put_grad(refs, first + 9 * a + 3 * b + c, block)


def last_body(info, mid_act, cot_own, keep_ref, send_ref):
    core = info[4]
    own = [in_order(cot_own, (p, r), core).astype(jnp.float32) for p in range(2) for r in range(2)]
    cot_rows = shifts_of(jnp.concatenate(own, axis=1))
    wide = jnp.concatenate([block_of(mid_act, a, 2, b, 2) for a, b in TAPS], axis=1)
    put_kernel_grad((keep_ref, send_ref), 0, dot(cot_rows, wide))


def back_body(
    info, act_window, mid, near, cross, weights_l, weights_m, mid_pre, level_pre, columns,
    keep_ref, send_ref, window, delta, turned,
):
    core = info[4]
    refs = (keep_ref, send_ref)
    fill_window(window, mid, near, cross, core)

    back = conv_backward(window, 0, 4, 0, 4, weights_l)
    here = jnp.where(inside(info), back * silu_slope(mid_pre[...].reshape(16 * CELLS, 128)), 0.0)
    delta[...] = here.astype(jnp.bfloat16).reshape(4, 4, CELLS, 128)

    for p in range(2):
        for r in range(2):
            at = (2 * p + r) * CELLS
            turned[:, at : at + CELLS] = delta[1 + p, 1 + r].astype(jnp.float32).T
    delta_rows = shifts_of(in_order(turned, (), core))
    wide = jnp.concatenate([block_of(act_window, 1 + a, 2, 1 + b, 2) for a, b in TAPS], axis=1)
    put_kernel_grad(refs, 0, dot(delta_rows, wide))

    back = conv_backward(delta, 0, 2, 0, 2, weights_m)
    pre = level_pre[...].reshape(4 * CELLS, 128)
    level_delta = (back * silu_slope(pre)).astype(jnp.bfloat16)
    grad = dot(columns[...], level_delta)
    for n in range(4):
        turned[:, n * 128 : n * 128 + 128] = grad[n * 128 : n * 128 + 128].T
    ordered = in_order(turned, (), core)
    for n in range(4):
        put_grad(refs, 27 + n, ordered[:, n * 128 : n * 128 + 128])
    for n in range(31, 37):
        put_grad(refs, n, jnp.zeros((128, 128), jnp.float32))


def finish_body(full_ref, stride_ref, middle_ref, last_ref):
    last_ref[...] = full_ref[0:27].astype(jnp.float32)
    middle_ref[...] = full_ref[27:54].astype(jnp.float32)
    for n in range(4):
        block = full_ref[54 + n].astype(jnp.float32)
        stride_ref[2 * n] = block[:, :64]
        stride_ref[2 * n + 1] = block[:, 64:]


def sum_body(terms_ref, out_ref):
    count, rows = terms_ref.shape[0], terms_ref.shape[1]
    for at in range(0, rows, 16):
        sums = [terms_ref[k, at : at + 16].astype(jnp.float32) for k in range(4)]
        for k in range(4, count):
            sums[k % 4] = sums[k % 4] + terms_ref[k, at : at + 16].astype(jnp.float32)
        total = ((sums[0] + sums[1]) + (sums[2] + sums[3])).astype(jnp.bfloat16)
        for d in range(out_ref.shape[0]):
            out_ref[d, at : at + 16] = total


def neighbourhood(info, own, beyond, first):
    def inner(d, f):
        return (d, 3 - f) if f in (1, 2) else (-1, f)

    pair = shifted(own, lambda d, f: (d ^ 1, f))
    column = call(
        "join",
        functools.partial(join_body, first),
        shape((6, 256, 128)),
        in_specs=[SMEM] + [VMEM] * 3,
    )(info, own, pair, beyond)
    cross = shifted(column, inner)
    near = swap_core(column)
    return [x.reshape(6, 2, 128, 128) for x in (column, near, cross)]


def whole(upper_level, stride_weight, middle_weight, last_weight, cotangent):
    depth = lax.axis_size("depth")
    chip, core = lax.axis_index("chip"), lax.axis_index("core")
    info = jnp.stack([lax.axis_index("depth"), 2 * chip + core, jnp.int32(depth), chip, core])
    cot_rows = cotangent.reshape(32, 2, 4, 2, 128).transpose(2, 3, 1, 0, 4)
    cot_parts = four_parts(cot_rows, 0)
    stride_parts = four_parts(stride_weight, 0)
    middle_parts = four_parts(middle_weight, 0)
    last_parts = four_parts(last_weight, 4)
    upper = upper_level.transpose(1, 2, 0, 3)

    level_act, level_pre, columns, cot_own, cot_cells, pack = call(
        "stride",
        stride_body,
        [
            shape((2, 256, 128)),
            shape((2, 2, 128, 128), jnp.float32),
            shape((512, 512)),
            shape((2, 2, 128, 128)),
            shape((2, 256, 128)),
            shape((2, 512, 128)),
        ],
        [pltpu.VMEM((128, 512), jnp.bfloat16)],
        flops=200_000_000,
        moved=1_500_000,
        in_specs=[SMEM] + [VMEM] * 9,
    )(info, upper, *stride_parts, *cot_parts)
    beyond = shifted(pack, lambda d, f: (d + 1 if d % 2 else d - 1, f))
    act_parts = neighbourhood(info, level_act, beyond, 0)
    back_parts = neighbourhood(info, cot_cells, beyond, 256)

    forward_m, forward_l, backward_l, backward_m = call(
        "weights",
        weights_body,
        [shape((384, 1152))] * 2 + [shape((1152, 384))] * 2,
        flops=1_000_000,
        moved=6_000_000,
        in_specs=[SMEM] + [VMEM] * 8,
    )(info, *middle_parts, *last_parts)

    mid_act, mid_pre, act_window = call(
        "middle",
        middle_body,
        [shape((4, 4, 128, 128)), shape((4, 4, 128, 128), jnp.float32), shape((6, 6, 128, 128))],
        flops=3_000_000_000,
        moved=4_000_000,
        in_specs=[SMEM] + [VMEM] * 4,
    )(info, *act_parts, forward_m)

    stay, leave = call(
        "result",
        result_body,
        [shape((2, 2, 2, 32, 128))] * 2,
        [pltpu.VMEM((128, 128), jnp.bfloat16)],
        flops=500_000_000,
        moved=2_000_000,
        in_specs=[SMEM] + [VMEM] * 2,
    )(info, mid_act, forward_l)
    result_near = swap_core(leave)
    result_far = swap_chip(jnp.stack([stay[1], result_near[1]]))

    keep_l, send_l = call(
        "grad_l",
        last_body,
        [shape((2, 27, 32, 128))] * 2,
        flops=500_000_000,
        moved=3_000_000,
        in_specs=[SMEM] + [VMEM] * 2,
    )(info, mid_act, cot_own)
    other_l = swap_core(send_l)

    keep, send = call(
        "back",
        back_body,
        [shape((2, 37, 32, 128))] * 2,
        [
            pltpu.VMEM((6, 6, 128, 128), jnp.bfloat16),
            pltpu.VMEM((4, 4, 128, 128), jnp.bfloat16),
            pltpu.VMEM((128, 512), jnp.float32),
        ],
        flops=4_000_000_000,
        moved=8_000_000,
        in_specs=[SMEM] + [VMEM] * 9,
    )(
        info, act_window, *back_parts, backward_l, backward_m, mid_pre, level_pre, columns
    )

    result = call(
        "rows", rows_body, shape((4, 2, 2, 32, 128)), in_specs=[SMEM] + [VMEM] * 3
    )(info, stay, result_near, result_far)
    result = result.transpose(3, 1, 0, 2, 4).reshape(32, 2, 8, 128)

    other = swap_core(send)
    terms = jnp.concatenate(
        [
            (x.astype(jnp.float32) + y.astype(jnp.float32)).astype(jnp.bfloat16)
            for x, y in ((keep_l, other_l), (keep, other))
        ],
        axis=1,
    )
    terms = lax.all_to_all(terms.reshape(2 * depth, 64, 128), ("chip", "depth"), 0, 0, tiled=True)
    spread = call("sum", sum_body, shape((depth, 64, 128)), in_specs=[VMEM])(terms)
    full = lax.all_to_all(spread, "depth", 0, 0, tiled=True)
    grads = call(
        "finish",
        finish_body,
        [
            shape((8, 32, 64), jnp.float32),
            shape((27, 32, 128), jnp.float32),
            shape((27, 32, 128), jnp.float32),
        ],
        in_specs=[VMEM],
    )(full.reshape(64, 32, 128))
    return (result, *grads)


def solution(mesh):
    placed = (
        P(None, "depth", FILT, None),
        P(None, FILT, None),
        P(None, FILT, None),
        P(None, FILT, None),
        P(FILT, "depth", None, None),
    )
    fine = Mesh(mesh.devices.reshape(-1, 2, 2), AXES)
    return jax.shard_map(
        whole,
        mesh=fine,
        in_specs=placed,
        out_specs=(
            P(FILT, "depth", None, None),
            P(None, FILT, None),
            P(None, FILT, None),
            P(None, FILT, None),
        ),
        check_vma=False,
    )
```

```python
import functools

import jax
import jax.numpy as jnp
from jax import lax
from jax.experimental import pallas as pl
from jax.experimental.pallas import tpu as pltpu
from jax.sharding import Mesh
from jax.sharding import PartitionSpec as P


AXES = ("depth", "chip", "core")
FILT = ("chip", "core")
CELLS = 128
LIMITS = {
    "stride": 8, "join": 6, "weights": 10, "middle": 20, "result": 8, "grad_l": 10, "back": 26,
    "rows": 2, "sum": 6, "finish": 4,
}
VMEM = pl.BlockSpec(memory_space=pltpu.VMEM)
SMEM = pl.BlockSpec(memory_space=pltpu.SMEM)
TAPS = [(a, b) for a in range(3) for b in range(3)]


def silu_slope(value):
    sigma = jax.nn.sigmoid(value)
    return sigma * (1.0 + value * (1.0 - sigma))


def pairs_of(move):
    depth, filt = lax.axis_size("depth"), lax.axis_size(FILT)
    found = []
    for d in range(depth):
        for f in range(filt):
            e, g = move(d, f)
            if 0 <= e < depth and 0 <= g < filt:
                found.append((d * filt + f, e * filt + g))
    return found


def shifted(value, move):
    return lax.ppermute(value, AXES, pairs_of(move))


def swap_core(value):
    return shifted(value, lambda d, f: (d, f ^ 1))


def swap_chip(value):
    return shifted(value, lambda d, f: (d, f ^ 2))


def four_parts(value, turn):
    far = shifted(value, lambda d, f: (d ^ turn, f ^ 2))
    return [value, swap_core(value), far, swap_core(far)]


def call(name, body, out_shape, scratch=(), flops=0, moved=0, in_specs=None):
    many = isinstance(out_shape, (list, tuple))
    return pl.pallas_call(
        body,
        out_shape=out_shape,
        in_specs=in_specs,
        out_specs=[VMEM] * len(out_shape) if many else VMEM,
        scratch_shapes=list(scratch),
        compiler_params=pltpu.CompilerParams(vmem_limit_bytes=LIMITS[name] << 20),
        cost_estimate=pl.CostEstimate(flops=flops, bytes_accessed=moved, transcendentals=0),
    )


def shape(dims, dtype=jnp.bfloat16):
    return jax.ShapeDtypeStruct(dims, dtype)


def dot(left, right):
    return jnp.dot(left, right, preferred_element_type=jnp.float32)


def dot_rows(left, right):
    return lax.dot_general(
        left, right, (((1,), (1,)), ((), ())), preferred_element_type=jnp.float32
    )


def stride_body(
    info, u_ref, s0, s1, s2, s3, c0, c1, c2, c3,
    act_ref, pre_ref, columns_ref, cot_ref, cells_ref, pack_ref, weights,
):
    filt = info[1]
    for j, part in enumerate((s0, s1, s2, s3)):
        start = pl.multiple_of((filt ^ j) * 32, 32)
        for tap in range(0, 8, 2):
            pair = jnp.concatenate([part[tap], part[tap + 1]], axis=1)
            weights[pl.ds(start, 32), tap * 64 : tap * 64 + 128] = pair
    source = lax.broadcasted_iota(jnp.int32, (256, 256), 0)
    target = lax.broadcasted_iota(jnp.int32, (256, 256), 1)
    pick = source == 2 * (target % 128) + target // 128
    pick = jnp.where(pick, 1.0, 0.0).astype(jnp.bfloat16)
    for p in range(2):
        for r in range(2):
            cell = 2 * p + r
            rows = []
            for a in range(2):
                for b in range(2):
                    split = dot(u_ref[2 * p + a, 2 * r + b], pick).astype(jnp.bfloat16)
                    rows += [split[:, :128], split[:, 128:]]
            block = jnp.concatenate(rows, axis=0)
            columns_ref[:, cell * 128 : cell * 128 + 128] = block
            pre = dot(weights[...], block).T
            pre_ref[p, r] = pre
            act = (pre * jax.nn.sigmoid(pre)).astype(jnp.bfloat16)
            act_ref[p, r * 128 : r * 128 + 128] = act
            pack_ref[p, r * 128 : r * 128 + 128] = act
            for j, part in enumerate((c0, c1, c2, c3)):
                start = pl.multiple_of((filt ^ j) * 32, 32)
                cot_ref[p, r, pl.ds(start, 32), :] = part[filt, r, p]
            cot = cot_ref[p, r].astype(jnp.float32).T.astype(jnp.bfloat16)
            cells_ref[p, r * 128 : r * 128 + 128] = cot
            pack_ref[p, 256 + r * 128 : 384 + r * 128] = cot


def join_body(first, info, own, pair, beyond, column_ref, halo_ref):
    odd = info[0] & 1
    column_ref[2:4] = own[...]
    column_ref[pl.ds(4 - 4 * odd, 2)] = pair[...]
    column_ref[pl.ds(4 * odd, 2)] = beyond[:, first : first + 256]
    halo_ref[pl.ds(2 - 2 * odd, 2)] = pair[...]
    halo_ref[pl.ds(2 * odd, 2)] = beyond[:, first : first + 256]


def fill_window(window, middle, near, cross, halo, core):
    window[:, 2:4] = middle[...]
    window[:, pl.ds(4 - 4 * core, 2)] = near[...]
    window[0:2, pl.ds(4 * core, 2)] = halo[0:2]
    window[2:4, pl.ds(4 * core, 2)] = cross[...]
    window[4:6, pl.ds(4 * core, 2)] = halo[2:4]


def fill_forward(weights, parts, filt):
    for j, part in enumerate(parts):
        start = (filt ^ j) * 32
        for n, (a, b) in enumerate(TAPS):
            for c in range(3):
                at = pl.multiple_of(start + c * 128, 32)
                weights[pl.ds(at, 32), n * 128 : n * 128 + 128] = part[9 * a + 3 * b + c]


def fill_backward(weights, parts, filt):
    for j, part in enumerate(parts):
        start = (filt ^ j) * 32
        for n, (a, b) in enumerate(TAPS):
            at = pl.multiple_of(start + n * 128, 32)
            for c in range(3):
                weights[pl.ds(at, 32), c * 128 : c * 128 + 128] = part[9 * a + 3 * b + c]


def weights_body(info, m0, m1, m2, m3, l0, l1, l2, l3, fm_ref, fl_ref, bl_ref, bm_ref):
    filt = info[1]
    fill_forward(fm_ref, (m0, m1, m2, m3), filt)
    fill_forward(fl_ref, (l0, l1, l2, l3), filt)
    fill_backward(bl_ref, (l0, l1, l2, l3), filt)
    fill_backward(bm_ref, (m0, m1, m2, m3), filt)


def column_of(size):
    return lax.broadcasted_iota(jnp.int32, (size, 1), 0) % CELLS


def from_before(value):
    size = value.shape[0]
    return jnp.where(column_of(size) == 0, 0.0, pltpu.roll(value, 1, 0))


def from_after(value):
    size = value.shape[0]
    return jnp.where(column_of(size) == CELLS - 1, 0.0, pltpu.roll(value, size - 1, 0))


def block_of(ref, p, planes, r, rows):
    return ref[pl.ds(p, planes), r : r + rows].reshape(planes * rows * CELLS, 128)


def conv_forward(ref, p, planes, r, rows, weights):
    wide = jnp.concatenate([block_of(ref, p + a, planes, r + b, rows) for a, b in TAPS], axis=1)
    out = dot_rows(wide, weights[...])
    return from_before(out[:, :128]) + out[:, 128:256] + from_after(out[:, 256:])


def conv_backward(ref, p, planes, r, rows, weights):
    wide = jnp.concatenate(
        [block_of(ref, p + 2 - a, planes, r + 2 - b, rows) for a, b in TAPS], axis=1
    )
    out = dot(wide, weights[...])
    return from_after(out[:, :128]) + out[:, 128:256] + from_before(out[:, 256:])


def inside(info):
    depth, filt = info[0], info[1]
    cell = lax.broadcasted_iota(jnp.int32, (16 * CELLS, 1), 0) // CELLS
    plane, row = cell // 4, cell % 4
    valid = (plane >= jnp.where(depth == 0, 1, 0)) & (row >= jnp.where(filt == 0, 1, 0))
    last = jnp.where(depth == lax.axis_size("depth") - 1, 2, 3)
    return valid & (plane <= last) & (row <= jnp.where(filt == 3, 2, 3))


def middle_body(info, mid, near, cross, halo, weights, act_ref, pre_ref, window):
    fill_window(window, mid, near, cross, halo, info[4])

    pre = conv_forward(window, 0, 4, 0, 4, weights)
    act = jnp.where(inside(info), pre * jax.nn.sigmoid(pre), 0.0)
    pre_ref[...] = pre.reshape(4, 4, CELLS, 128)
    act_ref[...] = act.astype(jnp.bfloat16).reshape(4, 4, CELLS, 128)


def result_body(info, act_ref, weights, near_ref, far_ref, turned):
    filt = info[1]
    out = conv_forward(act_ref, 0, 2, 0, 2, weights)
    for p in range(2):
        for r in range(2):
            at = (2 * p + r) * CELLS
            turned[...] = out[at : at + CELLS].T.astype(jnp.bfloat16)
            for j, ref in enumerate((near_ref, far_ref, near_ref, far_ref)):
                start = pl.multiple_of((filt ^ j) * 32, 32)
                ref[j // 2, p, r] = turned[pl.ds(start, 32), :]


def rows_body(info, own, near, far, out_ref):
    filt = info[1]
    for j, part in enumerate((own.at[0], near.at[0], far.at[0], far.at[1])):
        out_ref[filt ^ j] = part[...]


def shifts_of(value):
    lane = lax.broadcasted_iota(jnp.int32, value.shape, 1) % CELLS
    size = value.shape[1]
    after = jnp.where(lane == CELLS - 1, 0.0, pltpu.roll(value, size - 1, 1))
    before = jnp.where(lane == 0, 0.0, pltpu.roll(value, 1, 1))
    return jnp.concatenate([after, value, before], axis=0).astype(jnp.bfloat16)


def in_order(ref, at, core):
    rows = [ref[at + (pl.ds(pl.multiple_of((k ^ core) * 32, 32), 32),)] for k in range(4)]
    return jnp.concatenate(rows, axis=0)


def put_grad(refs, slot, block):
    for k in range(4):
        refs[k % 2][k // 2, slot] = block[k * 32 : k * 32 + 32].astype(jnp.bfloat16)


def put_kernel_grad(refs, first, grad):
    for n, (a, b) in enumerate(TAPS):
        for c in range(3):
            block = grad[c * 128 : c * 128 + 128, n * 128 : n * 128 + 128]
            put_grad(refs, first + 9 * a + 3 * b + c, block)


def last_body(info, mid_act, cot_own, keep_ref, send_ref):
    core = info[4]
    own = [in_order(cot_own, (p, r), core).astype(jnp.float32) for p in range(2) for r in range(2)]
    cot_rows = shifts_of(jnp.concatenate(own, axis=1))
    wide = jnp.concatenate([block_of(mid_act, a, 2, b, 2) for a, b in TAPS], axis=1)
    put_kernel_grad((keep_ref, send_ref), 0, dot(cot_rows, wide))


def back_body(
    info, act_window, mid, near, cross, halo, weights_l, weights_m, mid_pre, level_pre, columns,
    keep_ref, send_ref, window, delta, turned,
):
    core = info[4]
    refs = (keep_ref, send_ref)
    fill_window(window, mid, near, cross, halo, core)

    back = conv_backward(window, 0, 4, 0, 4, weights_l)
    here = jnp.where(inside(info), back * silu_slope(mid_pre[...].reshape(16 * CELLS, 128)), 0.0)
    delta[...] = here.astype(jnp.bfloat16).reshape(4, 4, CELLS, 128)

    for p in range(2):
        for r in range(2):
            at = (2 * p + r) * CELLS
            turned[:, at : at + CELLS] = delta[1 + p, 1 + r].astype(jnp.float32).T
    delta_rows = shifts_of(in_order(turned, (), core))
    wide = jnp.concatenate([block_of(act_window, 1 + a, 2, 1 + b, 2) for a, b in TAPS], axis=1)
    put_kernel_grad(refs, 0, dot(delta_rows, wide))

    back = conv_backward(delta, 0, 2, 0, 2, weights_m)
    pre = level_pre[...].reshape(4 * CELLS, 128)
    level_delta = (back * silu_slope(pre)).astype(jnp.bfloat16)
    grad = dot(columns[...], level_delta)
    for n in range(4):
        turned[:, n * 128 : n * 128 + 128] = grad[n * 128 : n * 128 + 128].T
    ordered = in_order(turned, (), core)
    for n in range(4):
        put_grad(refs, 27 + n, ordered[:, n * 128 : n * 128 + 128])
    for n in range(31, 37):
        put_grad(refs, n, jnp.zeros((128, 128), jnp.float32))


def finish_body(full_ref, stride_ref, middle_ref, last_ref):
    last_ref[...] = full_ref[0:27].astype(jnp.float32)
    middle_ref[...] = full_ref[27:54].astype(jnp.float32)
    for n in range(4):
        block = full_ref[54 + n].astype(jnp.float32)
        stride_ref[2 * n] = block[:, :64]
        stride_ref[2 * n + 1] = block[:, 64:]


def sum_body(terms_ref, out_ref):
    count, rows = terms_ref.shape[0], terms_ref.shape[1]
    for at in range(0, rows, 16):
        sums = [terms_ref[k, at : at + 16].astype(jnp.float32) for k in range(4)]
        for k in range(4, count):
            sums[k % 4] = sums[k % 4] + terms_ref[k, at : at + 16].astype(jnp.float32)
        total = ((sums[0] + sums[1]) + (sums[2] + sums[3])).astype(jnp.bfloat16)
        for d in range(out_ref.shape[0]):
            out_ref[d, at : at + 16] = total


def neighbourhood(info, own, beyond, first):
    def inner(d, f):
        return (d, 3 - f) if f in (1, 2) else (-1, f)

    pair = shifted(own, lambda d, f: (d ^ 1, f))
    cross = shifted(own, inner)
    column, halo = call(
        "join",
        functools.partial(join_body, first),
        [shape((6, 256, 128)), shape((4, 256, 128))],
        in_specs=[SMEM] + [VMEM] * 3,
    )(info, own, pair, beyond)
    halo = shifted(halo, inner)
    near = swap_core(column)
    return [x.reshape(x.shape[0], 2, 128, 128) for x in (column, near, cross, halo)]


def whole(upper_level, stride_weight, middle_weight, last_weight, cotangent):
    depth = lax.axis_size("depth")
    chip, core = lax.axis_index("chip"), lax.axis_index("core")
    info = jnp.stack([lax.axis_index("depth"), 2 * chip + core, jnp.int32(depth), chip, core])
    cot_rows = cotangent.reshape(32, 2, 4, 2, 128).transpose(2, 3, 1, 0, 4)
    cot_parts = four_parts(cot_rows, 0)
    stride_parts = four_parts(stride_weight, 0)
    middle_parts = four_parts(middle_weight, 0)
    last_parts = four_parts(last_weight, 4)
    upper = upper_level.transpose(1, 2, 0, 3)

    level_act, level_pre, columns, cot_own, cot_cells, pack = call(
        "stride",
        stride_body,
        [
            shape((2, 256, 128)),
            shape((2, 2, 128, 128), jnp.float32),
            shape((512, 512)),
            shape((2, 2, 128, 128)),
            shape((2, 256, 128)),
            shape((2, 512, 128)),
        ],
        [pltpu.VMEM((128, 512), jnp.bfloat16)],
        flops=200_000_000,
        moved=1_500_000,
        in_specs=[SMEM] + [VMEM] * 9,
    )(info, upper, *stride_parts, *cot_parts)
    beyond = shifted(pack, lambda d, f: (d + 1 if d % 2 else d - 1, f))
    act_parts = neighbourhood(info, level_act, beyond, 0)
    back_parts = neighbourhood(info, cot_cells, beyond, 256)

    forward_m, forward_l, backward_l, backward_m = call(
        "weights",
        weights_body,
        [shape((384, 1152))] * 2 + [shape((1152, 384))] * 2,
        flops=1_000_000,
        moved=6_000_000,
        in_specs=[SMEM] + [VMEM] * 8,
    )(info, *middle_parts, *last_parts)

    mid_act, mid_pre, act_window = call(
        "middle",
        middle_body,
        [shape((4, 4, 128, 128)), shape((4, 4, 128, 128), jnp.float32), shape((6, 6, 128, 128))],
        flops=3_000_000_000,
        moved=4_000_000,
        in_specs=[SMEM] + [VMEM] * 5,
    )(info, *act_parts, forward_m)

    stay, leave = call(
        "result",
        result_body,
        [shape((2, 2, 2, 32, 128))] * 2,
        [pltpu.VMEM((128, 128), jnp.bfloat16)],
        flops=500_000_000,
        moved=2_000_000,
        in_specs=[SMEM] + [VMEM] * 2,
    )(info, mid_act, forward_l)
    result_near = swap_core(leave)
    result_far = swap_chip(jnp.stack([stay[1], result_near[1]]))

    keep_l, send_l = call(
        "grad_l",
        last_body,
        [shape((2, 27, 32, 128))] * 2,
        flops=500_000_000,
        moved=3_000_000,
        in_specs=[SMEM] + [VMEM] * 2,
    )(info, mid_act, cot_own)
    other_l = swap_core(send_l)

    keep, send = call(
        "back",
        back_body,
        [shape((2, 37, 32, 128))] * 2,
        [
            pltpu.VMEM((6, 6, 128, 128), jnp.bfloat16),
            pltpu.VMEM((4, 4, 128, 128), jnp.bfloat16),
            pltpu.VMEM((128, 512), jnp.float32),
        ],
        flops=4_000_000_000,
        moved=8_000_000,
        in_specs=[SMEM] + [VMEM] * 10,
    )(
        info, act_window, *back_parts, backward_l, backward_m, mid_pre, level_pre, columns
    )

    result = call(
        "rows", rows_body, shape((4, 2, 2, 32, 128)), in_specs=[SMEM] + [VMEM] * 3
    )(info, stay, result_near, result_far)
    result = result.transpose(3, 1, 0, 2, 4).reshape(32, 2, 8, 128)

    other = swap_core(send)
    terms = jnp.concatenate(
        [
            (x.astype(jnp.float32) + y.astype(jnp.float32)).astype(jnp.bfloat16)
            for x, y in ((keep_l, other_l), (keep, other))
        ],
        axis=1,
    )
    terms = lax.all_to_all(terms.reshape(2 * depth, 64, 128), ("chip", "depth"), 0, 0, tiled=True)
    spread = call("sum", sum_body, shape((depth, 64, 128)), in_specs=[VMEM])(terms)
    full = lax.all_to_all(spread, "depth", 0, 0, tiled=True)
    grads = call(
        "finish",
        finish_body,
        [
            shape((8, 32, 64), jnp.float32),
            shape((27, 32, 128), jnp.float32),
            shape((27, 32, 128), jnp.float32),
        ],
        in_specs=[VMEM],
    )(full.reshape(64, 32, 128))
    return (result, *grads)


def solution(mesh):
    placed = (
        P(None, "depth", FILT, None),
        P(None, FILT, None),
        P(None, FILT, None),
        P(None, FILT, None),
        P(FILT, "depth", None, None),
    )
    fine = Mesh(mesh.devices.reshape(-1, 2, 2), AXES)
    return jax.shard_map(
        whole,
        mesh=fine,
        in_specs=placed,
        out_specs=(
            P(FILT, "depth", None, None),
            P(None, FILT, None),
            P(None, FILT, None),
            P(None, FILT, None),
        ),
        check_vma=False,
    )
```

```python
import functools

import jax
import jax.numpy as jnp
from jax import lax
from jax.experimental import pallas as pl
from jax.experimental.pallas import tpu as pltpu
from jax.sharding import Mesh
from jax.sharding import PartitionSpec as P


AXES = ("depth", "chip", "core")
FILT = ("chip", "core")
CELLS = 128
LIMITS = {
    "stride": 8, "join": 6, "weights": 10, "middle": 20, "result": 8, "grad_l": 10, "back": 26,
    "rows": 2, "sum": 6, "finish": 4,
}
VMEM = pl.BlockSpec(memory_space=pltpu.VMEM)
SMEM = pl.BlockSpec(memory_space=pltpu.SMEM)
TAPS = [(a, b) for a in range(3) for b in range(3)]


def silu_slope(value):
    sigma = jax.nn.sigmoid(value)
    return sigma * (1.0 + value * (1.0 - sigma))


def pairs_of(move):
    depth, filt = lax.axis_size("depth"), lax.axis_size(FILT)
    found = []
    for d in range(depth):
        for f in range(filt):
            e, g = move(d, f)
            if 0 <= e < depth and 0 <= g < filt:
                found.append((d * filt + f, e * filt + g))
    return found


def shifted(value, move):
    return lax.ppermute(value, AXES, pairs_of(move))


def swap_core(value):
    return shifted(value, lambda d, f: (d, f ^ 1))


def swap_chip(value):
    return shifted(value, lambda d, f: (d, f ^ 2))


def four_parts(value, turn):
    far = shifted(value, lambda d, f: (d ^ turn, f ^ 2))
    return [value, swap_core(value), far, swap_core(far)]


def call(name, body, out_shape, scratch=(), flops=0, moved=0, in_specs=None):
    many = isinstance(out_shape, (list, tuple))
    return pl.pallas_call(
        body,
        out_shape=out_shape,
        in_specs=in_specs,
        out_specs=[VMEM] * len(out_shape) if many else VMEM,
        scratch_shapes=list(scratch),
        compiler_params=pltpu.CompilerParams(vmem_limit_bytes=LIMITS[name] << 20),
        cost_estimate=pl.CostEstimate(flops=flops, bytes_accessed=moved, transcendentals=0),
    )


def shape(dims, dtype=jnp.bfloat16):
    return jax.ShapeDtypeStruct(dims, dtype)


def dot(left, right):
    return jnp.dot(left, right, preferred_element_type=jnp.float32)


def dot_rows(left, right):
    return lax.dot_general(
        left, right, (((1,), (1,)), ((), ())), preferred_element_type=jnp.float32
    )


def stride_body(
    info, u_ref, s0, s1, s2, s3, c0, c1, c2, c3,
    act_ref, pre_ref, columns_ref, cot_ref, cells_ref, pack_ref, weights,
):
    filt = info[1]
    for j, part in enumerate((s0, s1, s2, s3)):
        start = pl.multiple_of((filt ^ j) * 32, 32)
        for tap in range(0, 8, 2):
            pair = jnp.concatenate([part[tap], part[tap + 1]], axis=1)
            weights[pl.ds(start, 32), tap * 64 : tap * 64 + 128] = pair
    source = lax.broadcasted_iota(jnp.int32, (256, 256), 0)
    target = lax.broadcasted_iota(jnp.int32, (256, 256), 1)
    pick = source == 2 * (target % 128) + target // 128
    pick = jnp.where(pick, 1.0, 0.0).astype(jnp.bfloat16)
    for p in range(2):
        for r in range(2):
            cell = 2 * p + r
            rows = []
            for a in range(2):
                for b in range(2):
                    split = dot(u_ref[2 * p + a, 2 * r + b], pick).astype(jnp.bfloat16)
                    rows += [split[:, :128], split[:, 128:]]
            block = jnp.concatenate(rows, axis=0)
            columns_ref[:, cell * 128 : cell * 128 + 128] = block
            pre = dot(weights[...], block).T
            pre_ref[p, r] = pre
            act = (pre * jax.nn.sigmoid(pre)).astype(jnp.bfloat16)
            act_ref[p, r * 128 : r * 128 + 128] = act
            pack_ref[p, r * 128 : r * 128 + 128] = act
            for j, part in enumerate((c0, c1, c2, c3)):
                start = pl.multiple_of((filt ^ j) * 32, 32)
                cot_ref[p, r, pl.ds(start, 32), :] = part[filt, r, p]
            cot = cot_ref[p, r].astype(jnp.float32).T.astype(jnp.bfloat16)
            cells_ref[p, r * 128 : r * 128 + 128] = cot
            pack_ref[p, 256 + r * 128 : 384 + r * 128] = cot


def join_body(first, info, own, pair, beyond, column_ref, *halo):
    odd = info[0] & 1
    column_ref[2:4] = own[...]
    column_ref[pl.ds(4 - 4 * odd, 2)] = pair[...]
    column_ref[pl.ds(4 * odd, 2)] = beyond[:, first : first + 256]
    for halo_ref in halo:
        halo_ref[pl.ds(2 - 2 * odd, 2)] = pair[...]
        halo_ref[pl.ds(2 * odd, 2)] = beyond[:, first : first + 256]


def fill_window(window, middle, near, cross, core):
    window[:, 2:4] = middle[...]
    window[:, pl.ds(4 - 4 * core, 2)] = near[...]
    if len(cross) == 1:
        window[:, pl.ds(4 * core, 2)] = cross[0][...]
    else:
        window[0:2, pl.ds(4 * core, 2)] = cross[1][0:2]
        window[2:4, pl.ds(4 * core, 2)] = cross[0][...]
        window[4:6, pl.ds(4 * core, 2)] = cross[1][2:4]


def fill_forward(weights, parts, filt):
    for j, part in enumerate(parts):
        start = (filt ^ j) * 32
        for n, (a, b) in enumerate(TAPS):
            for c in range(3):
                at = pl.multiple_of(start + c * 128, 32)
                weights[pl.ds(at, 32), n * 128 : n * 128 + 128] = part[9 * a + 3 * b + c]


def fill_backward(weights, parts, filt):
    for j, part in enumerate(parts):
        start = (filt ^ j) * 32
        for n, (a, b) in enumerate(TAPS):
            at = pl.multiple_of(start + n * 128, 32)
            for c in range(3):
                weights[pl.ds(at, 32), c * 128 : c * 128 + 128] = part[9 * a + 3 * b + c]


def weights_body(info, m0, m1, m2, m3, l0, l1, l2, l3, fm_ref, fl_ref, bl_ref, bm_ref):
    filt = info[1]
    fill_forward(fm_ref, (m0, m1, m2, m3), filt)
    fill_forward(fl_ref, (l0, l1, l2, l3), filt)
    fill_backward(bl_ref, (l0, l1, l2, l3), filt)
    fill_backward(bm_ref, (m0, m1, m2, m3), filt)


def column_of(size):
    return lax.broadcasted_iota(jnp.int32, (size, 1), 0) % CELLS


def from_before(value):
    size = value.shape[0]
    return jnp.where(column_of(size) == 0, 0.0, pltpu.roll(value, 1, 0))


def from_after(value):
    size = value.shape[0]
    return jnp.where(column_of(size) == CELLS - 1, 0.0, pltpu.roll(value, size - 1, 0))


def block_of(ref, p, planes, r, rows):
    return ref[pl.ds(p, planes), r : r + rows].reshape(planes * rows * CELLS, 128)


def conv_forward(ref, p, planes, r, rows, weights):
    wide = jnp.concatenate([block_of(ref, p + a, planes, r + b, rows) for a, b in TAPS], axis=1)
    out = dot_rows(wide, weights[...])
    return from_before(out[:, :128]) + out[:, 128:256] + from_after(out[:, 256:])


def conv_backward(ref, p, planes, r, rows, weights):
    wide = jnp.concatenate(
        [block_of(ref, p + 2 - a, planes, r + 2 - b, rows) for a, b in TAPS], axis=1
    )
    out = dot(wide, weights[...])
    return from_after(out[:, :128]) + out[:, 128:256] + from_before(out[:, 256:])


def inside(info):
    depth, filt = info[0], info[1]
    cell = lax.broadcasted_iota(jnp.int32, (16 * CELLS, 1), 0) // CELLS
    plane, row = cell // 4, cell % 4
    valid = (plane >= jnp.where(depth == 0, 1, 0)) & (row >= jnp.where(filt == 0, 1, 0))
    last = jnp.where(depth == lax.axis_size("depth") - 1, 2, 3)
    return valid & (plane <= last) & (row <= jnp.where(filt == 3, 2, 3))


def middle_body(info, mid, near, cross, halo, weights, act_ref, pre_ref, window):
    fill_window(window, mid, near, (cross, halo), info[4])

    pre = conv_forward(window, 0, 4, 0, 4, weights)
    act = jnp.where(inside(info), pre * jax.nn.sigmoid(pre), 0.0)
    pre_ref[...] = pre.reshape(4, 4, CELLS, 128)
    act_ref[...] = act.astype(jnp.bfloat16).reshape(4, 4, CELLS, 128)


def result_body(info, act_ref, weights, near_ref, far_ref, turned):
    filt = info[1]
    out = conv_forward(act_ref, 0, 2, 0, 2, weights)
    for p in range(2):
        for r in range(2):
            at = (2 * p + r) * CELLS
            turned[...] = out[at : at + CELLS].T.astype(jnp.bfloat16)
            for j, ref in enumerate((near_ref, far_ref, near_ref, far_ref)):
                start = pl.multiple_of((filt ^ j) * 32, 32)
                ref[j // 2, p, r] = turned[pl.ds(start, 32), :]


def rows_body(info, own, near, far, out_ref):
    filt = info[1]
    for j, part in enumerate((own.at[0], near.at[0], far.at[0], far.at[1])):
        out_ref[filt ^ j] = part[...]


def shifts_of(value):
    lane = lax.broadcasted_iota(jnp.int32, value.shape, 1) % CELLS
    size = value.shape[1]
    after = jnp.where(lane == CELLS - 1, 0.0, pltpu.roll(value, size - 1, 1))
    before = jnp.where(lane == 0, 0.0, pltpu.roll(value, 1, 1))
    return jnp.concatenate([after, value, before], axis=0).astype(jnp.bfloat16)


def in_order(ref, at, core):
    rows = [ref[at + (pl.ds(pl.multiple_of((k ^ core) * 32, 32), 32),)] for k in range(4)]
    return jnp.concatenate(rows, axis=0)


def put_grad(refs, slot, block):
    for k in range(4):
        refs[k % 2][k // 2, slot] = block[k * 32 : k * 32 + 32].astype(jnp.bfloat16)


def put_kernel_grad(refs, first, grad):
    for n, (a, b) in enumerate(TAPS):
        for c in range(3):
            block = grad[c * 128 : c * 128 + 128, n * 128 : n * 128 + 128]
            put_grad(refs, first + 9 * a + 3 * b + c, block)


def last_body(info, mid_act, cot_own, keep_ref, send_ref):
    core = info[4]
    own = [in_order(cot_own, (p, r), core).astype(jnp.float32) for p in range(2) for r in range(2)]
    cot_rows = shifts_of(jnp.concatenate(own, axis=1))
    wide = jnp.concatenate([block_of(mid_act, a, 2, b, 2) for a, b in TAPS], axis=1)
    put_kernel_grad((keep_ref, send_ref), 0, dot(cot_rows, wide))


def back_body(
    info, act_window, mid, near, cross, weights_l, weights_m, mid_pre, level_pre, columns,
    keep_ref, send_ref, window, delta, turned,
):
    core = info[4]
    refs = (keep_ref, send_ref)
    fill_window(window, mid, near, (cross,), core)

    back = conv_backward(window, 0, 4, 0, 4, weights_l)
    here = jnp.where(inside(info), back * silu_slope(mid_pre[...].reshape(16 * CELLS, 128)), 0.0)
    delta[...] = here.astype(jnp.bfloat16).reshape(4, 4, CELLS, 128)

    for p in range(2):
        for r in range(2):
            at = (2 * p + r) * CELLS
            turned[:, at : at + CELLS] = delta[1 + p, 1 + r].astype(jnp.float32).T
    delta_rows = shifts_of(in_order(turned, (), core))
    wide = jnp.concatenate([block_of(act_window, 1 + a, 2, 1 + b, 2) for a, b in TAPS], axis=1)
    put_kernel_grad(refs, 0, dot(delta_rows, wide))

    back = conv_backward(delta, 0, 2, 0, 2, weights_m)
    pre = level_pre[...].reshape(4 * CELLS, 128)
    level_delta = (back * silu_slope(pre)).astype(jnp.bfloat16)
    grad = dot(columns[...], level_delta)
    for n in range(4):
        turned[:, n * 128 : n * 128 + 128] = grad[n * 128 : n * 128 + 128].T
    ordered = in_order(turned, (), core)
    for n in range(4):
        put_grad(refs, 27 + n, ordered[:, n * 128 : n * 128 + 128])
    for n in range(31, 37):
        put_grad(refs, n, jnp.zeros((128, 128), jnp.float32))


def finish_body(full_ref, stride_ref, middle_ref, last_ref):
    last_ref[...] = full_ref[0:27].astype(jnp.float32)
    middle_ref[...] = full_ref[27:54].astype(jnp.float32)
    for n in range(4):
        block = full_ref[54 + n].astype(jnp.float32)
        stride_ref[2 * n] = block[:, :64]
        stride_ref[2 * n + 1] = block[:, 64:]


def sum_body(terms_ref, out_ref):
    count, rows = terms_ref.shape[0], terms_ref.shape[1]
    for at in range(0, rows, 16):
        sums = [terms_ref[k, at : at + 16].astype(jnp.float32) for k in range(4)]
        for k in range(4, count):
            sums[k % 4] = sums[k % 4] + terms_ref[k, at : at + 16].astype(jnp.float32)
        total = ((sums[0] + sums[1]) + (sums[2] + sums[3])).astype(jnp.bfloat16)
        for d in range(out_ref.shape[0]):
            out_ref[d, at : at + 16] = total


def neighbourhood(info, own, beyond, first, split):
    def inner(d, f):
        return (d, 3 - f) if f in (1, 2) else (-1, f)

    pair = shifted(own, lambda d, f: (d ^ 1, f))
    cross = [shifted(own, inner)] if split else []
    column, *halo = call(
        "join",
        functools.partial(join_body, first),
        [shape((6, 256, 128))] + [shape((4, 256, 128))] * split,
        in_specs=[SMEM] + [VMEM] * 3,
    )(info, own, pair, beyond)
    cross += [shifted(halo[0] if split else column, inner)]
    near = swap_core(column)
    return [x.reshape(x.shape[0], 2, 128, 128) for x in (column, near, *cross)]


def whole(upper_level, stride_weight, middle_weight, last_weight, cotangent):
    depth = lax.axis_size("depth")
    chip, core = lax.axis_index("chip"), lax.axis_index("core")
    info = jnp.stack([lax.axis_index("depth"), 2 * chip + core, jnp.int32(depth), chip, core])
    cot_rows = cotangent.reshape(32, 2, 4, 2, 128).transpose(2, 3, 1, 0, 4)
    cot_parts = four_parts(cot_rows, 0)
    stride_parts = four_parts(stride_weight, 0)
    middle_parts = four_parts(middle_weight, 0)
    last_parts = four_parts(last_weight, 4)
    upper = upper_level.transpose(1, 2, 0, 3)

    level_act, level_pre, columns, cot_own, cot_cells, pack = call(
        "stride",
        stride_body,
        [
            shape((2, 256, 128)),
            shape((2, 2, 128, 128), jnp.float32),
            shape((512, 512)),
            shape((2, 2, 128, 128)),
            shape((2, 256, 128)),
            shape((2, 512, 128)),
        ],
        [pltpu.VMEM((128, 512), jnp.bfloat16)],
        flops=200_000_000,
        moved=1_500_000,
        in_specs=[SMEM] + [VMEM] * 9,
    )(info, upper, *stride_parts, *cot_parts)
    beyond = shifted(pack, lambda d, f: (d + 1 if d % 2 else d - 1, f))
    act_parts = neighbourhood(info, level_act, beyond, 0, True)
    back_parts = neighbourhood(info, cot_cells, beyond, 256, False)

    forward_m, forward_l, backward_l, backward_m = call(
        "weights",
        weights_body,
        [shape((384, 1152))] * 2 + [shape((1152, 384))] * 2,
        flops=1_000_000,
        moved=6_000_000,
        in_specs=[SMEM] + [VMEM] * 8,
    )(info, *middle_parts, *last_parts)

    mid_act, mid_pre, act_window = call(
        "middle",
        middle_body,
        [shape((4, 4, 128, 128)), shape((4, 4, 128, 128), jnp.float32), shape((6, 6, 128, 128))],
        flops=3_000_000_000,
        moved=4_000_000,
        in_specs=[SMEM] + [VMEM] * 5,
    )(info, *act_parts, forward_m)

    stay, leave = call(
        "result",
        result_body,
        [shape((2, 2, 2, 32, 128))] * 2,
        [pltpu.VMEM((128, 128), jnp.bfloat16)],
        flops=500_000_000,
        moved=2_000_000,
        in_specs=[SMEM] + [VMEM] * 2,
    )(info, mid_act, forward_l)
    result_near = swap_core(leave)
    result_far = swap_chip(jnp.stack([stay[1], result_near[1]]))

    keep_l, send_l = call(
        "grad_l",
        last_body,
        [shape((2, 27, 32, 128))] * 2,
        flops=500_000_000,
        moved=3_000_000,
        in_specs=[SMEM] + [VMEM] * 2,
    )(info, mid_act, cot_own)
    other_l = swap_core(send_l)

    keep, send = call(
        "back",
        back_body,
        [shape((2, 37, 32, 128))] * 2,
        [
            pltpu.VMEM((6, 6, 128, 128), jnp.bfloat16),
            pltpu.VMEM((4, 4, 128, 128), jnp.bfloat16),
            pltpu.VMEM((128, 512), jnp.float32),
        ],
        flops=4_000_000_000,
        moved=8_000_000,
        in_specs=[SMEM] + [VMEM] * 9,
    )(
        info, act_window, *back_parts, backward_l, backward_m, mid_pre, level_pre, columns
    )

    result = call(
        "rows", rows_body, shape((4, 2, 2, 32, 128)), in_specs=[SMEM] + [VMEM] * 3
    )(info, stay, result_near, result_far)
    result = result.transpose(3, 1, 0, 2, 4).reshape(32, 2, 8, 128)

    other = swap_core(send)
    terms = jnp.concatenate(
        [
            (x.astype(jnp.float32) + y.astype(jnp.float32)).astype(jnp.bfloat16)
            for x, y in ((keep_l, other_l), (keep, other))
        ],
        axis=1,
    )
    terms = lax.all_to_all(terms.reshape(2 * depth, 64, 128), ("chip", "depth"), 0, 0, tiled=True)
    spread = call("sum", sum_body, shape((depth, 64, 128)), in_specs=[VMEM])(terms)
    full = lax.all_to_all(spread, "depth", 0, 0, tiled=True)
    grads = call(
        "finish",
        finish_body,
        [
            shape((8, 32, 64), jnp.float32),
            shape((27, 32, 128), jnp.float32),
            shape((27, 32, 128), jnp.float32),
        ],
        in_specs=[VMEM],
    )(full.reshape(64, 32, 128))
    return (result, *grads)


def solution(mesh):
    placed = (
        P(None, "depth", FILT, None),
        P(None, FILT, None),
        P(None, FILT, None),
        P(None, FILT, None),
        P(FILT, "depth", None, None),
    )
    fine = Mesh(mesh.devices.reshape(-1, 2, 2), AXES)
    return jax.shard_map(
        whole,
        mesh=fine,
        in_specs=placed,
        out_specs=(
            P(FILT, "depth", None, None),
            P(None, FILT, None),
            P(None, FILT, None),
            P(None, FILT, None),
        ),
        check_vma=False,
    )
```
